32 devices in a mesh: section: 2 (over core), ctx: 4 (over z), fsdp: 4 (over y, x).
Axes of the slice: x: 2, y: 2, z: 4, core: 2. Of those that a mesh axis runs over, the one named last changes fastest.
Arguments:
- block_input: bfloat16 [24, 1024, 768], P('fsdp', 'ctx'), may hold values from -6 to 6
- positions: int32 [24, 1024], P('fsdp'), may hold values from 0 to 1023, each once within a row
- cotangent: bfloat16 [24, 1024, 768], P('fsdp', 'ctx'), may hold values from -6 to 6
- w_qkv: bfloat16 [2, 768, 2304], P('section', 'fsdp'), may hold values from -0.21875 to 0.21875
- w_proj: bfloat16 [2, 768, 768], P('section', 'fsdp'), may hold values from -1.25 to 1.25
- w_fc: bfloat16 [2, 768, 3072], P('section', 'fsdp'), may hold values from -0.21875 to 0.21875
- w_out: bfloat16 [2, 3072, 768], P('section', 'fsdp'), may hold values from -0.109375 to 0.109375
- ln_gain: bfloat16 [2, 2, 768], P('section', None, 'fsdp'), may hold values from 0.099609375 to 1.8984375
- ln_bias: bfloat16 [2, 2, 768], P('section', None, 'fsdp'), may hold values from -1.75 to 1.75
- attn_bias: bfloat16 [2, 2, 768], P('section', None, 'fsdp'), may hold values from -3 to 3
- out_bias: bfloat16 [2, 2, 768], P('section', None, 'fsdp'), may hold values from -1.75 to 1.75
- fc_bias: bfloat16 [2, 3072], P('section', 'fsdp'), may hold values from -3 to 3
Outputs:
- section_out: bfloat16 [2, 24, 1024, 768], P('section', 'fsdp', 'ctx')
- section_in_grad: bfloat16 [2, 24, 1024, 768], P('section', 'fsdp', 'ctx')
- grad_w_qkv: float32 [2, 768, 2304], P('section', 'fsdp')
- grad_w_proj: float32 [2, 768, 768], P('section', 'fsdp')
- grad_w_fc: float32 [2, 768, 3072], P('section', 'fsdp')
- grad_w_out: float32 [2, 3072, 768], P('section', 'fsdp')
- grad_ln_gain: float32 [2, 2, 768], P('section', None, 'fsdp')
- grad_ln_bias: float32 [2, 2, 768], P('section', None, 'fsdp')
- grad_attn_bias: float32 [2, 2, 768], P('section', None, 'fsdp')
- grad_out_bias: float32 [2, 2, 768], P('section', None, 'fsdp')
- grad_fc_bias: float32 [2, 3072], P('section', 'fsdp')
The draws below stay inside these ranges and needn't reach their ends.
Inputs may be any that keep to these rules, and one draw needn't show every extreme that they name: `positions`: each row is a permutation of the places 0 to 1023 of one sequence.
All inputs are finite; a program needn't handle non-finite values.
Results may differ from the reference program's by a relative error of at most 0.034.
Values may be sent and summed in bfloat16 or wider, within the bound.
A program may use at most 320 MiB of HBM per device.

```python
import math
import jax
import jax.numpy as jnp
from jax import lax

D = 768
H = 12
HD = 64
FF = 3072
SEQ = 1024
SEQS = 24


def levels(own_key, dims, shards, smallest, largest):
    def one(dim, shards_of):
        draws = jax.random.uniform(jax.random.fold_in(jax.random.fold_in(own_key, 6), dim), (shards_of,), jnp.float32, smallest / len(shards), largest / len(shards))
        return jnp.repeat(jnp.exp(draws), dims[dim] // shards_of).reshape((-1,) + (1,) * (len(dims) - dim - 1))

    level = one(*shards[0])
    for cut in shards[1:]:
        level = level * one(*cut)
    return level


def scatter_about(own_key, shape, scale, bound, pieces=(), kind=jnp.bfloat16):
    array = jax.random.normal(own_key, shape, jnp.float32) * scale
    if len(pieces) > 0:
        array = levels(own_key, shape, pieces, -0.22, 0.18) * array
    return jnp.clip(array, min=-bound, max=bound).astype(kind)


def setup_inputs(seed: int = 0) -> dict:
    streams_of = jax.random.split(jax.random.key(seed), 13)
    return {
        "block_input": scatter_about(streams_of[0], (SEQS, SEQ, D), 1.0, 6.0, ((0, 4), (1, 4))),
        "positions": jax.vmap(lambda own: jax.random.permutation(own, SEQ))(jax.random.split(streams_of[1], SEQS)).reshape((SEQS, SEQ)).astype(jnp.int32),
        "cotangent": scatter_about(streams_of[2], (SEQS, SEQ, D), 1.0, 6.0, ((0, 4), (1, 4))),
        "w_qkv": scatter_about(streams_of[3], (2, D, 3 * D), D ** -0.5, 0.21875, ((0, 2), (1, 4))),
        "w_proj": scatter_about(streams_of[4], (2, D, D), (D // 32) ** -0.5, 1.25, ((0, 2), (1, 4))),
        "w_fc": scatter_about(streams_of[5], (2, D, FF), D ** -0.5, 0.21875, ((0, 2), (1, 4))),
        "w_out": scatter_about(streams_of[6], (2, FF, D), FF ** -0.5, 0.109375, ((0, 2), (1, 4))),
        "ln_gain": jnp.clip(1.0 + 0.18 * jax.random.normal(streams_of[7], (2, 2, D), jnp.float32), 0.099609375, 1.8984375).astype(jnp.bfloat16),
        "ln_bias": scatter_about(streams_of[8], (2, 2, D), 0.3, 1.75, ((0, 2), (2, 4))),
        "attn_bias": scatter_about(streams_of[9], (2, 2, D), 0.5, 3.0, ((0, 2), (2, 4))),
        "out_bias": scatter_about(streams_of[10], (2, 2, D), 0.3, 1.75, ((0, 2), (2, 4))),
        "fc_bias": scatter_about(streams_of[11], (2, FF), 0.5, 3.0, ((0, 2), (1, 4))),
    }


@jax.custom_vjp
def low(v):
    return lax.optimization_barrier(v.astype(jnp.bfloat16)).astype(jnp.float32)

@jax.custom_vjp
def low_back(v):
    return v

def low_keep(v):
    return (low(v), None)

def low_pass(kept, grad):
    return (grad,)

def back_keep(v):
    return (v, None)

def back_low(kept, grad):
    return (low(grad),)
low.defvjp(low_keep, low_pass)
low_back.defvjp(back_keep, back_low)

def layer_norm(hidden, gain, offset):
    center = hidden - lax.optimization_barrier(jnp.mean(hidden, axis=-1, keepdims=True))
    spread = lax.optimization_barrier(jnp.mean(center * center, axis=-1, keepdims=True))
    return center * lax.rsqrt(spread + 1e-05) * gain + offset

def matmul(rows, matrix):
    return jnp.einsum('nsd,de->nse', rows, matrix, precision=lax.Precision.HIGHEST)

def attend_single(item):
    queries, key_rows, value_rows, places = item
    query_heads = queries.reshape(SEQ, H, HD)
    key_heads = key_rows.reshape(SEQ, H, HD)
    value_heads = value_rows.reshape(SEQ, H, HD)
    scores = low_back(jnp.einsum('qhd,khd->hqk', query_heads, key_heads, precision=lax.Precision.HIGHEST) * HD ** (-0.5))
    allowed = places[:, None] >= places[None, :]
    scores = jnp.where(allowed[None], scores, -1e+30)
    probs = jax.nn.softmax(scores, axis=-1)
    mixed = jnp.einsum('hqk,khd->qhd', low(probs), value_heads, precision=lax.Precision.HIGHEST)
    return mixed.reshape(SEQ, D)

def layer(params, hidden, places):
    w_qkv, w_proj, w_fc, w_out, gains, offsets, attn_bias, out_bias, fc_bias = params
    normed = low(layer_norm(hidden, gains[0], offsets[0]))
    project = matmul(normed, w_qkv)
    queries = low_back(low(project[..., :D] + attn_bias[0]))
    key_rows = low_back(low(project[..., D:2 * D]))
    value_rows = low_back(low(project[..., 2 * D:] + attn_bias[1]))
    mixed = lax.map(jax.checkpoint(attend_single), (queries, key_rows, value_rows, places))
    mixed = low_back(low(mixed))
    branch = low_back(matmul(mixed, w_proj) + out_bias[0])
    after = hidden + branch
    normed_two = low(layer_norm(after, gains[1], offsets[1]))
    inner = low_back(matmul(normed_two, w_fc) + fc_bias)
    active = low(jax.nn.gelu(inner, approximate=True))
    return after + matmul(active, w_out) + out_bias[1]

def reference(block_input, positions, cotangent, w_qkv, w_proj, w_fc, w_out, ln_gain, ln_bias, attn_bias, out_bias, fc_bias):
    stacked = tuple((arr.astype(jnp.float32) for arr in (w_qkv, w_proj, w_fc, w_out, ln_gain, ln_bias, attn_bias, out_bias, fc_bias)))
    first = tuple((arr[0] for arr in stacked))
    second = tuple((arr[1] for arr in stacked))
    group = math.gcd(SEQS, 4)
    count = SEQS // group
    inputs = block_input.astype(jnp.float32).reshape(count, group, SEQ, D)
    places_all = positions.reshape(count, group, SEQ)
    cotans = cotangent.astype(jnp.float32).reshape(count, group, SEQ, D)

    def one_group(totals, item):
        hidden, places, cotan = item

        def run(params, rows):
            return layer(params, rows, places)
        middle_raw, pull_first = jax.vjp(run, first, hidden)
        middle = low(middle_raw)
        final, pull_second = jax.vjp(run, second, middle)
        grads_second, grad_middle = pull_second(cotan)
        grad_middle = low(grad_middle)
        grads_first, grad_hidden = pull_first(grad_middle)
        totals = tuple((total + jnp.stack([one, two]) for total, one, two in zip(totals, grads_first, grads_second)))
        return (totals, (middle, final, grad_hidden, grad_middle))
    zeros_init = tuple((jnp.zeros(arr.shape, jnp.float32) for arr in stacked))
    totals, (middle, final, grad_hidden, grad_middle) = lax.scan(one_group, zeros_init, (inputs, places_all, cotans))
    section_out = jnp.stack([middle.reshape(SEQS, SEQ, D), final.reshape(SEQS, SEQ, D)]).astype(jnp.bfloat16)
    section_in_grad = jnp.stack([grad_hidden.reshape(SEQS, SEQ, D), grad_middle.reshape(SEQS, SEQ, D)]).astype(jnp.bfloat16)
    return (section_out, section_in_grad, totals[0], totals[1], totals[2], totals[3], totals[4], totals[5], totals[6], totals[7], totals[8])
```

```python
import functools

import jax
import jax.numpy as jnp
from jax import lax
from jax.experimental import pallas as pl
from jax.experimental.pallas import tpu as pltpu
from jax.sharding import PartitionSpec as P

H = 12
HD = 64
PAIR = 2 * HD
SCALE = HD**-0.5

masked_score = -1e30
norm_eps = 1e-05
f32 = jnp.float32
bf16 = jnp.bfloat16


def layer_norm(hidden, gain, offset):
    center = hidden - jnp.mean(hidden, axis=-1, keepdims=True)
    spread = jnp.mean(center * center, axis=-1, keepdims=True)
    return center * lax.rsqrt(spread + norm_eps) * gain + offset


def gelu_tanh(inputs):
    return jax.nn.gelu(inputs, approximate=True)


def mm(left, right):
    return lax.dot_general(left, right, (((1,), (0,)), ((), ())), preferred_element_type=f32)


def mm_nt(left, right):
    return lax.dot_general(left, right, (((1,), (1,)), ((), ())), preferred_element_type=f32)


def mm_tn(left, right):
    return lax.dot_general(left, right, (((0,), (0,)), ((), ())), preferred_element_type=f32)


def masked_scores(keys, queries, start, block):
    scores = mm_nt(keys, queries)
    down = lax.broadcasted_iota(jnp.int32, (block, block), 0)
    across = lax.broadcasted_iota(jnp.int32, (block, block), 1)
    corner = jnp.where(across >= down, scores[start:], masked_score)
    if start == 0:
        return corner
    return jnp.concatenate([scores[:start], corner], axis=0)


def attend_kernel(block, q_ref, k_ref, v_ref, o_ref, log_ref):
    length = q_ref.shape[0]
    for head in range(2):
        cols = slice(head * HD, (head + 1) * HD)
        for start in range(0, length, block):
            end = start + block
            queries = (q_ref[start:end, cols].astype(f32) * SCALE).astype(bf16)
            scores = masked_scores(k_ref[:end, cols], queries, start, block)
            top = jnp.max(scores, axis=0, keepdims=True)
            weights = jnp.exp(scores - top)
            total = jnp.sum(weights, axis=0, keepdims=True)
            mixed = mm_tn(v_ref[:end, cols], weights.astype(bf16)) / total
            o_ref[start:end, cols] = mixed.T.astype(bf16)
            log_ref[0, 0, head : head + 1, start:end] = top + jnp.log(total)


def attend_back_kernel(
    block, q_ref, k_ref, v_ref, do_ref, o_ref, log_ref, dq_ref, dk_ref, dv_ref, dk_sum, dv_sum
):
    length = q_ref.shape[0]
    for head in range(2):
        cols = slice(head * HD, (head + 1) * HD)
        for start in range(length - block, -1, -block):
            end = start + block
            queries = (q_ref[start:end, cols].astype(f32) * SCALE).astype(bf16)
            grads = do_ref[start:end, cols]
            product = grads.astype(f32) * o_ref[start:end, cols].astype(f32)
            delta = jnp.sum(product.T, axis=0, keepdims=True)
            keys = k_ref[:end, cols]
            scores = masked_scores(keys, queries, start, block)
            probs = jnp.exp(scores - log_ref[0, 0, head : head + 1, start:end])
            grad_probs = mm_nt(v_ref[:end, cols], grads)
            grad_scores = (probs * (grad_probs - delta)).astype(bf16)
            dv = mm(probs.astype(bf16), grads)
            dk = mm(grad_scores, queries)
            if end == length:
                dv_sum[:end, cols] = dv
                dk_sum[:end, cols] = dk
            else:
                dv_sum[:end, cols] += dv
                dk_sum[:end, cols] += dk
            dq = mm_tn(keys, grad_scores) * SCALE
            dq_ref[start:end, cols] = dq.T.astype(bf16)
    dk_ref[...] = dk_sum[...].astype(bf16)
    dv_ref[...] = dv_sum[...].astype(bf16)


def query_block(length):
    return 256 if length % 256 == 0 else length


def head_spec(length, offset):
    return pl.BlockSpec((length, PAIR), lambda b, h: (b, offset + h))


def log_spec(length):
    return pl.BlockSpec((1, 1, 2, length), lambda b, h: (b, h, 0, 0))


def attend_forward(project, length):
    rows = project.shape[0]
    count = rows // length
    pairs = H // 2
    return pl.pallas_call(
        functools.partial(attend_kernel, query_block(length)),
        grid=(count, pairs),
        in_specs=[head_spec(length, 0), head_spec(length, pairs), head_spec(length, 2 * pairs)],
        out_specs=[head_spec(length, 0), log_spec(length)],
        out_shape=[
            jax.ShapeDtypeStruct((rows, H * HD), bf16),
            jax.ShapeDtypeStruct((count, pairs, 2, length), f32),
        ],
        compiler_params=pltpu.CompilerParams(vmem_limit_bytes=40 * 1024 * 1024),
        cost_estimate=pl.CostEstimate(
            flops=8 * rows * length * H * HD,
            bytes_accessed=8 * rows * H * HD,
            transcendentals=rows * length * H // 2,
        ),
    )(project, project, project)


def attend_back(project, grad_mixed, mixed, log_total, length):
    rows = project.shape[0]
    count = rows // length
    pairs = H // 2
    return pl.pallas_call(
        functools.partial(attend_back_kernel, query_block(length)),
        grid=(count, pairs),
        in_specs=[
            head_spec(length, 0),
            head_spec(length, pairs),
            head_spec(length, 2 * pairs),
            head_spec(length, 0),
            head_spec(length, 0),
            log_spec(length),
        ],
        out_specs=[head_spec(length, 0)] * 3,
        out_shape=[jax.ShapeDtypeStruct((rows, H * HD), bf16)] * 3,
        scratch_shapes=[pltpu.VMEM((length, PAIR), f32)] * 2,
        compiler_params=pltpu.CompilerParams(vmem_limit_bytes=40 * 1024 * 1024),
        cost_estimate=pl.CostEstimate(
            flops=20 * rows * length * H * HD,
            bytes_accessed=16 * rows * H * HD,
            transcendentals=rows * length * H // 2,
        ),
    )(project, project, project, grad_mixed, mixed, log_total)


def layer_forward(weights, smalls, layer_in, length):
    w_qkv, w_proj, w_fc, w_out = weights
    gains, offsets, attn_bias, out_bias, fc_bias = smalls
    hidden = layer_in.astype(f32)
    width = hidden.shape[-1]
    normed = layer_norm(hidden, gains[0], offsets[0]).astype(bf16)
    bias = jnp.concatenate([attn_bias[0], jnp.zeros((width,), f32), attn_bias[1]])
    project = (mm(normed, w_qkv) + bias).astype(bf16)
    mixed, log_total = attend_forward(project, length)
    after = hidden + mm(mixed, w_proj) + out_bias[0]
    normed_two = layer_norm(after, gains[1], offsets[1]).astype(bf16)
    inner = mm(normed_two, w_fc) + fc_bias
    active = gelu_tanh(inner).astype(bf16)
    result = (after + mm(active, w_out) + out_bias[1]).astype(bf16)
    return result, (layer_in, normed, project, mixed, log_total, after, normed_two, inner, active)


def row_sum(rows):
    return jnp.sum(rows.astype(f32), axis=0)


def layer_back(weights, smalls, kept, grad_out, length, send):
    w_qkv, w_proj, w_fc, w_out = weights
    gains, offsets, attn_bias, out_bias, fc_bias = smalls
    layer_in, normed, project, mixed, log_total, after, normed_two, inner, active = kept
    grad_out, grad_w_out = lax.optimization_barrier(
        (grad_out, mm_tn(active, grad_out).astype(bf16))
    )
    grad_w_out = send(grad_w_out)
    grad_bias_two = row_sum(grad_out)
    grad_active = mm_nt(grad_out, w_out)
    _, gelu_pull = jax.vjp(gelu_tanh, inner)
    grad_inner = gelu_pull(grad_active)[0].astype(bf16)
    grad_inner, grad_w_fc = lax.optimization_barrier(
        (grad_inner, mm_tn(normed_two, grad_inner).astype(bf16))
    )
    grad_w_fc = send(grad_w_fc)
    grad_fc_bias = row_sum(grad_inner)
    grad_normed_two = mm_nt(grad_inner, w_fc)
    _, norm_pull = jax.vjp(layer_norm, after, gains[1], offsets[1])
    grad_after, grad_gain_two, grad_offset_two = norm_pull(grad_normed_two)
    grad_after = grad_after + grad_out.astype(f32)
    grad_branch = grad_after.astype(bf16)
    grad_branch, grad_w_proj = lax.optimization_barrier(
        (grad_branch, mm_tn(mixed, grad_branch).astype(bf16))
    )
    grad_w_proj = send(grad_w_proj)
    grad_bias_one = row_sum(grad_branch)
    grad_mixed = mm_nt(grad_branch, w_proj).astype(bf16)
    grad_q, grad_k, grad_v = attend_back(project, grad_mixed, mixed, log_total, length)
    grad_project = jnp.concatenate([grad_q, grad_k, grad_v], axis=-1)
    grad_project, grad_w_qkv = lax.optimization_barrier(
        (grad_project, mm_tn(normed, grad_project).astype(bf16))
    )
    grad_w_qkv = send(grad_w_qkv)
    grad_normed = mm_nt(grad_project, w_qkv)
    _, first_pull = jax.vjp(layer_norm, layer_in.astype(f32), gains[0], offsets[0])
    grad_hidden, grad_gain_one, grad_offset_one = first_pull(grad_normed)
    grad_input = (grad_after + grad_hidden).astype(bf16)
    small = (
        jnp.stack(
            [
                grad_gain_one,
                grad_gain_two,
                grad_offset_one,
                grad_offset_two,
                row_sum(grad_q),
                row_sum(grad_v),
                grad_bias_one,
                grad_bias_two,
            ]
        ),
        grad_fc_bias,
    )
    return grad_input, (grad_w_qkv, grad_w_proj, grad_w_fc, grad_w_out), small


MESH = pl.DeviceIdType.MESH
ANY = pl.BlockSpec(memory_space=pl.ANY)
CHUNK = 768


def greet(partners):
    barrier = pltpu.get_barrier_semaphore()
    for partner in partners:
        pl.semaphore_signal(barrier, inc=1, device_id=partner, device_id_type=MESH)
    pl.semaphore_wait(barrier, len(partners))


def remote(source, target, send, recv, device):
    return pltpu.make_async_remote_copy(
        src_ref=source,
        dst_ref=target,
        send_sem=send,
        recv_sem=recv,
        device_id=device,
        device_id_type=MESH,
    )


class Gather:
    def __init__(self, layer, shards, outs, send, recv, local):
        self.layer, self.shards, self.outs = layer, shards, outs
        self.send, self.recv, self.local = send, recv, local
        self.section = lax.axis_index("section")
        self.index = lax.axis_index("fsdp")
        self.sibling = {"section": 1 - self.section}

    def across(self, bits, section=None):
        where = {"fsdp": self.index ^ bits}
        if section is not None:
            where["section"] = section
        return where

    def copy(self, m, slot, source, target, device):
        return remote(source, target, self.send.at[m, slot], self.recv.at[m, slot], device)

    def first(self, m, bits, half):
        slot = 0 if bits == 1 else 1
        return remote(
            self.shards[m].at[half],
            self.outs[m].at[self.index, half],
            self.send.at[m, slot + 8 * half],
            self.recv.at[m, slot],
            self.across(bits, half),
        )

    def arrived(self, m, bits):
        slot = 0 if bits == 1 else 1
        place = self.outs[m].at[self.index ^ bits, self.section]
        return self.copy(m, slot, place, place, self.across(bits))

    def own(self, m):
        return self.copy(m, 2, self.shards[m], self.outs[m].at[self.index], self.sibling)

    def keep(self, m):
        return pltpu.make_async_copy(
            self.shards[m], self.outs[m].at[self.index], self.local.at[m]
        )

    def corner(self, m, bits):
        middle = self.outs[m].shape[2] // 2
        rows = pl.ds(0, middle) if bits == 1 else pl.ds(middle, middle)
        place = self.outs[m].at[self.index ^ bits, self.section, rows]
        return self.copy(m, 3 if bits == 1 else 4, place, place, self.across(3 ^ bits))

    def trade(self, m, bits):
        place = self.outs[m].at[self.index ^ bits, self.section]
        return self.copy(m, 4 + bits, place, place, self.sibling)

    def start(self):
        @pl.when(self.section == self.layer)
        def _():
            for m in range(len(self.shards)):
                for half in (1 - self.layer, self.layer):
                    for bits in (1, 2):
                        self.first(m, bits, half).start()
                self.own(m).start()
                self.keep(m).start()

    def middle(self, m):
        for bits in (1, 2):
            self.arrived(m, bits).wait_recv()
            self.corner(m, bits).start()
            self.trade(m, bits).start()

    def last(self, m):
        for bits in (1, 2):
            self.corner(m, bits).wait_recv()
        self.trade(m, 3).start()

    def finish(self, m):
        for bits in (1, 2, 3):
            copy = self.trade(m, bits)
            copy.wait_send()
            copy.wait_recv()
        for bits in (1, 2):
            self.corner(m, bits).wait_send()

        @pl.when(self.section == self.layer)
        def _():
            for half in (0, 1):
                for bits in (1, 2):
                    self.first(m, bits, half).wait_send()
            self.own(m).wait_send()
            self.keep(m).wait()

        @pl.when(self.section != self.layer)
        def _():
            self.own(m).wait_recv()

    def partners(self):
        return [self.sibling] + [
            self.across(bits, half) for bits in (1, 2) for half in (0, 1)
        ]


def gather_kernel(layer, count, *refs):
    shards, outs = refs[:count], refs[count : 2 * count]
    gather = Gather(layer, shards, outs, *refs[2 * count :])
    greet(gather.partners())
    gather.start()
    for m in range(count):
        gather.middle(m)
        if m > 0:
            gather.last(m - 1)
    gather.last(count - 1)
    for m in range(count):
        gather.finish(m)


def gather_layer(layer, shards):
    count = len(shards)
    shards = [shard.reshape(2, -1, shard.shape[-1]) for shard in shards]
    outs = pl.pallas_call(
        functools.partial(gather_kernel, layer, count),
        in_specs=[ANY] * count,
        out_specs=[ANY] * count,
        out_shape=[jax.ShapeDtypeStruct((4,) + shard.shape, shard.dtype) for shard in shards],
        scratch_shapes=[
            pltpu.SemaphoreType.DMA((count, 10)),
            pltpu.SemaphoreType.DMA((count, 8)),
            pltpu.SemaphoreType.DMA((count,)),
        ],
        compiler_params=pltpu.CompilerParams(collective_id=layer, has_side_effects=True),
    )(*shards)
    return tuple(out.reshape(-1, out.shape[-1]) for out in outs)


class Reduce:
    def __init__(self, line, items, out, scratch):
        self.line, self.items, self.out = line, items, out
        (
            self.own,
            self.twin,
            self.near_corner,
            self.far_corner,
            self.near,
            self.far,
            self.outer,
            self.inner,
            self.partial,
            self.total,
            self.send,
            self.recv,
            self.local,
        ) = scratch
        self.section = lax.axis_index("section")
        self.index = lax.axis_index("fsdp")
        self.z = lax.axis_index("ctx")
        self.count = self.own.shape[0]
        self.sibling = {"section": 1 - self.section}
        self.x = {"fsdp": self.index ^ 1}
        self.y = {"fsdp": self.index ^ 2}
        self.is_inner = (self.z == 1) | (self.z == 2)
        self.end = {"ctx": jnp.where(self.z == 1, 0, 3)}
        self.toward = {"ctx": jnp.where(self.z == 0, 1, 2)}
        self.opposite = {"ctx": 3 - self.z}

    def chunks(self):
        k = 0
        for item in self.items:
            rows, columns = item.shape[2:]
            depth = self.own.shape[2]
            for row in range(0, rows, depth):
                for column in range(0, columns, CHUNK):
                    yield k, item, pl.ds(row, depth), pl.ds(column, CHUNK)
                    k += 1

    def copy(self, k, slot, source, target, device):
        return remote(source, target, self.send.at[slot, k], self.recv.at[slot, k], device)

    def swap(self, k):
        return self.copy(k, 0, self.twin.at[k], self.twin.at[k], self.sibling)

    def load(self, k):
        return pltpu.make_async_copy(self.own.at[k], self.own.at[k], self.local.at[k])

    def corner(self, k, near):
        half = self.own.shape[2] // 2
        rows = pl.ds(0, half) if near else pl.ds(half, half)
        source = self.own.at[k, self.index ^ 3, rows]
        target = (self.near_corner if near else self.far_corner).at[k]
        return self.copy(k, 1 if near else 2, source, target, self.x if near else self.y)

    def side(self, k, near):
        source = self.own.at[k, self.index ^ (1 if near else 2)]
        target = (self.near if near else self.far).at[k]
        return self.copy(k, 3 if near else 4, source, target, self.x if near else self.y)

    def inward(self, k):
        return self.copy(k, 5, self.partial.at[k], self.outer.at[k], self.toward)

    def across(self, k):
        return self.copy(k, 6, self.partial.at[k], self.inner.at[k], self.opposite)

    def outward(self, k):
        return self.copy(k, 7, self.total.at[k], self.total.at[k], self.end)

    def greet(self):
        barrier = pltpu.get_barrier_semaphore()

        def signal(device):
            pl.semaphore_signal(barrier, inc=1, device_id=device, device_id_type=MESH)

        for device in (self.sibling, self.x, self.y):
            signal(device)
        if not self.line:
            pl.semaphore_wait(barrier, 3)
            return

        @pl.when(self.is_inner)
        def _():
            signal(self.end)
            signal(self.opposite)
            pl.semaphore_wait(barrier, 5)

        @pl.when(jnp.logical_not(self.is_inner))
        def _():
            signal(self.toward)
            pl.semaphore_wait(barrier, 4)

    def start(self):
        for k, item, rows, columns in self.chunks():
            theirs = item.at[:, 1 - self.section, rows, columns]
            mine = item.at[:, self.section, rows, columns]
            self.copy(k, 0, theirs, self.twin.at[k], self.sibling).start()
            pltpu.make_async_copy(mine, self.own.at[k], self.local.at[k]).start()

    def stage(self, number, k):
        half = self.own.shape[2] // 2
        near, far = self.index ^ 1, self.index ^ 2
        if number == 0:
            self.load(k).wait()
            self.swap(k).wait_recv()
            for j in range(4):
                self.own[k, j] = self.own[k, j] + self.twin[k, j]
            self.corner(k, True).start()
            self.corner(k, False).start()
        elif number == 1:
            self.corner(k, True).wait_recv()
            self.corner(k, False).wait_recv()
            self.own[k, far, :half] = self.own[k, far, :half] + self.near_corner[k]
            self.own[k, near, half:] = self.own[k, near, half:] + self.far_corner[k]
            self.side(k, True).start()
            self.side(k, False).start()
        elif number == 2:
            self.side(k, True).wait_recv()
            self.side(k, False).wait_recv()
            summed = (
                self.own[k, self.index].astype(f32)
                + self.near[k].astype(f32)
                + self.far[k].astype(f32)
            ).astype(bf16)
            if not self.line:
                self.total[k] = summed
                return
            self.partial[k] = summed

            @pl.when(jnp.logical_not(self.is_inner))
            def _():
                self.inward(k).start()
        elif number == 3 and self.line:

            @pl.when(self.is_inner)
            def _():
                self.inward(k).wait_recv()
                self.partial[k] = self.partial[k] + self.outer[k]
                self.across(k).start()
        elif number == 4 and self.line:

            @pl.when(self.is_inner)
            def _():
                self.across(k).wait_recv()
                self.total[k] = self.partial[k] + self.inner[k]
                self.outward(k).start()

    def step(self, t, lags):
        for number, lag in enumerate(lags):
            k = t - lag

            @pl.when((k >= 0) & (k < self.count))
            def _():
                self.stage(number, k)

    def finish(self, k):
        self.swap(k).wait_send()
        for near in (True, False):
            self.corner(k, near).wait_send()
            self.side(k, near).wait_send()
        if self.line:

            @pl.when(self.is_inner)
            def _():
                self.across(k).wait_send()
                self.outward(k).wait_send()

            @pl.when(jnp.logical_not(self.is_inner))
            def _():
                self.inward(k).wait_send()
                self.outward(k).wait_recv()

    def write(self):
        copy = pltpu.make_async_copy(self.total, self.out, self.local.at[0])
        copy.start()
        copy.wait()


LAGS = (0, 1, 3, 4, 5)


def reduce_kernel(line, count, *refs):
    reduce = Reduce(line, refs[:count], refs[count], refs[count + 1 :])
    reduce.greet()
    reduce.start()

    def step(t, _):
        reduce.step(t, LAGS)
        return 0

    lax.fori_loop(0, reduce.count + LAGS[-1], step, 0)

    def finish(k, _):
        reduce.finish(k)
        return 0

    lax.fori_loop(0, reduce.count, finish, 0)
    reduce.write()


def reduce_scratch(count, depth):
    block = (count, depth, CHUNK)
    half = (count, depth // 2, CHUNK)
    return (
        [pltpu.VMEM((count, 4, depth, CHUNK), bf16)] * 2
        + [pltpu.VMEM(half, bf16)] * 2
        + [pltpu.VMEM(block, bf16)] * 6
        + [
            pltpu.SemaphoreType.DMA((8, count)),
            pltpu.SemaphoreType.DMA((8, count)),
            pltpu.SemaphoreType.DMA((count,)),
        ]
    )


def reduce_grads(collective, grads, line):
    items = [grad.reshape(4, 2, -1, grad.shape[-1]) for grad in grads]
    depth = min(item.shape[2] for item in items)
    count = sum((item.shape[2] // depth) * (item.shape[3] // CHUNK) for item in items)
    out = pl.pallas_call(
        functools.partial(reduce_kernel, line, len(items)),
        in_specs=[ANY] * len(items),
        out_specs=ANY,
        out_shape=jax.ShapeDtypeStruct((count, depth, CHUNK), bf16),
        scratch_shapes=reduce_scratch(count, depth),
        compiler_params=pltpu.CompilerParams(
            collective_id=collective, has_side_effects=True, vmem_limit_bytes=48 * 1024 * 1024
        ),
    )(*items)
    return out if line else lax.psum(out, "ctx")


def unchunk(blocks, shapes):
    depth = blocks.shape[-2]
    parts, k = [], 0
    for rows, columns in shapes:
        high, wide = rows // depth, columns // CHUNK
        part = blocks[..., k : k + high * wide, :, :]
        if wide > 1:
            part = jnp.concatenate([part[..., j, :, :] for j in range(wide)], axis=-1)
        parts.append(part.reshape(blocks.shape[:-3] + (rows, columns)))
        k += high * wide
    return parts


def swap(value):
    return lax.ppermute(value, "section", [(0, 1), (1, 0)])


def cross(value, bit):
    return lax.ppermute(value, "fsdp", [(i, i ^ bit) for i in range(4)])


def add(left, right):
    return (left.astype(f32) + right.astype(f32)).astype(left.dtype)


def gather_fsdp(shard):
    if lax.axis_size("fsdp") != 4:
        return lax.all_gather(shard, "fsdp", axis=0)
    half = shard.shape[0] // 2
    near = cross(shard, 1)
    far = cross(shard, 2)
    corner = jnp.concatenate([cross(far[:half], 1), cross(near[half:], 2)], axis=0)
    index = lax.axis_index("fsdp")
    even, low = index % 2 == 0, index < 2
    a, b = jnp.where(even, shard, near), jnp.where(even, near, shard)
    c, d = jnp.where(even, far, corner), jnp.where(even, corner, far)
    return jnp.stack(
        [jnp.where(low, a, c), jnp.where(low, b, d), jnp.where(low, c, a), jnp.where(low, d, b)]
    )


def scatter_fsdp(parts):
    if lax.axis_size("fsdp") != 4:
        return lax.psum_scatter(parts, "fsdp", scatter_dimension=0, tiled=False)
    index = lax.axis_index("fsdp")
    half = parts.shape[1] // 2

    def part(bits):
        return lax.dynamic_index_in_dim(parts, index ^ bits, 0, keepdims=False)

    corner, far, near = part(3), part(2), part(1)
    from_near = cross(corner[:half], 1)
    from_far = cross(corner[half:], 2)
    far = jnp.concatenate([add(far[:half], from_near), far[half:]], axis=0)
    near = jnp.concatenate([near[:half], add(near[half:], from_far)], axis=0)
    total = part(0).astype(f32) + cross(near, 1).astype(f32) + cross(far, 2).astype(f32)
    return total.astype(parts.dtype)


def sum_ctx(value):
    if lax.axis_size("ctx") != 4:
        return lax.psum(value, "ctx")
    index = lax.axis_index("ctx")
    inner = (index == 1) | (index == 2)
    value = add(value, lax.ppermute(value, "ctx", [(0, 1), (3, 2)]))
    value = add(value, lax.ppermute(value, "ctx", [(1, 2), (2, 1)]))
    return jnp.where(inner, value, lax.ppermute(value, "ctx", [(1, 0), (2, 3)]))


def shards(
    block_input,
    positions,
    cotangent,
    w_qkv,
    w_proj,
    w_fc,
    w_out,
    ln_gain,
    ln_bias,
    attn_bias,
    out_bias,
    fc_bias,
):
    section = lax.axis_index("section")
    ctx_index = lax.axis_index("ctx")
    first = section == 0
    sections = lax.axis_size("section")
    ctxs = lax.axis_size("ctx")
    fsdps = lax.axis_size("fsdp")
    local_seqs, local_rows, width = block_input.shape
    length = positions.shape[1]
    per = -(-local_seqs // (sections * ctxs))
    slots = sections * ctxs * per
    spare = slots - local_seqs
    shard_width = ln_gain.shape[2]

    def trade(value):
        other = swap(value)
        return jnp.where(first, value, other), jnp.where(first, other, value)

    pack = jnp.concatenate(
        [ln_gain[0], ln_bias[0], attn_bias[0], out_bias[0], fc_bias[0].reshape(-1, shard_width)]
    )
    pack = gather_fsdp(pack)
    packs = trade(pack)

    def unpack(packed):
        vectors = jnp.transpose(packed[:, :8], (1, 0, 2)).reshape(8, -1).astype(f32)
        fc = packed[:, 8:].reshape(-1).astype(f32)
        return vectors[0:2], vectors[2:4], vectors[4:6], vectors[6:8], fc

    smalls = [unpack(packed) for packed in packs]

    shards_own = [matrix[0] for matrix in (w_qkv, w_proj, w_fc, w_out)]
    weights = [gather_layer(layer, shards_own) for layer in range(2)]

    def own(padded):
        return lax.dynamic_slice_in_dim(padded, section * (ctxs * per), ctxs * per, 0)

    def bring(rows):
        padded = jnp.pad(rows, ((0, spare), (0, 0), (0, 0)))
        mine = own(padded).reshape(ctxs, per, local_rows, width)
        moved = lax.all_to_all(mine, "ctx", 0, 0, tiled=True)
        return jnp.transpose(moved, (1, 0, 2, 3)).reshape(per, length, width)

    places = own(jnp.pad(positions, ((0, spare), (0, 0)))).reshape(ctxs, per, length)
    places = lax.dynamic_index_in_dim(places, ctx_index, 0, keepdims=False)
    order = (
        lax.broadcasted_iota(jnp.int32, (per, length, length), 1) == places[:, None, :]
    ).astype(bf16)
    order_back = (
        lax.broadcasted_iota(jnp.int32, (per, length, length), 2) == places[:, :, None]
    ).astype(bf16)

    def to_sorted(rows):
        return (
            jnp.einsum("bpt,btd->bpd", order, rows, preferred_element_type=f32)
            .astype(bf16)
            .reshape(per * length, width)
        )

    def spread(rows):
        stored = jnp.einsum(
            "btp,bpd->btd", order_back, rows.reshape(per, length, width), preferred_element_type=f32
        ).astype(bf16)
        cut = stored.reshape(per, ctxs, local_rows, width)
        moved = lax.all_to_all(cut, "ctx", 1, 1, tiled=True)
        return jnp.transpose(moved, (1, 0, 2, 3)).reshape(ctxs * per, local_rows, width)

    def home(zero, one):
        arrived = swap(jnp.where(first, one, zero))
        mine = jnp.where(first, zero, one)
        low, high = jnp.where(first, mine, arrived), jnp.where(first, arrived, mine)
        return jnp.concatenate([low, high], axis=0)[:local_seqs][None]

    start = to_sorted(bring(block_input))
    grad_final = to_sorted(bring(cotangent))
    middle, kept_zero = layer_forward(weights[0], smalls[0], start, length)
    final, kept_one = layer_forward(weights[1], smalls[1], middle, length)
    out_zero = spread(middle)
    out_one = spread(final)

    def send(grad):
        return grad

    grad_middle, grads_one, small_one = layer_back(
        weights[1], smalls[1], kept_one, grad_final, length, send
    )
    grad_middle, out_zero, out_one = lax.optimization_barrier((grad_middle, out_zero, out_one))
    in_one = spread(grad_middle)
    grad_start, grads_zero, small_zero = layer_back(
        weights[0], smalls[0], kept_zero, grad_middle, length, send
    )
    section_out = home(out_zero, out_one)
    section_in_grad = home(spread(grad_start), in_one)

    line = ctxs == 4
    reduced_one = reduce_grads(2, grads_one, line)
    reduced_zero = reduce_grads(3, grads_zero, line)
    arrived = swap(jnp.where(first, reduced_one, reduced_zero))
    mine = jnp.where(first, reduced_zero, reduced_one)
    low = jnp.where(first, mine, arrived)
    high = jnp.where(first, arrived, mine)
    shapes = [(matrix.shape[1] // 2, matrix.shape[2]) for matrix in (w_qkv, w_proj, w_fc, w_out)]
    big = [
        jnp.concatenate([a, b], axis=0).astype(f32)[None]
        for a, b in zip(unchunk(low, shapes), unchunk(high, shapes))
    ]

    def repack(small):
        vectors, fc = small
        vectors = jnp.transpose(vectors.reshape(8, fsdps, shard_width), (1, 0, 2))
        return jnp.concatenate([vectors, fc.reshape(fsdps, -1, shard_width)], axis=1)

    pack_zero, pack_one = repack(small_zero), repack(small_one)
    arrived = swap(jnp.where(first, pack_one, pack_zero))
    packed = sum_ctx(scatter_fsdp(jnp.where(first, pack_zero, pack_one) + arrived))
    return (
        section_out,
        section_in_grad,
        *big,
        packed[None, 0:2],
        packed[None, 2:4],
        packed[None, 4:6],
        packed[None, 6:8],
        packed[8:].reshape(1, -1),
    )


def solution(mesh):
    matrix = P("section", "fsdp", None)
    vectors = P("section", None, "fsdp")
    rows_out = P("section", "fsdp", "ctx", None)
    return jax.shard_map(
        shards,
        mesh=mesh,
        in_specs=(
            P("fsdp", "ctx", None),
            P("fsdp", None),
            P("fsdp", "ctx", None),
            *([matrix] * 4),
            *([vectors] * 4),
            P("section", "fsdp"),
        ),
        out_specs=(
            rows_out,
            rows_out,
            *([matrix] * 4),
            *([vectors] * 4),
            P("section", "fsdp"),
        ),
        check_vma=False,
    )
```

```python
import functools

import jax
import jax.numpy as jnp
from jax import lax
from jax.experimental import pallas as pl
from jax.experimental.pallas import tpu as pltpu
from jax.sharding import PartitionSpec as P

H = 12
HD = 64
PAIR = 2 * HD
SCALE = HD**-0.5

masked_score = -1e30
norm_eps = 1e-05
f32 = jnp.float32
bf16 = jnp.bfloat16


def layer_norm(hidden, gain, offset):
    center = hidden - jnp.mean(hidden, axis=-1, keepdims=True)
    spread = jnp.mean(center * center, axis=-1, keepdims=True)
    return center * lax.rsqrt(spread + norm_eps) * gain + offset


def gelu_tanh(inputs):
    return jax.nn.gelu(inputs, approximate=True)


def mm(left, right):
    return lax.dot_general(left, right, (((1,), (0,)), ((), ())), preferred_element_type=f32)


def mm_nt(left, right):
    return lax.dot_general(left, right, (((1,), (1,)), ((), ())), preferred_element_type=f32)


def mm_tn(left, right):
    return lax.dot_general(left, right, (((0,), (0,)), ((), ())), preferred_element_type=f32)


def masked_scores(keys, queries, start, block):
    scores = mm_nt(keys, queries)
    down = lax.broadcasted_iota(jnp.int32, (block, block), 0)
    across = lax.broadcasted_iota(jnp.int32, (block, block), 1)
    corner = jnp.where(across >= down, scores[start:], masked_score)
    if start == 0:
        return corner
    return jnp.concatenate([scores[:start], corner], axis=0)


def attend_kernel(block, q_ref, k_ref, v_ref, o_ref, log_ref):
    length = q_ref.shape[0]
    for head in range(2):
        cols = slice(head * HD, (head + 1) * HD)
        for start in range(0, length, block):
            end = start + block
            queries = (q_ref[start:end, cols].astype(f32) * SCALE).astype(bf16)
            scores = masked_scores(k_ref[:end, cols], queries, start, block)
            top = jnp.max(scores, axis=0, keepdims=True)
            weights = jnp.exp(scores - top)
            total = jnp.sum(weights, axis=0, keepdims=True)
            mixed = mm_tn(v_ref[:end, cols], weights.astype(bf16)) / total
            o_ref[start:end, cols] = mixed.T.astype(bf16)
            log_ref[0, 0, head : head + 1, start:end] = top + jnp.log(total)


def attend_back_kernel(
    block, q_ref, k_ref, v_ref, do_ref, o_ref, log_ref, dq_ref, dk_ref, dv_ref, dk_sum, dv_sum
):
    length = q_ref.shape[0]
    for head in range(2):
        cols = slice(head * HD, (head + 1) * HD)
        for start in range(length - block, -1, -block):
            end = start + block
            queries = (q_ref[start:end, cols].astype(f32) * SCALE).astype(bf16)
            grads = do_ref[start:end, cols]
            product = grads.astype(f32) * o_ref[start:end, cols].astype(f32)
            delta = jnp.sum(product.T, axis=0, keepdims=True)
            keys = k_ref[:end, cols]
            scores = masked_scores(keys, queries, start, block)
            probs = jnp.exp(scores - log_ref[0, 0, head : head + 1, start:end])
            grad_probs = mm_nt(v_ref[:end, cols], grads)
            grad_scores = (probs * (grad_probs - delta)).astype(bf16)
            dv = mm(probs.astype(bf16), grads)
            dk = mm(grad_scores, queries)
            if end == length:
                dv_sum[:end, cols] = dv
                dk_sum[:end, cols] = dk
            else:
                dv_sum[:end, cols] += dv
                dk_sum[:end, cols] += dk
            dq = mm_tn(keys, grad_scores) * SCALE
            dq_ref[start:end, cols] = dq.T.astype(bf16)
    dk_ref[...] = dk_sum[...].astype(bf16)
    dv_ref[...] = dv_sum[...].astype(bf16)


def query_block(length):
    return 256 if length % 256 == 0 else length


def head_spec(length, offset):
    return pl.BlockSpec((length, PAIR), lambda b, h: (b, offset + h))


def log_spec(length):
    return pl.BlockSpec((1, 1, 2, length), lambda b, h: (b, h, 0, 0))


def attend_forward(project, length):
    rows = project.shape[0]
    count = rows // length
    pairs = H // 2
    return pl.pallas_call(
        functools.partial(attend_kernel, query_block(length)),
        grid=(count, pairs),
        in_specs=[head_spec(length, 0), head_spec(length, pairs), head_spec(length, 2 * pairs)],
        out_specs=[head_spec(length, 0), log_spec(length)],
        out_shape=[
            jax.ShapeDtypeStruct((rows, H * HD), bf16),
            jax.ShapeDtypeStruct((count, pairs, 2, length), f32),
        ],
        compiler_params=pltpu.CompilerParams(vmem_limit_bytes=40 * 1024 * 1024),
        cost_estimate=pl.CostEstimate(
            flops=8 * rows * length * H * HD,
            bytes_accessed=8 * rows * H * HD,
            transcendentals=rows * length * H // 2,
        ),
    )(project, project, project)


def attend_back(project, grad_mixed, mixed, log_total, length):
    rows = project.shape[0]
    count = rows // length
    pairs = H // 2
    return pl.pallas_call(
        functools.partial(attend_back_kernel, query_block(length)),
        grid=(count, pairs),
        in_specs=[
            head_spec(length, 0),
            head_spec(length, pairs),
            head_spec(length, 2 * pairs),
            head_spec(length, 0),
            head_spec(length, 0),
            log_spec(length),
        ],
        out_specs=[head_spec(length, 0)] * 3,
        out_shape=[jax.ShapeDtypeStruct((rows, H * HD), bf16)] * 3,
        scratch_shapes=[pltpu.VMEM((length, PAIR), f32)] * 2,
        compiler_params=pltpu.CompilerParams(vmem_limit_bytes=40 * 1024 * 1024),
        cost_estimate=pl.CostEstimate(
            flops=20 * rows * length * H * HD,
            bytes_accessed=16 * rows * H * HD,
            transcendentals=rows * length * H // 2,
        ),
    )(project, project, project, grad_mixed, mixed, log_total)


def layer_forward(weights, smalls, layer_in, attend):
    w_qkv, w_proj, w_fc, w_out = weights
    gains, offsets, attn_bias, out_bias, fc_bias = smalls
    hidden = layer_in.astype(f32)
    width = hidden.shape[-1]
    normed = layer_norm(hidden, gains[0], offsets[0]).astype(bf16)
    bias = jnp.concatenate([attn_bias[0], jnp.zeros((width,), f32), attn_bias[1]])
    project = (mm(normed, w_qkv) + bias).astype(bf16)
    mixed, log_total = attend(project)
    after = hidden + mm(mixed, w_proj) + out_bias[0]
    normed_two = layer_norm(after, gains[1], offsets[1]).astype(bf16)
    inner = mm(normed_two, w_fc) + fc_bias
    active = gelu_tanh(inner).astype(bf16)
    result = (after + mm(active, w_out) + out_bias[1]).astype(bf16)
    return result, (layer_in, normed, project, mixed, log_total, after, normed_two, inner, active)


def row_sum(rows):
    return jnp.sum(rows.astype(f32), axis=0)


def layer_back(weights, smalls, kept, grad_out, length, send):
    w_qkv, w_proj, w_fc, w_out = weights
    gains, offsets, attn_bias, out_bias, fc_bias = smalls
    layer_in, normed, project, mixed, log_total, after, normed_two, inner, active = kept
    grad_out, grad_w_out = lax.optimization_barrier(
        (grad_out, mm_tn(active, grad_out).astype(bf16))
    )
    grad_w_out = send(grad_w_out)
    grad_bias_two = row_sum(grad_out)
    grad_active = mm_nt(grad_out, w_out)
    _, gelu_pull = jax.vjp(gelu_tanh, inner)
    grad_inner = gelu_pull(grad_active)[0].astype(bf16)
    grad_inner, grad_w_fc = lax.optimization_barrier(
        (grad_inner, mm_tn(normed_two, grad_inner).astype(bf16))
    )
    grad_w_fc = send(grad_w_fc)
    grad_fc_bias = row_sum(grad_inner)
    grad_normed_two = mm_nt(grad_inner, w_fc)
    _, norm_pull = jax.vjp(layer_norm, after, gains[1], offsets[1])
    grad_after, grad_gain_two, grad_offset_two = norm_pull(grad_normed_two)
    grad_after = grad_after + grad_out.astype(f32)
    grad_branch = grad_after.astype(bf16)
    grad_branch, grad_w_proj = lax.optimization_barrier(
        (grad_branch, mm_tn(mixed, grad_branch).astype(bf16))
    )
    grad_w_proj = send(grad_w_proj)
    grad_bias_one = row_sum(grad_branch)
    grad_mixed = mm_nt(grad_branch, w_proj).astype(bf16)
    grad_q, grad_k, grad_v = attend_back(project, grad_mixed, mixed, log_total, length)
    grad_project = jnp.concatenate([grad_q, grad_k, grad_v], axis=-1)
    grad_project, grad_w_qkv = lax.optimization_barrier(
        (grad_project, mm_tn(normed, grad_project).astype(bf16))
    )
    grad_w_qkv = send(grad_w_qkv)
    grad_normed = mm_nt(grad_project, w_qkv)
    _, first_pull = jax.vjp(layer_norm, layer_in.astype(f32), gains[0], offsets[0])
    grad_hidden, grad_gain_one, grad_offset_one = first_pull(grad_normed)
    grad_input = (grad_after + grad_hidden).astype(bf16)
    small = (
        jnp.stack(
            [
                grad_gain_one,
                grad_gain_two,
                grad_offset_one,
                grad_offset_two,
                row_sum(grad_q),
                row_sum(grad_v),
                grad_bias_one,
                grad_bias_two,
            ]
        ),
        grad_fc_bias,
    )
    return grad_input, (grad_w_qkv, grad_w_proj, grad_w_fc, grad_w_out), small


MESH = pl.DeviceIdType.MESH
ANY = pl.BlockSpec(memory_space=pl.ANY)
CHUNK = 768


def greet(partners):
    barrier = pltpu.get_barrier_semaphore()
    for partner in partners:
        pl.semaphore_signal(barrier, inc=1, device_id=partner, device_id_type=MESH)
    pl.semaphore_wait(barrier, len(partners))


def remote(source, target, send, recv, device):
    return pltpu.make_async_remote_copy(
        src_ref=source,
        dst_ref=target,
        send_sem=send,
        recv_sem=recv,
        device_id=device,
        device_id_type=MESH,
    )


class Gather:
    def __init__(self, layer, shards, outs, send, recv, local, *bounce):
        self.layer, self.shards, self.outs = layer, shards, outs
        self.bounce = bounce
        self.send, self.recv, self.local = send, recv, local
        self.section = lax.axis_index("section")
        self.index = lax.axis_index("fsdp")
        self.sibling = {"section": 1 - self.section}

    def across(self, bits, section=None):
        where = {"fsdp": self.index ^ bits}
        if section is not None:
            where["section"] = section
        return where

    def copy(self, m, slot, source, target, device):
        return remote(source, target, self.send.at[m, slot], self.recv.at[m, slot], device)

    def first(self, m, bits, half):
        slot = 0 if bits == 1 else 1
        return remote(
            self.shards[m].at[half],
            self.outs[m].at[self.index, half],
            self.send.at[m, slot + 8 * half],
            self.recv.at[m, slot],
            self.across(bits, half),
        )

    def arrived(self, m, bits):
        slot = 0 if bits == 1 else 1
        place = self.outs[m].at[self.index ^ bits, self.section]
        return self.copy(m, slot, place, place, self.across(bits))

    def own(self, m):
        return self.copy(m, 2, self.shards[m], self.outs[m].at[self.index], self.sibling)

    def take(self, m):
        return pltpu.make_async_copy(self.shards[m], self.bounce[m], self.local.at[0, m])

    def keep(self, m):
        return pltpu.make_async_copy(
            self.bounce[m], self.outs[m].at[self.index], self.local.at[1, m]
        )

    def corner(self, m, bits):
        middle = self.outs[m].shape[2] // 2
        rows = pl.ds(0, middle) if bits == 1 else pl.ds(middle, middle)
        place = self.outs[m].at[self.index ^ bits, self.section, rows]
        return self.copy(m, 3 if bits == 1 else 4, place, place, self.across(3 ^ bits))

    def trade(self, m, bits):
        place = self.outs[m].at[self.index ^ bits, self.section]
        return self.copy(m, 4 + bits, place, place, self.sibling)

    def start(self):
        @pl.when(self.section == self.layer)
        def _():
            for m in range(len(self.shards)):
                for half in (1 - self.layer, self.layer):
                    for bits in (1, 2):
                        self.first(m, bits, half).start()
                self.own(m).start()
                self.take(m).start()
            for m in range(len(self.shards)):
                self.take(m).wait()
                self.keep(m).start()

    def middle(self, m):
        for bits in (1, 2):
            self.arrived(m, bits).wait_recv()
            self.corner(m, bits).start()
            self.trade(m, bits).start()

    def last(self, m):
        for bits in (1, 2):
            self.corner(m, bits).wait_recv()
        self.trade(m, 3).start()

    def finish(self, m):
        for bits in (1, 2, 3):
            copy = self.trade(m, bits)
            copy.wait_send()
            copy.wait_recv()
        for bits in (1, 2):
            self.corner(m, bits).wait_send()

        @pl.when(self.section == self.layer)
        def _():
            for half in (0, 1):
                for bits in (1, 2):
                    self.first(m, bits, half).wait_send()
            self.own(m).wait_send()
            self.keep(m).wait()

        @pl.when(self.section != self.layer)
        def _():
            self.own(m).wait_recv()

    def partners(self):
        return [self.sibling] + [
            self.across(bits, half) for bits in (1, 2) for half in (0, 1)
        ]


def gather_kernel(layer, count, *refs):
    shards, outs = refs[:count], refs[count : 2 * count]
    gather = Gather(layer, shards, outs, *refs[2 * count :])
    greet(gather.partners())
    gather.start()
    for m in range(count):
        gather.middle(m)
        if m > 0:
            gather.last(m - 1)
    gather.last(count - 1)
    for m in range(count):
        gather.finish(m)


def gather_scratch(shards):
    count = len(shards)
    return [
        pltpu.SemaphoreType.DMA((count, 10)),
        pltpu.SemaphoreType.DMA((count, 8)),
        pltpu.SemaphoreType.DMA((2, count)),
    ] + [pltpu.VMEM(shard.shape, shard.dtype) for shard in shards]


def gather_shapes(shards):
    return [jax.ShapeDtypeStruct((4,) + shard.shape, shard.dtype) for shard in shards]


def split_shards(shards):
    return [shard.reshape(2, -1, shard.shape[-1]) for shard in shards]


def join_shards(outs):
    return tuple(out.reshape(-1, out.shape[-1]) for out in outs)


def gather_layer(layer, shards):
    count = len(shards)
    shards = split_shards(shards)
    outs = pl.pallas_call(
        functools.partial(gather_kernel, layer, count),
        in_specs=[ANY] * count,
        out_specs=[ANY] * count,
        out_shape=gather_shapes(shards),
        scratch_shapes=gather_scratch(shards),
        compiler_params=pltpu.CompilerParams(
            collective_id=0, has_side_effects=True, vmem_limit_bytes=40 * 1024 * 1024
        ),
    )(*shards)
    return join_shards(outs)


class Reduce:
    def __init__(self, line, items, out, scratch):
        self.line, self.items, self.out = line, items, out
        (
            self.own,
            self.twin,
            self.near_corner,
            self.far_corner,
            self.near,
            self.far,
            self.outer,
            self.inner,
            self.partial,
            self.total,
            self.send,
            self.recv,
            self.local,
        ) = scratch
        self.section = lax.axis_index("section")
        self.index = lax.axis_index("fsdp")
        self.z = lax.axis_index("ctx")
        self.count = self.own.shape[0]
        self.sibling = {"section": 1 - self.section}
        self.x = {"fsdp": self.index ^ 1}
        self.y = {"fsdp": self.index ^ 2}
        self.is_inner = (self.z == 1) | (self.z == 2)
        self.end = {"ctx": jnp.where(self.z == 1, 0, 3)}
        self.toward = {"ctx": jnp.where(self.z == 0, 1, 2)}
        self.opposite = {"ctx": 3 - self.z}

    def chunks(self):
        k = 0
        for item in self.items:
            rows, columns = item.shape[2:]
            depth = self.own.shape[2]
            for row in range(0, rows, depth):
                for column in range(0, columns, CHUNK):
                    yield k, item, pl.ds(row, depth), pl.ds(column, CHUNK)
                    k += 1

    def copy(self, k, slot, source, target, device):
        return remote(source, target, self.send.at[slot, k], self.recv.at[slot, k], device)

    def swap(self, k):
        return self.copy(k, 0, self.twin.at[k], self.twin.at[k], self.sibling)

    def load(self, k):
        return pltpu.make_async_copy(self.own.at[k], self.own.at[k], self.local.at[k])

    def corner(self, k, near):
        half = self.own.shape[2] // 2
        rows = pl.ds(0, half) if near else pl.ds(half, half)
        source = self.own.at[k, self.index ^ 3, rows]
        target = (self.near_corner if near else self.far_corner).at[k]
        return self.copy(k, 1 if near else 2, source, target, self.x if near else self.y)

    def side(self, k, near):
        source = self.own.at[k, self.index ^ (1 if near else 2)]
        target = (self.near if near else self.far).at[k]
        return self.copy(k, 3 if near else 4, source, target, self.x if near else self.y)

    def inward(self, k):
        return self.copy(k, 5, self.partial.at[k], self.outer.at[k], self.toward)

    def across(self, k):
        return self.copy(k, 6, self.partial.at[k], self.inner.at[k], self.opposite)

    def outward(self, k):
        return self.copy(k, 7, self.total.at[k], self.total.at[k], self.end)

    def greet(self):
        barrier = pltpu.get_barrier_semaphore()

        def signal(device):
            pl.semaphore_signal(barrier, inc=1, device_id=device, device_id_type=MESH)

        for device in (self.sibling, self.x, self.y):
            signal(device)
        if not self.line:
            pl.semaphore_wait(barrier, 3)
            return

        @pl.when(self.is_inner)
        def _():
            signal(self.end)
            signal(self.opposite)
            pl.semaphore_wait(barrier, 5)

        @pl.when(jnp.logical_not(self.is_inner))
        def _():
            signal(self.toward)
            pl.semaphore_wait(barrier, 4)

    def start(self):
        for k, item, rows, columns in self.chunks():
            theirs = item.at[:, 1 - self.section, rows, columns]
            mine = item.at[:, self.section, rows, columns]
            self.copy(k, 0, theirs, self.twin.at[k], self.sibling).start()
            pltpu.make_async_copy(mine, self.own.at[k], self.local.at[k]).start()

    def stage(self, number, k):
        half = self.own.shape[2] // 2
        near, far = self.index ^ 1, self.index ^ 2
        if number == 0:
            self.load(k).wait()
            self.swap(k).wait_recv()
            for j in range(4):
                self.own[k, j] = self.own[k, j] + self.twin[k, j]
            self.corner(k, True).start()
            self.corner(k, False).start()
        elif number == 1:
            self.corner(k, True).wait_recv()
            self.corner(k, False).wait_recv()
            self.own[k, far, :half] = self.own[k, far, :half] + self.near_corner[k]
            self.own[k, near, half:] = self.own[k, near, half:] + self.far_corner[k]
            self.side(k, True).start()
            self.side(k, False).start()
        elif number == 2:
            self.side(k, True).wait_recv()
            self.side(k, False).wait_recv()
            summed = (
                self.own[k, self.index].astype(f32)
                + self.near[k].astype(f32)
                + self.far[k].astype(f32)
            ).astype(bf16)
            if not self.line:
                self.total[k] = summed
                return
            self.partial[k] = summed

            @pl.when(jnp.logical_not(self.is_inner))
            def _():
                self.inward(k).start()
        elif number == 3 and self.line:

            @pl.when(self.is_inner)
            def _():
                self.inward(k).wait_recv()
                self.partial[k] = self.partial[k] + self.outer[k]
                self.across(k).start()
        elif number == 4 and self.line:

            @pl.when(self.is_inner)
            def _():
                self.across(k).wait_recv()
                self.total[k] = self.partial[k] + self.inner[k]
                self.outward(k).start()

    def step(self, t, lags):
        for number, lag in enumerate(lags):
            k = t - lag

            @pl.when((k >= 0) & (k < self.count))
            def _():
                self.stage(number, k)

    def finish(self, k):
        self.swap(k).wait_send()
        for near in (True, False):
            self.corner(k, near).wait_send()
            self.side(k, near).wait_send()
        if self.line:

            @pl.when(self.is_inner)
            def _():
                self.across(k).wait_send()
                self.outward(k).wait_send()

            @pl.when(jnp.logical_not(self.is_inner))
            def _():
                self.inward(k).wait_send()
                self.outward(k).wait_recv()

    def write(self):
        copy = pltpu.make_async_copy(self.total, self.out, self.local.at[0])
        copy.start()
        copy.wait()


LAGS = (0, 1, 3, 4, 5)


def reduce_kernel(line, count, *refs):
    reduce = Reduce(line, refs[:count], refs[count], refs[count + 1 :])
    reduce.greet()
    reduce.start()

    def step(t, _):
        reduce.step(t, LAGS)
        return 0

    lax.fori_loop(0, reduce.count + LAGS[-1], step, 0)

    def finish(k, _):
        reduce.finish(k)
        return 0

    lax.fori_loop(0, reduce.count, finish, 0)
    reduce.write()


def reduce_scratch(count, depth):
    block = (count, depth, CHUNK)
    half = (count, depth // 2, CHUNK)
    return (
        [pltpu.VMEM((count, 4, depth, CHUNK), bf16)] * 2
        + [pltpu.VMEM(half, bf16)] * 2
        + [pltpu.VMEM(block, bf16)] * 6
        + [
            pltpu.SemaphoreType.DMA((8, count)),
            pltpu.SemaphoreType.DMA((8, count)),
            pltpu.SemaphoreType.DMA((count,)),
        ]
    )


def reduce_grads(collective, grads, line):
    items = [grad.reshape(4, 2, -1, grad.shape[-1]) for grad in grads]
    depth = min(item.shape[2] for item in items)
    count = sum((item.shape[2] // depth) * (item.shape[3] // CHUNK) for item in items)
    out = pl.pallas_call(
        functools.partial(reduce_kernel, line, len(items)),
        in_specs=[ANY] * len(items),
        out_specs=ANY,
        out_shape=jax.ShapeDtypeStruct((count, depth, CHUNK), bf16),
        scratch_shapes=reduce_scratch(count, depth),
        compiler_params=pltpu.CompilerParams(
            collective_id=collective, has_side_effects=True, vmem_limit_bytes=48 * 1024 * 1024
        ),
    )(*items)
    return out if line else lax.psum(out, "ctx")


def unchunk(blocks, shapes):
    depth = blocks.shape[-2]
    parts, k = [], 0
    for rows, columns in shapes:
        high, wide = rows // depth, columns // CHUNK
        part = blocks[..., k : k + high * wide, :, :]
        if wide > 1:
            part = jnp.concatenate([part[..., j, :, :] for j in range(wide)], axis=-1)
        parts.append(part.reshape(blocks.shape[:-3] + (rows, columns)))
        k += high * wide
    return parts


def attend_gather_kernel(block, layer, count, q_ref, k_ref, v_ref, *refs):
    shards = refs[:count]
    o_ref, log_ref = refs[count : count + 2]
    outs = refs[count + 2 : 2 * count + 2]
    gather = Gather(layer, shards, outs, *refs[2 * count + 2 :])
    head = pl.program_id(1)
    steps = H // 2
    once = pl.program_id(0) == 0

    @pl.when(once & (head == 0))
    def _():
        greet(gather.partners())
        gather.start()

    for m in range(count):

        @pl.when(once & (head == steps - 2 - count + m))
        def _():
            gather.middle(m)

    @pl.when(once & (head == steps - 1))
    def _():
        for m in range(count):
            gather.last(m)

    attend_kernel(block, q_ref, k_ref, v_ref, o_ref, log_ref)

    @pl.when(once & (head == steps - 1))
    def _():
        for m in range(count):
            gather.finish(m)


def attend_gather(project, length, layer, shards):
    rows = project.shape[0]
    count = rows // length
    pairs = H // 2
    shards = split_shards(shards)
    mixed, log_total, *outs = pl.pallas_call(
        functools.partial(attend_gather_kernel, query_block(length), layer, len(shards)),
        grid=(count, pairs),
        in_specs=[head_spec(length, 0), head_spec(length, pairs), head_spec(length, 2 * pairs)]
        + [ANY] * len(shards),
        out_specs=[head_spec(length, 0), log_spec(length)] + [ANY] * len(shards),
        out_shape=[
            jax.ShapeDtypeStruct((rows, H * HD), bf16),
            jax.ShapeDtypeStruct((count, pairs, 2, length), f32),
        ]
        + gather_shapes(shards),
        scratch_shapes=gather_scratch(shards),
        compiler_params=pltpu.CompilerParams(
            collective_id=1, has_side_effects=True, vmem_limit_bytes=40 * 1024 * 1024
        ),
        cost_estimate=pl.CostEstimate(
            flops=8 * rows * length * H * HD,
            bytes_accessed=8 * rows * H * HD,
            transcendentals=rows * length * H // 2,
        ),
    )(project, project, project, *shards)
    return (mixed, log_total), join_shards(outs)


def swap(value):
    return lax.ppermute(value, "section", [(0, 1), (1, 0)])


def cross(value, bit):
    return lax.ppermute(value, "fsdp", [(i, i ^ bit) for i in range(4)])


def add(left, right):
    return (left.astype(f32) + right.astype(f32)).astype(left.dtype)


def gather_fsdp(shard):
    if lax.axis_size("fsdp") != 4:
        return lax.all_gather(shard, "fsdp", axis=0)
    half = shard.shape[0] // 2
    near = cross(shard, 1)
    far = cross(shard, 2)
    corner = jnp.concatenate([cross(far[:half], 1), cross(near[half:], 2)], axis=0)
    index = lax.axis_index("fsdp")
    even, low = index % 2 == 0, index < 2
    a, b = jnp.where(even, shard, near), jnp.where(even, near, shard)
    c, d = jnp.where(even, far, corner), jnp.where(even, corner, far)
    return jnp.stack(
        [jnp.where(low, a, c), jnp.where(low, b, d), jnp.where(low, c, a), jnp.where(low, d, b)]
    )


def scatter_fsdp(parts):
    if lax.axis_size("fsdp") != 4:
        return lax.psum_scatter(parts, "fsdp", scatter_dimension=0, tiled=False)
    index = lax.axis_index("fsdp")
    half = parts.shape[1] // 2

    def part(bits):
        return lax.dynamic_index_in_dim(parts, index ^ bits, 0, keepdims=False)

    corner, far, near = part(3), part(2), part(1)
    from_near = cross(corner[:half], 1)
    from_far = cross(corner[half:], 2)
    far = jnp.concatenate([add(far[:half], from_near), far[half:]], axis=0)
    near = jnp.concatenate([near[:half], add(near[half:], from_far)], axis=0)
    total = part(0).astype(f32) + cross(near, 1).astype(f32) + cross(far, 2).astype(f32)
    return total.astype(parts.dtype)


def sum_ctx(value):
    if lax.axis_size("ctx") != 4:
        return lax.psum(value, "ctx")
    index = lax.axis_index("ctx")
    inner = (index == 1) | (index == 2)
    value = add(value, lax.ppermute(value, "ctx", [(0, 1), (3, 2)]))
    value = add(value, lax.ppermute(value, "ctx", [(1, 2), (2, 1)]))
    return jnp.where(inner, value, lax.ppermute(value, "ctx", [(1, 0), (2, 3)]))


def shards(
    block_input,
    positions,
    cotangent,
    w_qkv,
    w_proj,
    w_fc,
    w_out,
    ln_gain,
    ln_bias,
    attn_bias,
    out_bias,
    fc_bias,
):
    section = lax.axis_index("section")
    ctx_index = lax.axis_index("ctx")
    first = section == 0
    sections = lax.axis_size("section")
    ctxs = lax.axis_size("ctx")
    fsdps = lax.axis_size("fsdp")
    local_seqs, local_rows, width = block_input.shape
    length = positions.shape[1]
    per = -(-local_seqs // (sections * ctxs))
    slots = sections * ctxs * per
    spare = slots - local_seqs
    shard_width = ln_gain.shape[2]

    def trade(value):
        other = swap(value)
        return jnp.where(first, value, other), jnp.where(first, other, value)

    pack = jnp.concatenate(
        [ln_gain[0], ln_bias[0], attn_bias[0], out_bias[0], fc_bias[0].reshape(-1, shard_width)]
    )
    pack = gather_fsdp(pack)
    packs = trade(pack)

    def unpack(packed):
        vectors = jnp.transpose(packed[:, :8], (1, 0, 2)).reshape(8, -1).astype(f32)
        fc = packed[:, 8:].reshape(-1).astype(f32)
        return vectors[0:2], vectors[2:4], vectors[4:6], vectors[6:8], fc

    smalls = [unpack(packed) for packed in packs]

    shards_own = [matrix[0] for matrix in (w_qkv, w_proj, w_fc, w_out)]
    weights_zero = gather_layer(0, shards_own)
    pieces = []
    for matrix in shards_own[2:]:
        rows = matrix.shape[0] // 2
        arrived = swap(jnp.where(first, matrix[rows:], matrix[:rows]))
        pieces.append(jnp.where(first, arrived, matrix[rows:]))
    weights_zero, pieces = lax.optimization_barrier((weights_zero, pieces))
    late = [lax.all_gather(piece, ("fsdp", "section"), axis=0, tiled=True) for piece in pieces]

    def own(padded):
        return lax.dynamic_slice_in_dim(padded, section * (ctxs * per), ctxs * per, 0)

    def bring(rows):
        padded = jnp.pad(rows, ((0, spare), (0, 0), (0, 0)))
        mine = own(padded).reshape(ctxs, per, local_rows, width)
        moved = lax.all_to_all(mine, "ctx", 0, 0, tiled=True)
        return jnp.transpose(moved, (1, 0, 2, 3)).reshape(per, length, width)

    places = own(jnp.pad(positions, ((0, spare), (0, 0)))).reshape(ctxs, per, length)
    places = lax.dynamic_index_in_dim(places, ctx_index, 0, keepdims=False)
    order = (
        lax.broadcasted_iota(jnp.int32, (per, length, length), 1) == places[:, None, :]
    ).astype(bf16)
    order_back = (
        lax.broadcasted_iota(jnp.int32, (per, length, length), 2) == places[:, :, None]
    ).astype(bf16)

    def to_sorted(rows):
        return (
            jnp.einsum("bpt,btd->bpd", order, rows, preferred_element_type=f32)
            .astype(bf16)
            .reshape(per * length, width)
        )

    def spread(rows):
        stored = jnp.einsum(
            "btp,bpd->btd", order_back, rows.reshape(per, length, width), preferred_element_type=f32
        ).astype(bf16)
        cut = stored.reshape(per, ctxs, local_rows, width)
        moved = lax.all_to_all(cut, "ctx", 1, 1, tiled=True)
        return jnp.transpose(moved, (1, 0, 2, 3)).reshape(ctxs * per, local_rows, width)

    def home(zero, one):
        arrived = swap(jnp.where(first, one, zero))
        mine = jnp.where(first, zero, one)
        low, high = jnp.where(first, mine, arrived), jnp.where(first, arrived, mine)
        return jnp.concatenate([low, high], axis=0)[:local_seqs][None]

    start = to_sorted(bring(block_input))
    grad_final = to_sorted(bring(cotangent))
    early = []

    def attend_zero(project):
        attended, gathered = attend_gather(project, length, 1, shards_own[:2])
        early.extend(gathered)
        return attended

    middle, kept_zero = layer_forward(weights_zero, smalls[0], start, attend_zero)
    weights = [weights_zero, (*early, *late)]
    final, kept_one = layer_forward(
        weights[1], smalls[1], middle, lambda project: attend_forward(project, length)
    )
    out_zero = spread(middle)
    out_one = spread(final)

    def send(grad):
        return grad

    grad_middle, grads_one, small_one = layer_back(
        weights[1], smalls[1], kept_one, grad_final, length, send
    )
    grad_middle, out_zero, out_one = lax.optimization_barrier((grad_middle, out_zero, out_one))
    in_one = spread(grad_middle)
    grad_start, grads_zero, small_zero = layer_back(
        weights[0], smalls[0], kept_zero, grad_middle, length, send
    )
    section_out = home(out_zero, out_one)
    section_in_grad = home(spread(grad_start), in_one)

    def repack(small):
        vectors, fc = small
        vectors = jnp.transpose(vectors.reshape(8, fsdps, shard_width), (1, 0, 2))
        packed = jnp.concatenate([vectors, fc.reshape(fsdps, -1, shard_width)], axis=1)
        packed = packed.reshape(fsdps, 1, -1, CHUNK)
        depth = w_qkv.shape[1] // 2
        return jnp.pad(packed, ((0, 0), (0, 0), (0, depth - packed.shape[2]), (0, 0))).astype(bf16)

    line = ctxs == 4
    reduced_one = reduce_grads(2, grads_one, line)
    pack = jnp.concatenate([repack(small_zero), repack(small_one)], axis=1)
    pack = pack.reshape(-1, CHUNK)
    reduced_zero = reduce_grads(3, (*grads_zero, pack), line)
    packed = reduced_zero[-1].reshape(-1, shard_width)[:12].astype(f32)
    reduced_zero = reduced_zero[:-1]
    arrived = swap(jnp.where(first, reduced_one, reduced_zero))
    mine = jnp.where(first, reduced_zero, reduced_one)
    low = jnp.where(first, mine, arrived)
    high = jnp.where(first, arrived, mine)
    shapes = [(matrix.shape[1] // 2, matrix.shape[2]) for matrix in (w_qkv, w_proj, w_fc, w_out)]
    big = [
        jnp.concatenate([a, b], axis=0).astype(f32)[None]
        for a, b in zip(unchunk(low, shapes), unchunk(high, shapes))
    ]

    return (
        section_out,
        section_in_grad,
        *big,
        packed[None, 0:2],
        packed[None, 2:4],
        packed[None, 4:6],
        packed[None, 6:8],
        packed[8:].reshape(1, -1),
    )


def solution(mesh):
    matrix = P("section", "fsdp", None)
    vectors = P("section", None, "fsdp")
    rows_out = P("section", "fsdp", "ctx", None)
    return jax.shard_map(
        shards,
        mesh=mesh,
        in_specs=(
            P("fsdp", "ctx", None),
            P("fsdp", None),
            P("fsdp", "ctx", None),
            *([matrix] * 4),
            *([vectors] * 4),
            P("section", "fsdp"),
        ),
        out_specs=(
            rows_out,
            rows_out,
            *([matrix] * 4),
            *([vectors] * 4),
            P("section", "fsdp"),
        ),
        check_vma=False,
    )
```

```python
import functools

import jax
import jax.numpy as jnp
from jax import lax
from jax.experimental import pallas as pl
from jax.experimental.pallas import tpu as pltpu
from jax.sharding import PartitionSpec as P

H = 12
HD = 64
PAIR = 2 * HD
SCALE = HD**-0.5

masked_score = -1e30
norm_eps = 1e-05
f32 = jnp.float32
bf16 = jnp.bfloat16


def layer_norm(hidden, gain, offset):
    center = hidden - jnp.mean(hidden, axis=-1, keepdims=True)
    spread = jnp.mean(center * center, axis=-1, keepdims=True)
    return center * lax.rsqrt(spread + norm_eps) * gain + offset


def gelu_tanh(inputs):
    return jax.nn.gelu(inputs, approximate=True)


def mm(left, right):
    return lax.dot_general(left, right, (((1,), (0,)), ((), ())), preferred_element_type=f32)


def mm_nt(left, right):
    return lax.dot_general(left, right, (((1,), (1,)), ((), ())), preferred_element_type=f32)


def mm_tn(left, right):
    return lax.dot_general(left, right, (((0,), (0,)), ((), ())), preferred_element_type=f32)


def masked_scores(keys, queries, start, block):
    scores = mm_nt(keys, queries)
    down = lax.broadcasted_iota(jnp.int32, (block, block), 0)
    across = lax.broadcasted_iota(jnp.int32, (block, block), 1)
    corner = jnp.where(across >= down, scores[start:], masked_score)
    if start == 0:
        return corner
    return jnp.concatenate([scores[:start], corner], axis=0)


def attend_kernel(block, q_ref, k_ref, v_ref, o_ref, log_ref):
    length = q_ref.shape[0]
    for head in range(2):
        cols = slice(head * HD, (head + 1) * HD)
        for start in range(0, length, block):
            end = start + block
            queries = (q_ref[start:end, cols].astype(f32) * SCALE).astype(bf16)
            scores = masked_scores(k_ref[:end, cols], queries, start, block)
            top = jnp.max(scores, axis=0, keepdims=True)
            weights = jnp.exp(scores - top)
            total = jnp.sum(weights, axis=0, keepdims=True)
            mixed = mm_tn(v_ref[:end, cols], weights.astype(bf16)) / total
            o_ref[start:end, cols] = mixed.T.astype(bf16)
            log_ref[0, 0, head : head + 1, start:end] = top + jnp.log(total)


def attend_back_kernel(
    block, q_ref, k_ref, v_ref, do_ref, o_ref, log_ref, dq_ref, dk_ref, dv_ref, dk_sum, dv_sum
):
    length = q_ref.shape[0]
    for head in range(2):
        cols = slice(head * HD, (head + 1) * HD)
        for start in range(length - block, -1, -block):
            end = start + block
            queries = (q_ref[start:end, cols].astype(f32) * SCALE).astype(bf16)
            grads = do_ref[start:end, cols]
            product = grads.astype(f32) * o_ref[start:end, cols].astype(f32)
            delta = jnp.sum(product.T, axis=0, keepdims=True)
            keys = k_ref[:end, cols]
            scores = masked_scores(keys, queries, start, block)
            probs = jnp.exp(scores - log_ref[0, 0, head : head + 1, start:end])
            grad_probs = mm_nt(v_ref[:end, cols], grads)
            grad_scores = (probs * (grad_probs - delta)).astype(bf16)
            dv = mm(probs.astype(bf16), grads)
            dk = mm(grad_scores, queries)
            if end == length:
                dv_sum[:end, cols] = dv
                dk_sum[:end, cols] = dk
            else:
                dv_sum[:end, cols] += dv
                dk_sum[:end, cols] += dk
            dq = mm_tn(keys, grad_scores) * SCALE
            dq_ref[start:end, cols] = dq.T.astype(bf16)
    dk_ref[...] = dk_sum[...].astype(bf16)
    dv_ref[...] = dv_sum[...].astype(bf16)


def query_block(length):
    return 256 if length % 256 == 0 else length


def head_spec(length, offset):
    return pl.BlockSpec((length, PAIR), lambda b, h: (b, offset + h))


def log_spec(length):
    return pl.BlockSpec((1, 1, 2, length), lambda b, h: (b, h, 0, 0))


def attend_forward(project, length, stay, stored):
    rows = project.shape[0]
    count = rows // length
    pairs = H // 2
    seats = Seats(stored[0])
    body = functools.partial(attend_kernel, query_block(length))
    return pl.pallas_call(
        functools.partial(carry_deliver, body, 3, 2, 0),
        grid=(count, pairs),
        in_specs=[head_spec(length, 0), head_spec(length, pairs), head_spec(length, 2 * pairs), ANY],
        out_specs=[head_spec(length, 0), log_spec(length), ANY],
        out_shape=[
            jax.ShapeDtypeStruct((rows, H * HD), bf16),
            jax.ShapeDtypeStruct((count, pairs, 2, length), f32),
            jax.ShapeDtypeStruct(stored, bf16),
        ],
        scratch_shapes=Deliver.scratch(stored[0], seats.per, seats.places),
        compiler_params=pltpu.CompilerParams(
            collective_id=4, has_side_effects=True, vmem_limit_bytes=40 * 1024 * 1024
        ),
        cost_estimate=pl.CostEstimate(
            flops=8 * rows * length * H * HD,
            bytes_accessed=8 * rows * H * HD,
            transcendentals=rows * length * H // 2,
        ),
    )(project, project, project, stay)


def attend_back(project, grad_mixed, mixed, log_total, length, stay, stored):
    rows = project.shape[0]
    count = rows // length
    pairs = H // 2
    seats = Seats(stored[0])
    body = functools.partial(attend_back_kernel, query_block(length))
    if stay is not None:
        body = functools.partial(carry_deliver, body, 6, 3, 1)
    carried = int(stay is not None)
    return pl.pallas_call(
        body,
        grid=(count, pairs),
        in_specs=[
            head_spec(length, 0),
            head_spec(length, pairs),
            head_spec(length, 2 * pairs),
            head_spec(length, 0),
            head_spec(length, 0),
            log_spec(length),
        ]
        + [ANY] * carried,
        out_specs=[head_spec(length, 0)] * 3 + [ANY] * carried,
        out_shape=[jax.ShapeDtypeStruct((rows, H * HD), bf16)] * 3
        + [jax.ShapeDtypeStruct(stored, bf16)] * carried,
        scratch_shapes=Deliver.scratch(stored[0], seats.per, seats.places) * carried
        + [pltpu.VMEM((length, PAIR), f32)] * 2,
        compiler_params=pltpu.CompilerParams(
            collective_id=5 if carried else None,
            has_side_effects=bool(carried),
            vmem_limit_bytes=40 * 1024 * 1024,
        ),
        cost_estimate=pl.CostEstimate(
            flops=20 * rows * length * H * HD,
            bytes_accessed=16 * rows * H * HD,
            transcendentals=rows * length * H // 2,
        ),
    )(project, project, project, grad_mixed, mixed, log_total, *([stay] if carried else []))


def layer_forward(weights, smalls, layer_in, attend):
    w_qkv, w_proj, w_fc, w_out = weights
    gains, offsets, attn_bias, out_bias, fc_bias = smalls
    hidden = layer_in.astype(f32)
    width = hidden.shape[-1]
    normed = layer_norm(hidden, gains[0], offsets[0]).astype(bf16)
    bias = jnp.concatenate([attn_bias[0], jnp.zeros((width,), f32), attn_bias[1]])
    project = (mm(normed, w_qkv) + bias).astype(bf16)
    mixed, log_total = attend(project)
    after = hidden + mm(mixed, w_proj) + out_bias[0]
    normed_two = layer_norm(after, gains[1], offsets[1]).astype(bf16)
    inner = mm(normed_two, w_fc) + fc_bias
    active = gelu_tanh(inner).astype(bf16)
    result = (after + mm(active, w_out) + out_bias[1]).astype(bf16)
    return result, (layer_in, normed, project, mixed, log_total, after, normed_two, inner, active)


def row_sum(rows):
    return jnp.sum(rows.astype(f32), axis=0)


def layer_back(weights, smalls, kept, grad_out, attend_pull):
    w_qkv, w_proj, w_fc, w_out = weights
    gains, offsets, attn_bias, out_bias, fc_bias = smalls
    layer_in, normed, project, mixed, log_total, after, normed_two, inner, active = kept
    grad_out, grad_w_out = lax.optimization_barrier(
        (grad_out, mm_tn(active, grad_out).astype(bf16))
    )
    grad_bias_two = row_sum(grad_out)
    grad_active = mm_nt(grad_out, w_out)
    _, gelu_pull = jax.vjp(gelu_tanh, inner)
    grad_inner = gelu_pull(grad_active)[0].astype(bf16)
    grad_inner, grad_w_fc = lax.optimization_barrier(
        (grad_inner, mm_tn(normed_two, grad_inner).astype(bf16))
    )
    grad_fc_bias = row_sum(grad_inner)
    grad_normed_two = mm_nt(grad_inner, w_fc)
    _, norm_pull = jax.vjp(layer_norm, after, gains[1], offsets[1])
    grad_after, grad_gain_two, grad_offset_two = norm_pull(grad_normed_two)
    grad_after = grad_after + grad_out.astype(f32)
    grad_branch = grad_after.astype(bf16)
    grad_branch, grad_w_proj = lax.optimization_barrier(
        (grad_branch, mm_tn(mixed, grad_branch).astype(bf16))
    )
    grad_bias_one = row_sum(grad_branch)
    grad_mixed = mm_nt(grad_branch, w_proj).astype(bf16)
    grad_q, grad_k, grad_v = attend_pull(project, grad_mixed, mixed, log_total)
    grad_project = jnp.concatenate([grad_q, grad_k, grad_v], axis=-1)
    grad_project, grad_w_qkv = lax.optimization_barrier(
        (grad_project, mm_tn(normed, grad_project).astype(bf16))
    )
    grad_normed = mm_nt(grad_project, w_qkv)
    _, first_pull = jax.vjp(layer_norm, layer_in.astype(f32), gains[0], offsets[0])
    grad_hidden, grad_gain_one, grad_offset_one = first_pull(grad_normed)
    grad_input = (grad_after + grad_hidden).astype(bf16)
    small = (
        jnp.stack(
            [
                grad_gain_one,
                grad_gain_two,
                grad_offset_one,
                grad_offset_two,
                row_sum(grad_q),
                row_sum(grad_v),
                grad_bias_one,
                grad_bias_two,
            ]
        ),
        grad_fc_bias,
    )
    return grad_input, (grad_w_qkv, grad_w_proj, grad_w_fc, grad_w_out), small


MESH = pl.DeviceIdType.MESH
ANY = pl.BlockSpec(memory_space=pl.ANY)
CHUNK = 768


def greet(partners):
    barrier = pltpu.get_barrier_semaphore()
    for partner in partners:
        pl.semaphore_signal(barrier, inc=1, device_id=partner, device_id_type=MESH)
    pl.semaphore_wait(barrier, len(partners))


def chip_group(diagonal):
    section, index = lax.axis_index("section"), lax.axis_index("fsdp")
    group = [{"section": 1 - section}]
    for bits in (1, 2, 3) if diagonal else (1, 2):
        group += [{"section": half, "fsdp": index ^ bits} for half in (0, 1)]
    return group


def line_group():
    z, places = lax.axis_index("ctx"), lax.axis_size("ctx")
    return [{"ctx": lax.rem(z + step, places)} for step in range(1, places)]


def column_group():
    section = lax.axis_index("section")
    both = [dict(place, section=half) for place in line_group() for half in (0, 1)]
    return [{"section": 1 - section}] + both


def remote(source, target, send, recv, device):
    return pltpu.make_async_remote_copy(
        src_ref=source,
        dst_ref=target,
        send_sem=send,
        recv_sem=recv,
        device_id=device,
        device_id_type=MESH,
    )


class Gather:
    def __init__(self, layer, shards, outs, send, recv, local, *bounce):
        self.layer, self.shards, self.outs = layer, shards, outs
        self.bounce = bounce
        self.send, self.recv, self.local = send, recv, local
        self.section = lax.axis_index("section")
        self.index = lax.axis_index("fsdp")
        self.sibling = {"section": 1 - self.section}

    def across(self, bits, section=None):
        where = {"fsdp": self.index ^ bits}
        if section is not None:
            where["section"] = section
        return where

    def copy(self, m, slot, source, target, device):
        return remote(source, target, self.send.at[m, slot], self.recv.at[m, slot], device)

    def first(self, m, bits, half):
        slot = 0 if bits == 1 else 1
        return remote(
            self.shards[m].at[half],
            self.outs[m].at[self.index, half],
            self.send.at[m, slot + 8 * half],
            self.recv.at[m, slot],
            self.across(bits, half),
        )

    def arrived(self, m, bits):
        slot = 0 if bits == 1 else 1
        place = self.outs[m].at[self.index ^ bits, self.section]
        return self.copy(m, slot, place, place, self.across(bits))

    def own(self, m):
        return self.copy(m, 2, self.shards[m], self.outs[m].at[self.index], self.sibling)

    def take(self, m):
        return pltpu.make_async_copy(self.shards[m], self.bounce[m], self.local.at[0, m])

    def keep(self, m):
        return pltpu.make_async_copy(
            self.bounce[m], self.outs[m].at[self.index], self.local.at[1, m]
        )

    def corner(self, m, bits):
        middle = self.outs[m].shape[2] // 2
        rows = pl.ds(0, middle) if bits == 1 else pl.ds(middle, middle)
        place = self.outs[m].at[self.index ^ bits, self.section, rows]
        return self.copy(m, 3 if bits == 1 else 4, place, place, self.across(3 ^ bits))

    def trade(self, m, bits):
        place = self.outs[m].at[self.index ^ bits, self.section]
        return self.copy(m, 4 + bits, place, place, self.sibling)

    def start(self):
        @pl.when(self.section == self.layer)
        def _():
            for m in range(len(self.shards)):
                for half in (1 - self.layer, self.layer):
                    for bits in (1, 2):
                        self.first(m, bits, half).start()
                self.own(m).start()
                self.take(m).start()
            for m in range(len(self.shards)):
                self.take(m).wait()
                self.keep(m).start()

    def middle(self, m):
        for bits in (1, 2):
            self.arrived(m, bits).wait_recv()
            self.corner(m, bits).start()
            self.trade(m, bits).start()

    def last(self, m):
        for bits in (1, 2):
            self.corner(m, bits).wait_recv()
        self.trade(m, 3).start()

    def finish(self, m):
        for bits in (1, 2, 3):
            copy = self.trade(m, bits)
            copy.wait_send()
            copy.wait_recv()
        for bits in (1, 2):
            self.corner(m, bits).wait_send()

        @pl.when(self.section == self.layer)
        def _():
            for half in (0, 1):
                for bits in (1, 2):
                    self.first(m, bits, half).wait_send()
            self.own(m).wait_send()
            self.keep(m).wait()

        @pl.when(self.section != self.layer)
        def _():
            self.own(m).wait_recv()

class Seats:
    def __init__(self, seqs):
        self.sections, self.places = lax.axis_size("section"), lax.axis_size("ctx")
        self.seqs = seqs
        self.per = -(-seqs // (self.sections * self.places))
        self.size = self.places * self.per
        self.real = [min(max(seqs - i * self.size, 0), self.size) for i in range(self.sections)]
        self.skip = [(self.size - real) // 2 for real in self.real]

    def of(self, section, slot):
        real = jnp.where(section == 0, self.real[0], self.real[1])
        skip = jnp.where(section == 0, self.skip[0], self.skip[1])
        taken = (slot >= skip) & (slot < skip + real)
        return taken, jnp.clip(section * self.size + slot - skip, 0, self.seqs - 1)

    def home(self, seq):
        section, slot = seq // self.size, seq % self.size + self.skip[seq // self.size]
        return section, slot // self.per, slot % self.per


class Bring:
    def __init__(self, rows, outs, send, recv, local, zeros):
        self.rows, self.outs = rows, outs
        self.send, self.recv, self.local, self.zeros = send, recv, local, zeros
        self.seats = Seats(rows[0].shape[0])
        self.section, self.z = lax.axis_index("section"), lax.axis_index("ctx")
        self.depth = rows[0].shape[1]

    @staticmethod
    def scratch(rows, per, places):
        return [
            pltpu.SemaphoreType.DMA((len(rows), places * per)),
            pltpu.SemaphoreType.DMA((len(rows), per, places)),
            pltpu.SemaphoreType.DMA((len(rows), per, places)),
            pltpu.VMEM(rows[0].shape[1:], bf16),
        ]

    def span(self, z):
        return pl.ds(z * self.depth, self.depth)

    def copy(self, a, seq, place, p):
        return remote(
            self.rows[a].at[seq],
            self.outs[a].at[p, self.span(self.z)],
            self.send.at[a, place * self.seats.per + p],
            self.recv.at[a, p, self.z],
            {"ctx": place},
        )

    def arrival(self, a, p, place):
        target = self.outs[a].at[p, self.span(place)]
        return remote(target, target, self.send.at[a, 0], self.recv.at[a, p, place], {"ctx": place})

    def stay(self, a, seq, p):
        return pltpu.make_async_copy(
            self.rows[a].at[seq], self.outs[a].at[p, self.span(self.z)], self.local.at[a, p, 0]
        )

    def blank(self, a, p, place):
        return pltpu.make_async_copy(
            self.zeros, self.outs[a].at[p, self.span(place)], self.local.at[a, p, place]
        )

    def each(self, a, going, staying, coming, empty):
        for p in range(self.seats.per):
            for place in range(self.seats.places):
                taken, seq = self.seats.of(self.section, place * self.seats.per + p)

                @pl.when(taken & (place != self.z))
                def _():
                    going(a, seq, place, p)

            taken, seq = self.seats.of(self.section, self.z * self.seats.per + p)

            @pl.when(taken)
            def _():
                staying(a, seq, p)
                for place in range(self.seats.places):

                    @pl.when(place != self.z)
                    def _():
                        coming(a, p, place)

            @pl.when(jnp.logical_not(taken))
            def _():
                for place in range(self.seats.places):
                    empty(a, p, place)

    def clear(self):
        self.zeros[...] = jnp.zeros(self.zeros.shape, bf16)

    def start(self, a):
        self.each(
            a,
            lambda *at: self.copy(*at).start(),
            lambda *at: self.stay(*at).start(),
            lambda *at: None,
            lambda *at: self.blank(*at).start(),
        )

    def finish(self, a):
        self.each(
            a,
            lambda *at: self.copy(*at).wait_send(),
            lambda *at: self.stay(*at).wait(),
            lambda *at: self.arrival(*at).wait_recv(),
            lambda *at: self.blank(*at).wait(),
        )


class Deliver:
    def __init__(self, layer, rows, out, send, recv, local):
        self.layer, self.rows, self.out = layer, rows, out
        self.send, self.recv, self.local = send, recv, local
        self.seats = Seats(out.shape[0])
        self.section, self.z = lax.axis_index("section"), lax.axis_index("ctx")
        self.depth = out.shape[1]

    @staticmethod
    def scratch(seqs, per, places):
        return [
            pltpu.SemaphoreType.DMA((per, places)),
            pltpu.SemaphoreType.DMA((seqs,)),
            pltpu.SemaphoreType.DMA((per,)),
        ]

    def source(self, p, place):
        return self.rows.at[p, pl.ds(place * self.depth, self.depth)]

    def copy(self, p, place, seq):
        return remote(
            self.source(p, place),
            self.out.at[seq],
            self.send.at[p, place],
            self.recv.at[seq],
            {"section": self.layer, "ctx": place},
        )

    def stay(self, p, place, seq):
        return pltpu.make_async_copy(self.source(p, place), self.out.at[seq], self.local.at[p])

    def each(self, going, staying):
        for p in range(self.seats.per):
            taken, seq = self.seats.of(self.section, self.z * self.seats.per + p)
            for place in range(self.seats.places):
                here = (self.section == self.layer) & (self.z == place)

                @pl.when(taken & here)
                def _():
                    staying(p, place, seq)

                @pl.when(taken & jnp.logical_not(here))
                def _():
                    going(p, place, seq)

    def start(self):
        self.each(
            lambda *at: self.copy(*at).start(),
            lambda *at: self.stay(*at).start(),
        )

    def finish(self):
        self.each(
            lambda *at: self.copy(*at).wait_send(),
            lambda *at: self.stay(*at).wait(),
        )
        for seq in range(self.seats.seqs):
            section, place, p = self.seats.home(seq)

            @pl.when(
                (self.section == self.layer)
                & ((self.section != section) | (self.z != place))
            )
            def _():
                target = self.out.at[seq]
                remote(
                    target, target, self.send.at[0, 0], self.recv.at[seq], {"section": 1 - self.section}
                ).wait_recv()


class Spread:
    def __init__(self, block, out, send, recv, local):
        self.block, self.out, self.send, self.recv, self.local = block, out, send, recv, local
        self.section, self.index = lax.axis_index("section"), lax.axis_index("fsdp")

    @staticmethod
    def scratch():
        return [
            pltpu.SemaphoreType.DMA((8,)),
            pltpu.SemaphoreType.DMA((8,)),
            pltpu.SemaphoreType.DMA,
        ]

    def copies(self):
        for flip in (0, 1):
            for bits in range(4):
                if flip or bits:
                    yield remote(
                        self.block,
                        self.out.at[self.section, self.index],
                        self.send.at[4 * flip + bits],
                        self.recv.at[4 * flip + bits],
                        {"section": self.section ^ flip, "fsdp": self.index ^ bits},
                    )

    def stay(self):
        return pltpu.make_async_copy(
            self.block, self.out.at[self.section, self.index], self.local
        )

    def start(self):
        for copy in self.copies():
            copy.start()
        self.stay().start()

    def finish(self):
        for copy in self.copies():
            copy.wait_send()
            copy.wait_recv()
        self.stay().wait()


def open_kernel(count, *refs):
    shards, rows, pack = refs[:count], refs[count : count + 2], refs[count + 2]
    refs = refs[count + 3 :]
    outs, brought, packs = refs[:count], refs[count : count + 2], refs[count + 2]
    refs = refs[count + 3 :]
    spread = Spread(pack, packs, *refs[:3])
    bring = Bring(rows, brought, *refs[3:7])
    gather = Gather(0, shards, outs, *refs[7:])
    greet(chip_group(True) + line_group())
    bring.clear()
    bring.start(0)
    spread.start()
    gather.start()
    for m in range(count):
        gather.middle(m)
        if m > 0:
            gather.last(m - 1)
        if m == 1:
            bring.start(1)
    gather.last(count - 1)
    spread.finish()
    bring.finish(0)
    bring.finish(1)
    for m in range(count):
        gather.finish(m)


def open_call(shards, rows, pack):
    count = len(shards)
    shards = split_shards(shards)
    seats = Seats(rows[0].shape[0])
    seqs, depth, width = rows[0].shape
    whole = (seats.per, depth * seats.places, width)
    outs = pl.pallas_call(
        functools.partial(open_kernel, count),
        in_specs=[ANY] * (count + 3),
        out_specs=[ANY] * (count + 3),
        out_shape=gather_shapes(shards)
        + [jax.ShapeDtypeStruct(whole, bf16)] * 2
        + [jax.ShapeDtypeStruct((2, 4) + pack.shape, bf16)],
        scratch_shapes=Spread.scratch()
        + Bring.scratch(rows, seats.per, seats.places)
        + gather_scratch(shards),
        compiler_params=pltpu.CompilerParams(
            collective_id=0, has_side_effects=True, vmem_limit_bytes=40 * 1024 * 1024
        ),
    )(*shards, *rows, pack)
    return join_shards(outs[:count]), outs[count], outs[count + 1], outs[count + 2]


def gather_scratch(shards):
    count = len(shards)
    return [
        pltpu.SemaphoreType.DMA((count, 10)),
        pltpu.SemaphoreType.DMA((count, 8)),
        pltpu.SemaphoreType.DMA((2, count)),
    ] + [pltpu.VMEM(shard.shape, shard.dtype) for shard in shards]


def gather_shapes(shards):
    return [jax.ShapeDtypeStruct((4,) + shard.shape, shard.dtype) for shard in shards]


def split_shards(shards):
    return [shard.reshape(2, -1, shard.shape[-1]) for shard in shards]


def join_shards(outs):
    return tuple(out.reshape(-1, out.shape[-1]) for out in outs)


class Reduce:
    def __init__(self, line, items, out, scratch):
        self.line, self.items, self.out = line, items, out
        (
            self.own,
            self.twin,
            self.near_corner,
            self.far_corner,
            self.near,
            self.far,
            self.outer,
            self.inner,
            self.partial,
            self.total,
            self.send,
            self.recv,
            self.local,
        ) = scratch
        self.section = lax.axis_index("section")
        self.index = lax.axis_index("fsdp")
        self.z = lax.axis_index("ctx")
        self.count = self.own.shape[0]
        self.sibling = {"section": 1 - self.section}
        self.x = {"fsdp": self.index ^ 1}
        self.y = {"fsdp": self.index ^ 2}
        self.is_inner = (self.z == 1) | (self.z == 2)
        self.end = {"ctx": jnp.where(self.z == 1, 0, 3)}
        self.toward = {"ctx": jnp.where(self.z == 0, 1, 2)}
        self.opposite = {"ctx": 3 - self.z}

    def chunks(self):
        k = 0
        for item in self.items:
            rows, columns = item.shape[2:]
            depth = self.own.shape[2]
            for row in range(0, rows, depth):
                for column in range(0, columns, CHUNK):
                    yield k, item, pl.ds(row, depth), pl.ds(column, CHUNK)
                    k += 1

    def copy(self, k, slot, source, target, device):
        return remote(source, target, self.send.at[slot, k], self.recv.at[slot, k], device)

    def swap(self, k):
        return self.copy(k, 0, self.twin.at[k], self.twin.at[k], self.sibling)

    def load(self, k):
        return pltpu.make_async_copy(self.own.at[k], self.own.at[k], self.local.at[k])

    def corner(self, k, near):
        half = self.own.shape[2] // 2
        rows = pl.ds(0, half) if near else pl.ds(half, half)
        source = self.own.at[k, self.index ^ 3, rows]
        target = (self.near_corner if near else self.far_corner).at[k]
        return self.copy(k, 1 if near else 2, source, target, self.x if near else self.y)

    def side(self, k, near):
        source = self.own.at[k, self.index ^ (1 if near else 2)]
        target = (self.near if near else self.far).at[k]
        return self.copy(k, 3 if near else 4, source, target, self.x if near else self.y)

    def inward(self, k):
        return self.copy(k, 5, self.partial.at[k], self.outer.at[k], self.toward)

    def across(self, k):
        return self.copy(k, 6, self.partial.at[k], self.inner.at[k], self.opposite)

    def outward(self, k):
        return self.copy(k, 7, self.total.at[k], self.total.at[k], self.end)

    def greet(self):
        greet(column_group() + [self.x, self.y])

    def start(self):
        for k, item, rows, columns in self.chunks():
            theirs = item.at[:, 1 - self.section, rows, columns]
            mine = item.at[:, self.section, rows, columns]
            self.copy(k, 0, theirs, self.twin.at[k], self.sibling).start()
            pltpu.make_async_copy(mine, self.own.at[k], self.local.at[k]).start()

    def stage(self, number, k):
        half = self.own.shape[2] // 2
        near, far = self.index ^ 1, self.index ^ 2
        if number == 0:
            self.load(k).wait()
            self.swap(k).wait_recv()
            for j in range(4):
                self.own[k, j] = self.own[k, j] + self.twin[k, j]
            self.corner(k, True).start()
            self.corner(k, False).start()
        elif number == 1:
            self.corner(k, True).wait_recv()
            self.corner(k, False).wait_recv()
            self.own[k, far, :half] = self.own[k, far, :half] + self.near_corner[k]
            self.own[k, near, half:] = self.own[k, near, half:] + self.far_corner[k]
            self.side(k, True).start()
            self.side(k, False).start()
        elif number == 2:
            self.side(k, True).wait_recv()
            self.side(k, False).wait_recv()
            summed = (
                self.own[k, self.index].astype(f32)
                + self.near[k].astype(f32)
                + self.far[k].astype(f32)
            ).astype(bf16)
            if not self.line:
                self.total[k] = summed
                return
            self.partial[k] = summed

            @pl.when(jnp.logical_not(self.is_inner))
            def _():
                self.inward(k).start()
        elif number == 3 and self.line:

            @pl.when(self.is_inner)
            def _():
                self.inward(k).wait_recv()
                self.partial[k] = self.partial[k] + self.outer[k]
                self.across(k).start()
        elif number == 4 and self.line:

            @pl.when(self.is_inner)
            def _():
                self.across(k).wait_recv()
                self.total[k] = self.partial[k] + self.inner[k]
                self.outward(k).start()

    def step(self, t, lags):
        for number, lag in enumerate(lags):
            k = t - lag

            @pl.when((k >= 0) & (k < self.count))
            def _():
                self.stage(number, k)

    def finish(self, k):
        self.swap(k).wait_send()
        for near in (True, False):
            self.corner(k, near).wait_send()
            self.side(k, near).wait_send()
        if self.line:

            @pl.when(self.is_inner)
            def _():
                self.across(k).wait_send()
                self.outward(k).wait_send()

            @pl.when(jnp.logical_not(self.is_inner))
            def _():
                self.inward(k).wait_send()
                self.outward(k).wait_recv()

    def write(self):
        copy = pltpu.make_async_copy(self.total, self.out, self.local.at[0])
        copy.start()
        copy.wait()


LAGS = (0, 1, 3, 4, 5)


def reduce_kernel(line, layer, count, *refs):
    rows, out, delivered = refs[count : count + 3]
    deliver = Deliver(layer, rows, delivered, *refs[count + 3 : count + 6])
    reduce = Reduce(line, refs[:count], out, refs[count + 6 :])
    reduce.greet()
    reduce.start()
    deliver.start()

    def step(t, _):
        reduce.step(t, LAGS)
        return 0

    lax.fori_loop(0, reduce.count + LAGS[-1], step, 0)

    def finish(k, _):
        reduce.finish(k)
        return 0

    lax.fori_loop(0, reduce.count, finish, 0)
    reduce.write()
    deliver.finish()


def reduce_scratch(count, depth):
    block = (count, depth, CHUNK)
    half = (count, depth // 2, CHUNK)
    return (
        [pltpu.VMEM((count, 4, depth, CHUNK), bf16)] * 2
        + [pltpu.VMEM(half, bf16)] * 2
        + [pltpu.VMEM(block, bf16)] * 6
        + [
            pltpu.SemaphoreType.DMA((8, count)),
            pltpu.SemaphoreType.DMA((8, count)),
            pltpu.SemaphoreType.DMA((count,)),
        ]
    )


def reduce_grads(collective, grads, line, layer, rows, stored):
    items = [grad.reshape(4, 2, -1, grad.shape[-1]) for grad in grads]
    depth = min(item.shape[2] for item in items)
    count = sum((item.shape[2] // depth) * (item.shape[3] // CHUNK) for item in items)
    seats = Seats(stored[0])
    rows = rows.reshape(seats.per, -1, rows.shape[-1])
    out, delivered = pl.pallas_call(
        functools.partial(reduce_kernel, line, layer, len(items)),
        in_specs=[ANY] * (len(items) + 1),
        out_specs=[ANY] * 2,
        out_shape=[
            jax.ShapeDtypeStruct((count, depth, CHUNK), bf16),
            jax.ShapeDtypeStruct(stored, bf16),
        ],
        scratch_shapes=Deliver.scratch(stored[0], seats.per, seats.places)
        + reduce_scratch(count, depth),
        compiler_params=pltpu.CompilerParams(
            collective_id=collective, has_side_effects=True, vmem_limit_bytes=48 * 1024 * 1024
        ),
    )(*items, rows)
    return out if line else lax.psum(out, "ctx"), delivered


def unchunk(blocks, shapes):
    depth = blocks.shape[-2]
    parts, k = [], 0
    for rows, columns in shapes:
        high, wide = rows // depth, columns // CHUNK
        part = blocks[..., k : k + high * wide, :, :]
        if wide > 1:
            part = jnp.concatenate([part[..., j, :, :] for j in range(wide)], axis=-1)
        parts.append(part.reshape(blocks.shape[:-3] + (rows, columns)))
        k += high * wide
    return parts


def attend_gather_kernel(block, layer, count, q_ref, k_ref, v_ref, *refs):
    shards = refs[:count]
    o_ref, log_ref = refs[count : count + 2]
    outs = refs[count + 2 : 2 * count + 2]
    gather = Gather(layer, shards, outs, *refs[2 * count + 2 :])
    head = pl.program_id(1)
    steps = H // 2
    once = pl.program_id(0) == 0

    @pl.when(once & (head == 0))
    def _():
        greet(chip_group(False))
        gather.start()

    for m in range(count):

        @pl.when(once & (head == steps - 2 - count + m))
        def _():
            gather.middle(m)

    @pl.when(once & (head == steps - 1))
    def _():
        for m in range(count):
            gather.last(m)

    attend_kernel(block, q_ref, k_ref, v_ref, o_ref, log_ref)

    @pl.when(once & (head == steps - 1))
    def _():
        for m in range(count):
            gather.finish(m)


def attend_gather(project, length, layer, shards):
    rows = project.shape[0]
    count = rows // length
    pairs = H // 2
    shards = split_shards(shards)
    mixed, log_total, *outs = pl.pallas_call(
        functools.partial(attend_gather_kernel, query_block(length), layer, len(shards)),
        grid=(count, pairs),
        in_specs=[head_spec(length, 0), head_spec(length, pairs), head_spec(length, 2 * pairs)]
        + [ANY] * len(shards),
        out_specs=[head_spec(length, 0), log_spec(length)] + [ANY] * len(shards),
        out_shape=[
            jax.ShapeDtypeStruct((rows, H * HD), bf16),
            jax.ShapeDtypeStruct((count, pairs, 2, length), f32),
        ]
        + gather_shapes(shards),
        scratch_shapes=gather_scratch(shards),
        compiler_params=pltpu.CompilerParams(
            collective_id=1, has_side_effects=True, vmem_limit_bytes=40 * 1024 * 1024
        ),
        cost_estimate=pl.CostEstimate(
            flops=8 * rows * length * H * HD,
            bytes_accessed=8 * rows * H * HD,
            transcendentals=rows * length * H // 2,
        ),
    )(project, project, project, *shards)
    return (mixed, log_total), join_shards(outs)


def carry_deliver(body, ins, outs, layer, *refs):
    rows, delivered = refs[ins], refs[ins + 1 + outs]
    rest = refs[ins + outs + 2 :]
    deliver = Deliver(layer, rows, delivered, *rest[:3])
    step = pl.program_id(0) * pl.num_programs(1) + pl.program_id(1)

    @pl.when(step == 0)
    def _():
        greet(column_group())
        deliver.start()

    body(*refs[:ins], *refs[ins + 1 : ins + 1 + outs], *rest[3:])

    @pl.when(step == pl.num_programs(0) * pl.num_programs(1) - 1)
    def _():
        deliver.finish()


def swap(value):
    return lax.ppermute(value, "section", [(0, 1), (1, 0)])


def shards(
    block_input,
    positions,
    cotangent,
    w_qkv,
    w_proj,
    w_fc,
    w_out,
    ln_gain,
    ln_bias,
    attn_bias,
    out_bias,
    fc_bias,
):
    section = lax.axis_index("section")
    first = section == 0
    ctxs = lax.axis_size("ctx")
    fsdps = lax.axis_size("fsdp")
    local_seqs, local_rows, width = block_input.shape
    stored = block_input.shape
    length = positions.shape[1]
    seats = Seats(local_seqs)
    per = seats.per
    shard_width = ln_gain.shape[2]

    pack = jnp.concatenate(
        [ln_gain[0], ln_bias[0], attn_bias[0], out_bias[0], fc_bias[0].reshape(-1, shard_width)]
    )
    pack = jnp.pad(pack, ((0, 16 - pack.shape[0]), (0, 256 - shard_width)))

    def unpack(packed):
        packed = packed[:, :12, :shard_width]
        vectors = jnp.transpose(packed[:, :8], (1, 0, 2)).reshape(8, -1).astype(f32)
        fc = packed[:, 8:].reshape(-1).astype(f32)
        return vectors[0:2], vectors[2:4], vectors[4:6], vectors[6:8], fc

    shards_own = [matrix[0] for matrix in (w_qkv, w_proj, w_fc, w_out)]
    weights_zero, block_rows, cotangent_rows, packs = open_call(
        shards_own, (block_input, cotangent), pack
    )
    smalls = [unpack(packs[layer]) for layer in range(2)]
    pieces = []
    for matrix in shards_own[2:]:
        rows = matrix.shape[0] // 2
        arrived = swap(jnp.where(first, matrix[rows:], matrix[:rows]))
        pieces.append(jnp.where(first, arrived, matrix[rows:]))
    weights_zero, pieces = lax.optimization_barrier((weights_zero, pieces))
    late = [lax.all_gather(piece, ("fsdp", "section"), axis=0, tiled=True) for piece in pieces]

    places = jnp.stack(
        [
            lax.dynamic_index_in_dim(
                positions, seats.of(section, lax.axis_index("ctx") * per + p)[1], 0, keepdims=False
            )
            for p in range(per)
        ]
    )
    order = (
        lax.broadcasted_iota(jnp.int32, (per, length, length), 1) == places[:, None, :]
    ).astype(bf16)
    order_back = (
        lax.broadcasted_iota(jnp.int32, (per, length, length), 2) == places[:, :, None]
    ).astype(bf16)

    def to_sorted(rows):
        return (
            jnp.einsum("bpt,btd->bpd", order, rows, preferred_element_type=f32)
            .astype(bf16)
            .reshape(per * length, width)
        )

    def to_stored(rows):
        return jnp.einsum(
            "btp,bpd->btd", order_back, rows.reshape(per, length, width), preferred_element_type=f32
        ).astype(bf16)

    start = to_sorted(block_rows)
    grad_final = to_sorted(cotangent_rows)
    early = []

    def attend_zero(project):
        attended, gathered = attend_gather(project, length, 1, shards_own[:2])
        early.extend(gathered)
        return attended

    middle, kept_zero = layer_forward(weights_zero, smalls[0], start, attend_zero)
    weights = [weights_zero, (*early, *late)]
    outs = []

    def attend_one(project):
        *attended, out_zero = attend_forward(project, length, to_stored(middle), stored)
        outs.append(out_zero)
        return attended

    final, kept_one = layer_forward(weights[1], smalls[1], middle, attend_one)

    def pull_one(*kept):
        *grads, out_one = attend_back(*kept, length, to_stored(final), stored)
        outs.append(out_one)
        return grads

    def pull_zero(*kept):
        return attend_back(*kept, length, None, stored)

    line = ctxs == 4
    grad_middle, grads_one, small_one = layer_back(
        weights[1], smalls[1], kept_one, grad_final, pull_one
    )
    reduced_one, in_one = reduce_grads(2, grads_one, line, 1, to_stored(grad_middle), stored)
    grad_start, grads_zero, small_zero = layer_back(
        weights[0], smalls[0], kept_zero, grad_middle, pull_zero
    )

    def repack(small):
        vectors, fc = small
        vectors = jnp.transpose(vectors.reshape(8, fsdps, shard_width), (1, 0, 2))
        packed = jnp.concatenate([vectors, fc.reshape(fsdps, -1, shard_width)], axis=1)
        packed = packed.reshape(fsdps, 1, -1, CHUNK)
        depth = w_qkv.shape[1] // 2
        return jnp.pad(packed, ((0, 0), (0, 0), (0, depth - packed.shape[2]), (0, 0))).astype(bf16)

    pack = jnp.concatenate([repack(small_zero), repack(small_one)], axis=1)
    pack = pack.reshape(-1, CHUNK)
    reduced_zero, in_zero = reduce_grads(
        3, (*grads_zero, pack), line, 0, to_stored(grad_start), stored
    )
    section_out = jnp.where(first, outs[0], outs[1])[None]
    section_in_grad = jnp.where(first, in_zero, in_one)[None]
    packed = reduced_zero[-1].reshape(-1, shard_width)[:12].astype(f32)
    reduced_zero = reduced_zero[:-1]
    arrived = swap(jnp.where(first, reduced_one, reduced_zero))
    mine = jnp.where(first, reduced_zero, reduced_one)
    low = jnp.where(first, mine, arrived)
    high = jnp.where(first, arrived, mine)
    shapes = [(matrix.shape[1] // 2, matrix.shape[2]) for matrix in (w_qkv, w_proj, w_fc, w_out)]
    big = [
        jnp.concatenate([a, b], axis=0).astype(f32)[None]
        for a, b in zip(unchunk(low, shapes), unchunk(high, shapes))
    ]

    return (
        section_out,
        section_in_grad,
        *big,
        packed[None, 0:2],
        packed[None, 2:4],
        packed[None, 4:6],
        packed[None, 6:8],
        packed[8:].reshape(1, -1),
    )


def solution(mesh):
    matrix = P("section", "fsdp", None)
    vectors = P("section", None, "fsdp")
    rows_out = P("section", "fsdp", "ctx", None)
    return jax.shard_map(
        shards,
        mesh=mesh,
        in_specs=(
            P("fsdp", "ctx", None),
            P("fsdp", None),
            P("fsdp", "ctx", None),
            *([matrix] * 4),
            *([vectors] * 4),
            P("section", "fsdp"),
        ),
        out_specs=(
            rows_out,
            rows_out,
            *([matrix] * 4),
            *([vectors] * 4),
            P("section", "fsdp"),
        ),
        check_vma=False,
    )
```

```python
import functools

import jax
import jax.numpy as jnp
from jax import lax
from jax.experimental import pallas as pl
from jax.experimental.pallas import tpu as pltpu
from jax.sharding import PartitionSpec as P

H = 12
HD = 64
PAIR = 2 * HD
SCALE = HD**-0.5

masked_score = -1e30
norm_eps = 1e-05
f32 = jnp.float32
bf16 = jnp.bfloat16


def layer_norm(hidden, gain, offset):
    center = hidden - jnp.mean(hidden, axis=-1, keepdims=True)
    spread = jnp.mean(center * center, axis=-1, keepdims=True)
    return center * lax.rsqrt(spread + norm_eps) * gain + offset


def gelu_tanh(inputs):
    return jax.nn.gelu(inputs, approximate=True)


def mm(left, right):
    return lax.dot_general(left, right, (((1,), (0,)), ((), ())), preferred_element_type=f32)


def mm_nt(left, right):
    return lax.dot_general(left, right, (((1,), (1,)), ((), ())), preferred_element_type=f32)


def mm_tn(left, right):
    return lax.dot_general(left, right, (((0,), (0,)), ((), ())), preferred_element_type=f32)


def masked_scores(keys, queries, start, block):
    scores = mm_nt(keys, queries)
    down = lax.broadcasted_iota(jnp.int32, (block, block), 0)
    across = lax.broadcasted_iota(jnp.int32, (block, block), 1)
    corner = jnp.where(across >= down, scores[start:], masked_score)
    if start == 0:
        return corner
    return jnp.concatenate([scores[:start], corner], axis=0)


def attend_kernel(block, q_ref, k_ref, v_ref, o_ref, log_ref):
    length = q_ref.shape[0]
    for head in range(2):
        cols = slice(head * HD, (head + 1) * HD)
        for start in range(0, length, block):
            end = start + block
            queries = (q_ref[start:end, cols].astype(f32) * SCALE).astype(bf16)
            scores = masked_scores(k_ref[:end, cols], queries, start, block)
            top = jnp.max(scores, axis=0, keepdims=True)
            weights = jnp.exp(scores - top)
            total = jnp.sum(weights, axis=0, keepdims=True)
            mixed = mm_tn(v_ref[:end, cols], weights.astype(bf16)) / total
            o_ref[start:end, cols] = mixed.T.astype(bf16)
            log_ref[0, 0, head : head + 1, start:end] = top + jnp.log(total)


def attend_back_kernel(
    block, q_ref, k_ref, v_ref, do_ref, o_ref, log_ref, dq_ref, dk_ref, dv_ref, dk_sum, dv_sum
):
    length = q_ref.shape[0]
    for head in range(2):
        cols = slice(head * HD, (head + 1) * HD)
        for start in range(length - block, -1, -block):
            end = start + block
            queries = (q_ref[start:end, cols].astype(f32) * SCALE).astype(bf16)
            grads = do_ref[start:end, cols]
            product = grads.astype(f32) * o_ref[start:end, cols].astype(f32)
            delta = jnp.sum(product.T, axis=0, keepdims=True)
            keys = k_ref[:end, cols]
            scores = masked_scores(keys, queries, start, block)
            probs = jnp.exp(scores - log_ref[0, 0, head : head + 1, start:end])
            grad_probs = mm_nt(v_ref[:end, cols], grads)
            grad_scores = (probs * (grad_probs - delta)).astype(bf16)
            dv = mm(probs.astype(bf16), grads)
            dk = mm(grad_scores, queries)
            if end == length:
                dv_sum[:end, cols] = dv
                dk_sum[:end, cols] = dk
            else:
                dv_sum[:end, cols] += dv
                dk_sum[:end, cols] += dk
            dq = mm_tn(keys, grad_scores) * SCALE
            dq_ref[start:end, cols] = dq.T.astype(bf16)
    dk_ref[...] = dk_sum[...].astype(bf16)
    dv_ref[...] = dv_sum[...].astype(bf16)


def query_block(length):
    return 256 if length % 256 == 0 else length


def head_spec(length, offset):
    return pl.BlockSpec((length, PAIR), lambda b, h: (b, offset + h))


def log_spec(length):
    return pl.BlockSpec((1, 1, 2, length), lambda b, h: (b, h, 0, 0))


def attend_forward(project, length, carry):
    rows = project.shape[0]
    count = rows // length
    pairs = H // 2
    grid = (count, pairs)
    body = functools.partial(attend_kernel, query_block(length))
    outs = pl.pallas_call(
        carry.kernel(body, 3, 2, 0, grid),
        grid=grid,
        in_specs=[head_spec(length, 0), head_spec(length, pairs), head_spec(length, 2 * pairs)]
        + [ANY] * len(carry.ins),
        out_specs=[head_spec(length, 0), log_spec(length)] + [ANY] * len(carry.outs),
        out_shape=[
            jax.ShapeDtypeStruct((rows, H * HD), bf16),
            jax.ShapeDtypeStruct((count, pairs, 2, length), f32),
        ]
        + carry.outs,
        scratch_shapes=carry.scratch,
        compiler_params=carry.params(40),
        cost_estimate=pl.CostEstimate(
            flops=8 * rows * length * H * HD,
            bytes_accessed=8 * rows * H * HD,
            transcendentals=rows * length * H // 2,
        ),
    )(project, project, project, *carry.ins)
    return outs[:2], carry.result(outs[2:])


def attend_back(project, grad_mixed, mixed, log_total, length, carry):
    rows = project.shape[0]
    count = rows // length
    pairs = H // 2
    grid = (count, pairs)
    body = functools.partial(attend_back_kernel, query_block(length))
    outs = pl.pallas_call(
        carry.kernel(body, 6, 3, 2, grid),
        grid=grid,
        in_specs=[
            head_spec(length, 0),
            head_spec(length, pairs),
            head_spec(length, 2 * pairs),
            head_spec(length, 0),
            head_spec(length, 0),
            log_spec(length),
        ]
        + [ANY] * len(carry.ins),
        out_specs=[head_spec(length, 0)] * 3 + [ANY] * len(carry.outs),
        out_shape=[jax.ShapeDtypeStruct((rows, H * HD), bf16)] * 3 + carry.outs,
        scratch_shapes=[pltpu.VMEM((length, PAIR), f32)] * 2 + carry.scratch,
        compiler_params=carry.params(48),
        cost_estimate=pl.CostEstimate(
            flops=20 * rows * length * H * HD,
            bytes_accessed=16 * rows * H * HD,
            transcendentals=rows * length * H // 2,
        ),
    )(project, project, project, grad_mixed, mixed, log_total, *carry.ins)
    return outs[:3], carry.result(outs[3:])


TILE = 512
BLOCK = 256
ROOT = 0.7978845608028654
CUBE = 0.044715


def mlp_back_kernel(
    dy_ref,
    normed_ref,
    inner_ref,
    w_fc_ref,
    w_out_ref,
    after_ref,
    mixed_ref,
    w_proj_ref,
    gain_ref,
    dw_out_ref,
    dw_fc_ref,
    dfc_ref,
    dw_proj_ref,
    dmixed_ref,
    dafter_ref,
    sums_ref,
    total,
    active,
    dinner,
    dbranch,
):
    step = pl.program_id(0)
    rows = dy_ref.shape[0]

    @pl.when(step == 0)
    def _():
        total[...] = jnp.zeros(total.shape, f32)

    for start in range(0, rows, BLOCK):
        here = slice(start, start + BLOCK)
        inner = inner_ref[here]
        square = inner * inner
        bend = jnp.tanh(ROOT * (inner + CUBE * (square * inner)))
        half = 0.5 * (1.0 + bend)
        active[here] = (inner * half).astype(bf16)
        slope = half + (0.5 * ROOT) * inner * (1.0 - bend * bend) * (1.0 + (3.0 * CUBE) * square)
        grad = (mm_nt(dy_ref[here], w_out_ref[...]) * slope).astype(bf16)
        dinner[here] = grad
        total[here] += mm_nt(grad, w_fc_ref[...])
    dw_out_ref[...] = mm_tn(active[...], dy_ref[...]).astype(bf16)
    dw_fc_ref[...] = mm_tn(normed_ref[...], dinner[...]).astype(bf16)
    dfc_ref[...] = jnp.sum(dinner[...].astype(f32), axis=0, keepdims=True)

    @pl.when(step == pl.num_programs(0) - 1)
    def _():
        sums_ref[...] = jnp.zeros(sums_ref.shape, f32)
        for start in range(0, rows, BLOCK):
            here = slice(start, start + BLOCK)
            grad = total[here]
            out = dy_ref[here].astype(f32)
            center = after_ref[here]
            center = center - jnp.mean(center, axis=-1, keepdims=True)
            scale = lax.rsqrt(jnp.mean(center * center, axis=-1, keepdims=True) + norm_eps)
            unit = center * scale
            scaled = grad * gain_ref[...]
            shift = jnp.mean(scaled, axis=-1, keepdims=True)
            tilt = jnp.mean(scaled * unit, axis=-1, keepdims=True)
            after = out + (scaled - shift - unit * tilt) * scale
            dafter_ref[here] = after
            branch = after.astype(bf16)
            dbranch[here] = branch
            sums_ref[0:1] += jnp.sum(grad * unit, axis=0, keepdims=True)
            sums_ref[1:2] += jnp.sum(grad, axis=0, keepdims=True)
            sums_ref[2:3] += jnp.sum(branch.astype(f32), axis=0, keepdims=True)
            sums_ref[3:4] += jnp.sum(out, axis=0, keepdims=True)
            dmixed_ref[here] = mm_nt(branch, w_proj_ref[...]).astype(bf16)
        dw_proj_ref[...] = mm_tn(mixed_ref[...], dbranch[...]).astype(bf16)


def mlp_back(weights, gain, kept, grad_out, carry):
    _, w_proj, w_fc, w_out = weights
    _, _, _, mixed, _, after, normed_two, inner = kept
    rows, width = grad_out.shape
    wide = inner.shape[1]
    tile = TILE if wide % TILE == 0 else wide
    grid = (wide // tile,)
    once = pl.Buffered(1)

    def whole(shape):
        return pl.BlockSpec(shape, lambda i: (0, 0), pipeline_mode=once)

    across = pl.BlockSpec((tile, width), lambda i: (i, 0))

    def along(height):
        return pl.BlockSpec((height, tile), lambda i: (0, i))

    outs = pl.pallas_call(
        carry.kernel(mlp_back_kernel, 9, 7, 4, grid) if carry else mlp_back_kernel,
        grid=grid,
        in_specs=[
            whole((rows, width)),
            whole((rows, width)),
            along(rows),
            along(width),
            across,
            whole((rows, width)),
            whole((rows, width)),
            whole((width, width)),
            whole((1, width)),
        ]
        + ([ANY] * len(carry.ins) if carry else []),
        out_specs=[
            across,
            along(width),
            along(1),
            whole((width, width)),
            whole((rows, width)),
            whole((rows, width)),
            whole((8, width)),
        ]
        + ([ANY] * len(carry.outs) if carry else []),
        out_shape=[
            jax.ShapeDtypeStruct((wide, width), bf16),
            jax.ShapeDtypeStruct((width, wide), bf16),
            jax.ShapeDtypeStruct((1, wide), f32),
            jax.ShapeDtypeStruct((width, width), bf16),
            jax.ShapeDtypeStruct((rows, width), bf16),
            jax.ShapeDtypeStruct((rows, width), f32),
            jax.ShapeDtypeStruct((8, width), f32),
        ]
        + (carry.outs if carry else []),
        scratch_shapes=[
            pltpu.VMEM((rows, width), f32),
            pltpu.VMEM((rows, tile), bf16),
            pltpu.VMEM((rows, tile), bf16),
            pltpu.VMEM((rows, width), bf16),
        ]
        + (carry.scratch if carry else []),
        compiler_params=carry.params(60)
        if carry
        else pltpu.CompilerParams(vmem_limit_bytes=60 * 1024 * 1024),
        cost_estimate=pl.CostEstimate(
            flops=8 * rows * width * wide + 4 * rows * width * width,
            bytes_accessed=4 * rows * wide + 8 * wide * width + 16 * rows * width,
            transcendentals=rows * wide,
        ),
    )(
        grad_out,
        normed_two,
        inner,
        w_fc,
        w_out,
        after,
        mixed,
        w_proj,
        gain[None],
        *(carry.ins if carry else []),
    )
    return outs[:7], carry.result(outs[7:]) if carry else []


def layer_forward(weights, smalls, layer_in, attend):
    w_qkv, w_proj, w_fc, w_out = weights
    gains, offsets, attn_bias, out_bias, fc_bias = smalls
    hidden = layer_in.astype(f32)
    width = hidden.shape[-1]
    normed = layer_norm(hidden, gains[0], offsets[0]).astype(bf16)
    bias = jnp.concatenate([attn_bias[0], jnp.zeros((width,), f32), attn_bias[1]])
    project = (mm(normed, w_qkv) + bias).astype(bf16)
    mixed, log_total = attend(project)
    after = hidden + mm(mixed, w_proj) + out_bias[0]
    normed_two = layer_norm(after, gains[1], offsets[1]).astype(bf16)
    inner = mm(normed_two, w_fc) + fc_bias
    active = gelu_tanh(inner).astype(bf16)
    result = (after + mm(active, w_out) + out_bias[1]).astype(bf16)
    return result, (layer_in, normed, project, mixed, log_total, after, normed_two, inner)


def row_sum(rows):
    return jnp.sum(rows.astype(f32), axis=0)


def layer_back(weights, smalls, kept, grad_out, carry, attend_pull):
    w_qkv, w_proj, w_fc, w_out = weights
    gains, offsets, attn_bias, out_bias, fc_bias = smalls
    layer_in, normed, project, mixed, log_total, after, normed_two, inner = kept
    grads, carried = mlp_back(weights, gains[1], kept, grad_out, carry)
    grad_w_out, grad_w_fc, grad_fc_bias, grad_w_proj, grad_mixed, grad_after, sums = grads
    grad_q, grad_k, grad_v = attend_pull(
        (project, grad_mixed, mixed, log_total), (grad_w_fc, grad_w_out)
    )
    grad_project = jnp.concatenate([grad_q, grad_k, grad_v], axis=-1)
    grad_w_qkv = mm_tn(normed, grad_project).astype(bf16)
    grad_normed = mm_nt(grad_project, w_qkv)
    _, first_pull = jax.vjp(layer_norm, layer_in.astype(f32), gains[0], offsets[0])
    grad_hidden, grad_gain_one, grad_offset_one = first_pull(grad_normed)
    grad_input = (grad_after + grad_hidden).astype(bf16)
    small = (
        jnp.stack(
            [
                grad_gain_one,
                sums[0],
                grad_offset_one,
                sums[1],
                row_sum(grad_q),
                row_sum(grad_v),
                sums[2],
                sums[3],
            ]
        ),
        grad_fc_bias[0],
    )
    return grad_input, (grad_w_qkv, grad_w_proj), small, carried


MESH = pl.DeviceIdType.MESH
ANY = pl.BlockSpec(memory_space=pl.ANY)
CHUNK = 768


def greet(partners):
    barrier = pltpu.get_barrier_semaphore()
    for partner in partners:
        pl.semaphore_signal(barrier, inc=1, device_id=partner, device_id_type=MESH)
    pl.semaphore_wait(barrier, len(partners))


def chip_group(diagonal):
    section, index = lax.axis_index("section"), lax.axis_index("fsdp")
    group = [{"section": 1 - section}]
    for bits in (1, 2, 3) if diagonal else (1, 2):
        group += [{"section": half, "fsdp": index ^ bits} for half in (0, 1)]
    return group


def line_group():
    z, places = lax.axis_index("ctx"), lax.axis_size("ctx")
    return [{"ctx": lax.rem(z + step, places)} for step in range(1, places)]


def column_group():
    section = lax.axis_index("section")
    both = [dict(place, section=half) for place in line_group() for half in (0, 1)]
    return [{"section": 1 - section}] + both


def remote(source, target, send, recv, device):
    return pltpu.make_async_remote_copy(
        src_ref=source,
        dst_ref=target,
        send_sem=send,
        recv_sem=recv,
        device_id=device,
        device_id_type=MESH,
    )


class Gather:
    def __init__(self, layer, shards, outs, send, recv, local, *bounce):
        self.layer, self.shards, self.outs = layer, shards, outs
        self.bounce = bounce
        self.send, self.recv, self.local = send, recv, local
        self.section = lax.axis_index("section")
        self.index = lax.axis_index("fsdp")
        self.sibling = {"section": 1 - self.section}

    def across(self, bits, section=None):
        where = {"fsdp": self.index ^ bits}
        if section is not None:
            where["section"] = section
        return where

    def copy(self, m, slot, source, target, device):
        return remote(source, target, self.send.at[m, slot], self.recv.at[m, slot], device)

    def first(self, m, bits, half):
        slot = 0 if bits == 1 else 1
        return remote(
            self.shards[m].at[half],
            self.outs[m].at[self.index, half],
            self.send.at[m, slot + 8 * half],
            self.recv.at[m, slot],
            self.across(bits, half),
        )

    def arrived(self, m, bits):
        slot = 0 if bits == 1 else 1
        place = self.outs[m].at[self.index ^ bits, self.section]
        return self.copy(m, slot, place, place, self.across(bits))

    def own(self, m):
        return self.copy(m, 2, self.shards[m], self.outs[m].at[self.index], self.sibling)

    def take(self, m):
        return pltpu.make_async_copy(self.shards[m], self.bounce[m], self.local.at[0, m])

    def keep(self, m):
        return pltpu.make_async_copy(
            self.bounce[m], self.outs[m].at[self.index], self.local.at[1, m]
        )

    def corner(self, m, bits):
        middle = self.outs[m].shape[2] // 2
        rows = pl.ds(0, middle) if bits == 1 else pl.ds(middle, middle)
        place = self.outs[m].at[self.index ^ bits, self.section, rows]
        return self.copy(m, 3 if bits == 1 else 4, place, place, self.across(3 ^ bits))

    def trade(self, m, bits):
        place = self.outs[m].at[self.index ^ bits, self.section]
        return self.copy(m, 4 + bits, place, place, self.sibling)

    def start(self):
        @pl.when(self.section == self.layer)
        def _():
            for m in range(len(self.shards)):
                for half in (1 - self.layer, self.layer):
                    for bits in (1, 2):
                        self.first(m, bits, half).start()
                self.own(m).start()
                self.take(m).start()
            for m in range(len(self.shards)):
                self.take(m).wait()
                self.keep(m).start()

    def middle(self, m):
        for bits in (1, 2):
            self.arrived(m, bits).wait_recv()
            self.corner(m, bits).start()
            self.trade(m, bits).start()

    def last(self, m):
        for bits in (1, 2):
            self.corner(m, bits).wait_recv()
        self.trade(m, 3).start()

    def finish(self, m):
        for bits in (1, 2, 3):
            copy = self.trade(m, bits)
            copy.wait_send()
            copy.wait_recv()
        for bits in (1, 2):
            self.corner(m, bits).wait_send()

        @pl.when(self.section == self.layer)
        def _():
            for half in (0, 1):
                for bits in (1, 2):
                    self.first(m, bits, half).wait_send()
            self.own(m).wait_send()
            self.keep(m).wait()

        @pl.when(self.section != self.layer)
        def _():
            self.own(m).wait_recv()

class Seats:
    def __init__(self, seqs):
        self.sections, self.places = lax.axis_size("section"), lax.axis_size("ctx")
        self.seqs = seqs
        self.per = -(-seqs // (self.sections * self.places))
        self.size = self.places * self.per
        self.real = [min(max(seqs - i * self.size, 0), self.size) for i in range(self.sections)]
        self.skip = [(self.size - real) // 2 for real in self.real]

    def of(self, section, slot):
        real = jnp.where(section == 0, self.real[0], self.real[1])
        skip = jnp.where(section == 0, self.skip[0], self.skip[1])
        taken = (slot >= skip) & (slot < skip + real)
        return taken, jnp.clip(section * self.size + slot - skip, 0, self.seqs - 1)

    def home(self, seq):
        section, slot = seq // self.size, seq % self.size + self.skip[seq // self.size]
        return section, slot // self.per, slot % self.per


class Bring:
    def __init__(self, rows, outs, send, recv, local, zeros):
        self.rows, self.outs = rows, outs
        self.send, self.recv, self.local, self.zeros = send, recv, local, zeros
        self.seats = Seats(rows[0].shape[0])
        self.section, self.z = lax.axis_index("section"), lax.axis_index("ctx")
        self.depth = rows[0].shape[1]

    @staticmethod
    def scratch(rows, per, places):
        return [
            pltpu.SemaphoreType.DMA((len(rows), places * per)),
            pltpu.SemaphoreType.DMA((len(rows), per, places)),
            pltpu.SemaphoreType.DMA((len(rows), per, places)),
            pltpu.VMEM(rows[0].shape[1:], bf16),
        ]

    def span(self, z):
        return pl.ds(z * self.depth, self.depth)

    def copy(self, a, seq, place, p):
        return remote(
            self.rows[a].at[seq],
            self.outs[a].at[p, self.span(self.z)],
            self.send.at[a, place * self.seats.per + p],
            self.recv.at[a, p, self.z],
            {"ctx": place},
        )

    def arrival(self, a, p, place):
        target = self.outs[a].at[p, self.span(place)]
        return remote(target, target, self.send.at[a, 0], self.recv.at[a, p, place], {"ctx": place})

    def stay(self, a, seq, p):
        return pltpu.make_async_copy(
            self.rows[a].at[seq], self.outs[a].at[p, self.span(self.z)], self.local.at[a, p, 0]
        )

    def blank(self, a, p, place):
        return pltpu.make_async_copy(
            self.zeros, self.outs[a].at[p, self.span(place)], self.local.at[a, p, place]
        )

    def each(self, a, going, staying, coming, empty):
        for p in range(self.seats.per):
            for place in range(self.seats.places):
                taken, seq = self.seats.of(self.section, place * self.seats.per + p)

                @pl.when(taken & (place != self.z))
                def _():
                    going(a, seq, place, p)

            taken, seq = self.seats.of(self.section, self.z * self.seats.per + p)

            @pl.when(taken)
            def _():
                staying(a, seq, p)
                for place in range(self.seats.places):

                    @pl.when(place != self.z)
                    def _():
                        coming(a, p, place)

            @pl.when(jnp.logical_not(taken))
            def _():
                for place in range(self.seats.places):
                    empty(a, p, place)

    def clear(self):
        self.zeros[...] = jnp.zeros(self.zeros.shape, bf16)

    def start(self, a):
        self.each(
            a,
            lambda *at: self.copy(*at).start(),
            lambda *at: self.stay(*at).start(),
            lambda *at: None,
            lambda *at: self.blank(*at).start(),
        )

    def finish(self, a):
        self.each(
            a,
            lambda *at: self.copy(*at).wait_send(),
            lambda *at: self.stay(*at).wait(),
            lambda *at: self.arrival(*at).wait_recv(),
            lambda *at: self.blank(*at).wait(),
        )


class Deliver:
    def __init__(self, layer, rows, out, send, recv, local):
        self.layer, self.rows, self.out = layer, rows, out
        self.send, self.recv, self.local = send, recv, local
        self.seats = Seats(out.shape[0])
        self.section, self.z = lax.axis_index("section"), lax.axis_index("ctx")
        self.depth = out.shape[1]

    @staticmethod
    def scratch(seqs, per, places):
        return [
            pltpu.SemaphoreType.DMA((per, places)),
            pltpu.SemaphoreType.DMA((seqs,)),
            pltpu.SemaphoreType.DMA((per,)),
        ]

    def source(self, p, place):
        return self.rows.at[p, pl.ds(place * self.depth, self.depth)]

    def copy(self, p, place, seq):
        return remote(
            self.source(p, place),
            self.out.at[seq],
            self.send.at[p, place],
            self.recv.at[seq],
            {"section": self.layer, "ctx": place},
        )

    def stay(self, p, place, seq):
        return pltpu.make_async_copy(self.source(p, place), self.out.at[seq], self.local.at[p])

    def each(self, going, staying):
        for p in range(self.seats.per):
            taken, seq = self.seats.of(self.section, self.z * self.seats.per + p)
            for place in range(self.seats.places):
                here = (self.section == self.layer) & (self.z == place)

                @pl.when(taken & here)
                def _():
                    staying(p, place, seq)

                @pl.when(taken & jnp.logical_not(here))
                def _():
                    going(p, place, seq)

    def start(self):
        self.each(
            lambda *at: self.copy(*at).start(),
            lambda *at: self.stay(*at).start(),
        )

    def finish(self):
        self.each(
            lambda *at: self.copy(*at).wait_send(),
            lambda *at: self.stay(*at).wait(),
        )
        for seq in range(self.seats.seqs):
            section, place, p = self.seats.home(seq)

            @pl.when(
                (self.section == self.layer)
                & ((self.section != section) | (self.z != place))
            )
            def _():
                target = self.out.at[seq]
                remote(
                    target, target, self.send.at[0, 0], self.recv.at[seq], {"section": 1 - self.section}
                ).wait_recv()


class Spread:
    def __init__(self, block, out, send, recv, local):
        self.block, self.out, self.send, self.recv, self.local = block, out, send, recv, local
        self.section, self.index = lax.axis_index("section"), lax.axis_index("fsdp")

    @staticmethod
    def scratch():
        return [
            pltpu.SemaphoreType.DMA((8,)),
            pltpu.SemaphoreType.DMA((8,)),
            pltpu.SemaphoreType.DMA,
        ]

    def copies(self):
        for flip in (0, 1):
            for bits in range(4):
                if flip or bits:
                    yield remote(
                        self.block,
                        self.out.at[self.section, self.index],
                        self.send.at[4 * flip + bits],
                        self.recv.at[4 * flip + bits],
                        {"section": self.section ^ flip, "fsdp": self.index ^ bits},
                    )

    def stay(self):
        return pltpu.make_async_copy(
            self.block, self.out.at[self.section, self.index], self.local
        )

    def start(self):
        for copy in self.copies():
            copy.start()
        self.stay().start()

    def finish(self):
        for copy in self.copies():
            copy.wait_send()
            copy.wait_recv()
        self.stay().wait()


def open_kernel(count, *refs):
    shards, rows, pack = refs[:count], refs[count : count + 2], refs[count + 2]
    refs = refs[count + 3 :]
    outs, brought, packs = refs[:count], refs[count : count + 2], refs[count + 2]
    refs = refs[count + 3 :]
    spread = Spread(pack, packs, *refs[:3])
    bring = Bring(rows, brought, *refs[3:7])
    gather = Gather(0, shards, outs, *refs[7:])
    greet(chip_group(True) + line_group())
    bring.clear()
    bring.start(0)
    spread.start()
    gather.start()
    for m in range(count):
        gather.middle(m)
        if m > 0:
            gather.last(m - 1)
        if m == 1:
            bring.start(1)
    gather.last(count - 1)
    spread.finish()
    bring.finish(0)
    bring.finish(1)
    for m in range(count):
        gather.finish(m)


def open_call(shards, rows, pack):
    count = len(shards)
    shards = split_shards(shards)
    seats = Seats(rows[0].shape[0])
    seqs, depth, width = rows[0].shape
    whole = (seats.per, depth * seats.places, width)
    outs = pl.pallas_call(
        functools.partial(open_kernel, count),
        in_specs=[ANY] * (count + 3),
        out_specs=[ANY] * (count + 3),
        out_shape=gather_shapes(shards)
        + [jax.ShapeDtypeStruct(whole, bf16)] * 2
        + [jax.ShapeDtypeStruct((2, 4) + pack.shape, bf16)],
        scratch_shapes=Spread.scratch()
        + Bring.scratch(rows, seats.per, seats.places)
        + gather_scratch(shards),
        compiler_params=pltpu.CompilerParams(
            collective_id=0, has_side_effects=True, vmem_limit_bytes=40 * 1024 * 1024
        ),
    )(*shards, *rows, pack)
    return join_shards(outs[:count]), outs[count], outs[count + 1], outs[count + 2]


def gather_scratch(shards):
    count = len(shards)
    return [
        pltpu.SemaphoreType.DMA((count, 10)),
        pltpu.SemaphoreType.DMA((count, 8)),
        pltpu.SemaphoreType.DMA((2, count)),
    ] + [pltpu.VMEM(shard.shape, shard.dtype) for shard in shards]


def gather_shapes(shards):
    return [jax.ShapeDtypeStruct((4,) + shard.shape, shard.dtype) for shard in shards]


def split_shards(shards):
    return [shard.reshape(2, -1, shard.shape[-1]) for shard in shards]


def join_shards(outs):
    return tuple(out.reshape(-1, out.shape[-1]) for out in outs)


class Reduce:
    def __init__(self, line, items, out, scratch):
        self.line, self.items, self.out = line, items, out
        (
            self.own,
            self.twin,
            self.near_corner,
            self.far_corner,
            self.near,
            self.far,
            self.outer,
            self.inner,
            self.partial,
            self.total,
            self.send,
            self.recv,
            self.local,
        ) = scratch
        self.section = lax.axis_index("section")
        self.index = lax.axis_index("fsdp")
        self.z = lax.axis_index("ctx")
        self.count = self.own.shape[0]
        self.sibling = {"section": 1 - self.section}
        self.x = {"fsdp": self.index ^ 1}
        self.y = {"fsdp": self.index ^ 2}
        self.is_inner = (self.z == 1) | (self.z == 2)
        self.end = {"ctx": jnp.where(self.z == 1, 0, 3)}
        self.toward = {"ctx": jnp.where(self.z == 0, 1, 2)}
        self.opposite = {"ctx": 3 - self.z}

    def chunks(self):
        k = 0
        for item in self.items:
            rows, columns = item.shape[2:]
            depth = self.own.shape[2]
            for row in range(0, rows, depth):
                for column in range(0, columns, CHUNK):
                    yield k, item, pl.ds(row, depth), pl.ds(column, CHUNK)
                    k += 1

    def copy(self, k, slot, source, target, device):
        return remote(source, target, self.send.at[slot, k], self.recv.at[slot, k], device)

    def swap(self, k):
        return self.copy(k, 0, self.twin.at[k], self.twin.at[k], self.sibling)

    def load(self, k):
        return pltpu.make_async_copy(self.own.at[k], self.own.at[k], self.local.at[k])

    def corner(self, k, near):
        half = self.own.shape[2] // 2
        rows = pl.ds(0, half) if near else pl.ds(half, half)
        source = self.own.at[k, self.index ^ 3, rows]
        target = (self.near_corner if near else self.far_corner).at[k]
        return self.copy(k, 1 if near else 2, source, target, self.x if near else self.y)

    def side(self, k, near):
        source = self.own.at[k, self.index ^ (1 if near else 2)]
        target = (self.near if near else self.far).at[k]
        return self.copy(k, 3 if near else 4, source, target, self.x if near else self.y)

    def inward(self, k):
        return self.copy(k, 5, self.partial.at[k], self.outer.at[k], self.toward)

    def across(self, k):
        return self.copy(k, 6, self.partial.at[k], self.inner.at[k], self.opposite)

    def outward(self, k):
        return self.copy(k, 7, self.total.at[k], self.total.at[k], self.end)

    def greet(self):
        greet(column_group() + [self.x, self.y])

    def start(self):
        for k, item, rows, columns in self.chunks():
            theirs = item.at[:, 1 - self.section, rows, columns]
            mine = item.at[:, self.section, rows, columns]
            self.copy(k, 0, theirs, self.twin.at[k], self.sibling).start()
            pltpu.make_async_copy(mine, self.own.at[k], self.local.at[k]).start()

    def stage(self, number, k):
        half = self.own.shape[2] // 2
        near, far = self.index ^ 1, self.index ^ 2
        if number == 0:
            self.load(k).wait()
            self.swap(k).wait_recv()
            for j in range(4):
                self.own[k, j] = self.own[k, j] + self.twin[k, j]
            self.corner(k, True).start()
            self.corner(k, False).start()
        elif number == 1:
            self.corner(k, True).wait_recv()
            self.corner(k, False).wait_recv()
            self.own[k, far, :half] = self.own[k, far, :half] + self.near_corner[k]
            self.own[k, near, half:] = self.own[k, near, half:] + self.far_corner[k]
            self.side(k, True).start()
            self.side(k, False).start()
        elif number == 2:
            self.side(k, True).wait_recv()
            self.side(k, False).wait_recv()
            summed = (
                self.own[k, self.index].astype(f32)
                + self.near[k].astype(f32)
                + self.far[k].astype(f32)
            ).astype(bf16)
            if not self.line:
                self.total[k] = summed
                return
            self.partial[k] = summed

            @pl.when(jnp.logical_not(self.is_inner))
            def _():
                self.inward(k).start()
        elif number == 3 and self.line:

            @pl.when(self.is_inner)
            def _():
                self.inward(k).wait_recv()
                self.partial[k] = self.partial[k] + self.outer[k]
                self.across(k).start()
        elif number == 4 and self.line:

            @pl.when(self.is_inner)
            def _():
                self.across(k).wait_recv()
                self.total[k] = self.partial[k] + self.inner[k]
                self.outward(k).start()

    def step(self, t, lags):
        for number, lag in enumerate(lags):
            k = t - lag

            @pl.when((k >= 0) & (k < self.count))
            def _():
                self.stage(number, k)

    def finish(self, k):
        self.swap(k).wait_send()
        for near in (True, False):
            self.corner(k, near).wait_send()
            self.side(k, near).wait_send()
        if self.line:

            @pl.when(self.is_inner)
            def _():
                self.across(k).wait_send()
                self.outward(k).wait_send()

            @pl.when(jnp.logical_not(self.is_inner))
            def _():
                self.inward(k).wait_send()
                self.outward(k).wait_recv()

    def write(self):
        copy = pltpu.make_async_copy(self.total, self.out, self.local.at[0])
        copy.start()
        copy.wait()


LAGS = (0, 1, 3, 4, 5)
CARRIED_LAGS = (0, 2, 4, 6, 8)


class Carry:
    def __init__(self, collective, grads=(), line=True, layer=None, rows=None, stored=None):
        self.collective, self.line, self.layer = collective, line, layer
        self.ins = [grad.reshape(4, 2, -1, grad.shape[-1]) for grad in grads]
        self.count = len(self.ins)
        self.outs, self.scratch, self.chunks = [], [], 0
        if self.count:
            depth = min(item.shape[2] for item in self.ins)
            self.chunks = sum(
                (item.shape[2] // depth) * (item.shape[3] // CHUNK) for item in self.ins
            )
            self.outs.append(jax.ShapeDtypeStruct((self.chunks, depth, CHUNK), bf16))
            self.scratch += reduce_scratch(self.chunks, depth)
        self.reducing = len(self.scratch)
        if rows is not None:
            seats = Seats(stored[0])
            self.ins.append(rows.reshape(seats.per, -1, rows.shape[-1]))
            self.outs.append(jax.ShapeDtypeStruct(stored, bf16))
            self.scratch += Deliver.scratch(stored[0], seats.per, seats.places)

    def params(self, limit):
        return pltpu.CompilerParams(
            collective_id=self.collective,
            has_side_effects=True,
            vmem_limit_bytes=limit * 1024 * 1024,
        )

    def bind(self, ins, outs, scratch):
        reduce = deliver = None
        if self.count:
            reduce = Reduce(self.line, ins[: self.count], outs[0], scratch[: self.reducing])
        if self.layer is not None:
            deliver = Deliver(self.layer, ins[-1], outs[-1], *scratch[self.reducing :])
        return reduce, deliver

    def begin(self, reduce, deliver):
        if reduce is None:
            greet(column_group())
        else:
            reduce.greet()
            reduce.start()
        if deliver is not None:
            deliver.start()

    def ticks(self, reduce, first, count, lags):
        if reduce is not None:

            def step(t, _):
                reduce.step(first + t, lags)
                return 0

            lax.fori_loop(0, count, step, 0)

    def end(self, reduce, deliver):
        if reduce is not None:

            def finish(k, _):
                reduce.finish(k)
                return 0

            lax.fori_loop(0, reduce.count, finish, 0)
            reduce.write()
        if deliver is not None:
            deliver.finish()

    def kernel(self, body, ins, outs, scratch, grid):
        steps = 1
        for size in grid:
            steps *= size
        lags = CARRIED_LAGS
        share = -(-(self.chunks + lags[-1]) // steps)

        def run(*refs):
            parts, at = [], 0
            for size in (ins, len(self.ins), outs, len(self.outs), scratch, len(self.scratch)):
                parts.append(refs[at : at + size])
                at += size
            reduce, deliver = self.bind(parts[1], parts[3], parts[5])
            step = pl.program_id(0)
            for axis in range(1, len(grid)):
                step = step * grid[axis] + pl.program_id(axis)

            @pl.when(step == 0)
            def _():
                self.begin(reduce, deliver)

            body(*parts[0], *parts[2], *parts[4])
            self.ticks(reduce, step * share, share, lags)

            @pl.when(step == steps - 1)
            def _():
                self.end(reduce, deliver)

        return run

    def alone(self):
        def run(*refs):
            ins = refs[: len(self.ins)]
            outs = refs[len(self.ins) : len(self.ins) + len(self.outs)]
            reduce, deliver = self.bind(ins, outs, refs[len(self.ins) + len(self.outs) :])
            self.begin(reduce, deliver)
            self.ticks(reduce, 0, self.chunks + LAGS[-1], LAGS)
            self.end(reduce, deliver)

        outs = pl.pallas_call(
            run,
            in_specs=[ANY] * len(self.ins),
            out_specs=[ANY] * len(self.outs),
            out_shape=self.outs,
            scratch_shapes=self.scratch,
            compiler_params=self.params(48),
        )(*self.ins)
        return self.result(outs)

    def result(self, outs):
        outs = list(outs)
        if self.count and not self.line:
            outs[0] = lax.psum(outs[0], "ctx")
        return outs


def reduce_scratch(count, depth):
    block = (count, depth, CHUNK)
    half = (count, depth // 2, CHUNK)
    return (
        [pltpu.VMEM((count, 4, depth, CHUNK), bf16)] * 2
        + [pltpu.VMEM(half, bf16)] * 2
        + [pltpu.VMEM(block, bf16)] * 6
        + [
            pltpu.SemaphoreType.DMA((8, count)),
            pltpu.SemaphoreType.DMA((8, count)),
            pltpu.SemaphoreType.DMA((count,)),
        ]
    )


def unchunk(blocks, shapes):
    depth = blocks.shape[-2]
    parts, k = [], 0
    for rows, columns in shapes:
        high, wide = rows // depth, columns // CHUNK
        part = blocks[..., k : k + high * wide, :, :]
        if wide > 1:
            part = jnp.concatenate([part[..., j, :, :] for j in range(wide)], axis=-1)
        parts.append(part.reshape(blocks.shape[:-3] + (rows, columns)))
        k += high * wide
    return parts


def attend_gather_kernel(block, layer, count, q_ref, k_ref, v_ref, *refs):
    shards = refs[:count]
    o_ref, log_ref = refs[count : count + 2]
    outs = refs[count + 2 : 2 * count + 2]
    gather = Gather(layer, shards, outs, *refs[2 * count + 2 :])
    head = pl.program_id(1)
    steps = H // 2
    once = pl.program_id(0) == 0

    @pl.when(once & (head == 0))
    def _():
        greet(chip_group(False))
        gather.start()

    for m in range(count):

        @pl.when(once & (head == steps - 2 - count + m))
        def _():
            gather.middle(m)

    @pl.when(once & (head == steps - 1))
    def _():
        for m in range(count):
            gather.last(m)

    attend_kernel(block, q_ref, k_ref, v_ref, o_ref, log_ref)

    @pl.when(once & (head == steps - 1))
    def _():
        for m in range(count):
            gather.finish(m)


def attend_gather(project, length, layer, shards):
    rows = project.shape[0]
    count = rows // length
    pairs = H // 2
    shards = split_shards(shards)
    mixed, log_total, *outs = pl.pallas_call(
        functools.partial(attend_gather_kernel, query_block(length), layer, len(shards)),
        grid=(count, pairs),
        in_specs=[head_spec(length, 0), head_spec(length, pairs), head_spec(length, 2 * pairs)]
        + [ANY] * len(shards),
        out_specs=[head_spec(length, 0), log_spec(length)] + [ANY] * len(shards),
        out_shape=[
            jax.ShapeDtypeStruct((rows, H * HD), bf16),
            jax.ShapeDtypeStruct((count, pairs, 2, length), f32),
        ]
        + gather_shapes(shards),
        scratch_shapes=gather_scratch(shards),
        compiler_params=pltpu.CompilerParams(
            collective_id=1, has_side_effects=True, vmem_limit_bytes=40 * 1024 * 1024
        ),
        cost_estimate=pl.CostEstimate(
            flops=8 * rows * length * H * HD,
            bytes_accessed=8 * rows * H * HD,
            transcendentals=rows * length * H // 2,
        ),
    )(project, project, project, *shards)
    return (mixed, log_total), join_shards(outs)


def swap(value):
    return lax.ppermute(value, "section", [(0, 1), (1, 0)])


def shards(
    block_input,
    positions,
    cotangent,
    w_qkv,
    w_proj,
    w_fc,
    w_out,
    ln_gain,
    ln_bias,
    attn_bias,
    out_bias,
    fc_bias,
):
    section = lax.axis_index("section")
    first = section == 0
    ctxs = lax.axis_size("ctx")
    fsdps = lax.axis_size("fsdp")
    local_seqs, local_rows, width = block_input.shape
    stored = block_input.shape
    length = positions.shape[1]
    seats = Seats(local_seqs)
    per = seats.per
    shard_width = ln_gain.shape[2]

    pack = jnp.concatenate(
        [ln_gain[0], ln_bias[0], attn_bias[0], out_bias[0], fc_bias[0].reshape(-1, shard_width)]
    )
    pack = jnp.pad(pack, ((0, 16 - pack.shape[0]), (0, 256 - shard_width)))

    def unpack(packed):
        packed = packed[:, :12, :shard_width]
        vectors = jnp.transpose(packed[:, :8], (1, 0, 2)).reshape(8, -1).astype(f32)
        fc = packed[:, 8:].reshape(-1).astype(f32)
        return vectors[0:2], vectors[2:4], vectors[4:6], vectors[6:8], fc

    shards_own = [matrix[0] for matrix in (w_qkv, w_proj, w_fc, w_out)]
    weights_zero, block_rows, cotangent_rows, packs = open_call(
        shards_own, (block_input, cotangent), pack
    )
    smalls = [unpack(packs[layer]) for layer in range(2)]
    pieces = []
    for matrix in shards_own[2:]:
        rows = matrix.shape[0] // 2
        arrived = swap(jnp.where(first, matrix[rows:], matrix[:rows]))
        pieces.append(jnp.where(first, arrived, matrix[rows:]))
    weights_zero, pieces = lax.optimization_barrier((weights_zero, pieces))
    late = [lax.all_gather(piece, ("fsdp", "section"), axis=0, tiled=True) for piece in pieces]

    places = jnp.stack(
        [
            lax.dynamic_index_in_dim(
                positions, seats.of(section, lax.axis_index("ctx") * per + p)[1], 0, keepdims=False
            )
            for p in range(per)
        ]
    )
    order = (
        lax.broadcasted_iota(jnp.int32, (per, length, length), 1) == places[:, None, :]
    ).astype(bf16)
    order_back = (
        lax.broadcasted_iota(jnp.int32, (per, length, length), 2) == places[:, :, None]
    ).astype(bf16)

    def to_sorted(rows):
        return (
            jnp.einsum("bpt,btd->bpd", order, rows, preferred_element_type=f32)
            .astype(bf16)
            .reshape(per * length, width)
        )

    def to_stored(rows):
        return jnp.einsum(
            "btp,bpd->btd", order_back, rows.reshape(per, length, width), preferred_element_type=f32
        ).astype(bf16)

    start = to_sorted(block_rows)
    grad_final = to_sorted(cotangent_rows)
    early = []

    def attend_zero(project):
        attended, gathered = attend_gather(project, length, 1, shards_own[:2])
        early.extend(gathered)
        return attended

    middle, kept_zero = layer_forward(weights_zero, smalls[0], start, attend_zero)
    weights = [weights_zero, (*early, *late)]
    line = ctxs == 4
    outs = []

    def attend_one(project):
        carry = Carry(4, layer=0, rows=to_stored(middle), stored=stored)
        attended, (out_zero,) = attend_forward(project, length, carry)
        outs.append(out_zero)
        return attended

    final, kept_one = layer_forward(weights[1], smalls[1], middle, attend_one)
    halves = []

    def pull_one(kept, grads):
        carry = Carry(5, grads, line, 1, to_stored(final), stored)
        pulled, (reduced, out_one) = attend_back(*kept, length, carry)
        outs.append(out_one)
        halves.append(reduced)
        return pulled

    def pull_zero(kept, grads):
        carry = Carry(6, grads, line)
        pulled, (reduced,) = attend_back(*kept, length, carry)
        halves.append(reduced)
        return pulled

    grad_middle, grads_one, small_one, _ = layer_back(
        weights[1], smalls[1], kept_one, grad_final, None, pull_one
    )
    carry = Carry(2, grads_one, line, 1, to_stored(grad_middle), stored)
    grad_start, grads_zero, small_zero, (rest_one, in_one) = layer_back(
        weights[0], smalls[0], kept_zero, grad_middle, carry, pull_zero
    )

    def repack(small):
        vectors, fc = small
        vectors = jnp.transpose(vectors.reshape(8, fsdps, shard_width), (1, 0, 2))
        packed = jnp.concatenate([vectors, fc.reshape(fsdps, -1, shard_width)], axis=1)
        packed = packed.reshape(fsdps, 1, -1, CHUNK)
        depth = w_qkv.shape[1] // 2
        return jnp.pad(packed, ((0, 0), (0, 0), (0, depth - packed.shape[2]), (0, 0))).astype(bf16)

    pack = jnp.concatenate([repack(small_zero), repack(small_one)], axis=1)
    pack = pack.reshape(-1, CHUNK)
    rest_zero, in_zero = Carry(
        3, (*grads_zero, pack), line, 0, to_stored(grad_start), stored
    ).alone()
    reduced_one = jnp.concatenate([rest_one, halves[0]], axis=0)
    packed = rest_zero[-1].reshape(-1, shard_width)[:12].astype(f32)
    reduced_zero = jnp.concatenate([rest_zero[:-1], halves[1]], axis=0)
    section_out = jnp.where(first, outs[0], outs[1])[None]
    section_in_grad = jnp.where(first, in_zero, in_one)[None]
    arrived = swap(jnp.where(first, reduced_one, reduced_zero))
    mine = jnp.where(first, reduced_zero, reduced_one)
    low = jnp.where(first, mine, arrived)
    high = jnp.where(first, arrived, mine)
    shapes = [(matrix.shape[1] // 2, matrix.shape[2]) for matrix in (w_qkv, w_proj, w_fc, w_out)]
    big = [
        jnp.concatenate([a, b], axis=0).astype(f32)[None]
        for a, b in zip(unchunk(low, shapes), unchunk(high, shapes))
    ]

    return (
        section_out,
        section_in_grad,
        *big,
        packed[None, 0:2],
        packed[None, 2:4],
        packed[None, 4:6],
        packed[None, 6:8],
        packed[8:].reshape(1, -1),
    )


def solution(mesh):
    matrix = P("section", "fsdp", None)
    vectors = P("section", None, "fsdp")
    rows_out = P("section", "fsdp", "ctx", None)
    return jax.shard_map(
        shards,
        mesh=mesh,
        in_specs=(
            P("fsdp", "ctx", None),
            P("fsdp", None),
            P("fsdp", "ctx", None),
            *([matrix] * 4),
            *([vectors] * 4),
            P("section", "fsdp"),
        ),
        out_specs=(
            rows_out,
            rows_out,
            *([matrix] * 4),
            *([vectors] * 4),
            P("section", "fsdp"),
        ),
        check_vma=False,
    )
```

```python
import functools

import jax
import jax.numpy as jnp
from jax import lax
from jax.experimental import pallas as pl
from jax.experimental.pallas import tpu as pltpu
from jax.sharding import PartitionSpec as P

H = 12
HD = 64
PAIR = 2 * HD
SCALE = HD**-0.5

masked_score = -1e30
norm_eps = 1e-05
f32 = jnp.float32
bf16 = jnp.bfloat16


def layer_norm(hidden, gain, offset):
    center = hidden - jnp.mean(hidden, axis=-1, keepdims=True)
    spread = jnp.mean(center * center, axis=-1, keepdims=True)
    return center * lax.rsqrt(spread + norm_eps) * gain + offset


def gelu_tanh(inputs):
    return jax.nn.gelu(inputs, approximate=True)


def mm(left, right):
    return lax.dot_general(left, right, (((1,), (0,)), ((), ())), preferred_element_type=f32)


def mm_nt(left, right):
    return lax.dot_general(left, right, (((1,), (1,)), ((), ())), preferred_element_type=f32)


def mm_tn(left, right):
    return lax.dot_general(left, right, (((0,), (0,)), ((), ())), preferred_element_type=f32)


def masked_scores(keys, queries, start, block):
    scores = mm_nt(keys, queries)
    down = lax.broadcasted_iota(jnp.int32, (block, block), 0)
    across = lax.broadcasted_iota(jnp.int32, (block, block), 1)
    corner = jnp.where(across >= down, scores[start:], masked_score)
    if start == 0:
        return corner
    return jnp.concatenate([scores[:start], corner], axis=0)


def attend_kernel(block, q_ref, k_ref, v_ref, o_ref, log_ref):
    length = q_ref.shape[0]
    for head in range(2):
        cols = slice(head * HD, (head + 1) * HD)
        for start in range(0, length, block):
            end = start + block
            queries = (q_ref[start:end, cols].astype(f32) * SCALE).astype(bf16)
            scores = masked_scores(k_ref[:end, cols], queries, start, block)
            top = jnp.max(scores, axis=0, keepdims=True)
            weights = jnp.exp(scores - top)
            total = jnp.sum(weights, axis=0, keepdims=True)
            mixed = mm_tn(v_ref[:end, cols], weights.astype(bf16)) / total
            o_ref[start:end, cols] = mixed.T.astype(bf16)
            log_ref[0, 0, head : head + 1, start:end] = top + jnp.log(total)


def attend_back_kernel(
    block, q_ref, k_ref, v_ref, do_ref, o_ref, log_ref, dq_ref, dk_ref, dv_ref, dk_sum, dv_sum
):
    length = q_ref.shape[0]
    for head in range(2):
        cols = slice(head * HD, (head + 1) * HD)
        for start in range(length - block, -1, -block):
            end = start + block
            queries = (q_ref[start:end, cols].astype(f32) * SCALE).astype(bf16)
            grads = do_ref[start:end, cols]
            product = grads.astype(f32) * o_ref[start:end, cols].astype(f32)
            delta = jnp.sum(product.T, axis=0, keepdims=True)
            keys = k_ref[:end, cols]
            scores = masked_scores(keys, queries, start, block)
            probs = jnp.exp(scores - log_ref[0, 0, head : head + 1, start:end])
            grad_probs = mm_nt(v_ref[:end, cols], grads)
            grad_scores = (probs * (grad_probs - delta)).astype(bf16)
            dv = mm(probs.astype(bf16), grads)
            dk = mm(grad_scores, queries)
            if end == length:
                dv_sum[:end, cols] = dv
                dk_sum[:end, cols] = dk
            else:
                dv_sum[:end, cols] += dv
                dk_sum[:end, cols] += dk
            dq = mm_tn(keys, grad_scores) * SCALE
            dq_ref[start:end, cols] = dq.T.astype(bf16)
    dk_ref[...] = dk_sum[...].astype(bf16)
    dv_ref[...] = dv_sum[...].astype(bf16)


def query_block(length):
    return 256 if length % 256 == 0 else length


def head_spec(length, offset):
    return pl.BlockSpec((length, PAIR), lambda b, h: (b, offset + h))


def log_spec(length):
    return pl.BlockSpec((1, 1, 2, length), lambda b, h: (b, h, 0, 0))


def attend_forward(project, length, carry):
    rows = project.shape[0]
    count = rows // length
    pairs = H // 2
    grid = (count, pairs)
    body = functools.partial(attend_kernel, query_block(length))
    outs = pl.pallas_call(
        carry.kernel(body, 3, 2, 0, grid),
        grid=grid,
        in_specs=[head_spec(length, 0), head_spec(length, pairs), head_spec(length, 2 * pairs)]
        + [ANY] * len(carry.ins),
        out_specs=[head_spec(length, 0), log_spec(length)] + [ANY] * len(carry.outs),
        out_shape=[
            jax.ShapeDtypeStruct((rows, H * HD), bf16),
            jax.ShapeDtypeStruct((count, pairs, 2, length), f32),
        ]
        + carry.outs,
        scratch_shapes=carry.scratch,
        compiler_params=carry.params(),
        cost_estimate=pl.CostEstimate(
            flops=8 * rows * length * H * HD,
            bytes_accessed=8 * rows * H * HD,
            transcendentals=rows * length * H // 2,
        ),
    )(project, project, project, *carry.ins)
    return outs[:2], carry.result(outs[2:])


def attend_back(project, grad_mixed, mixed, log_total, length, carry):
    rows = project.shape[0]
    count = rows // length
    pairs = H // 2
    grid = (count, pairs)
    body = functools.partial(attend_back_kernel, query_block(length))
    outs = pl.pallas_call(
        carry.kernel(body, 6, 3, 2, grid),
        grid=grid,
        in_specs=[
            head_spec(length, 0),
            head_spec(length, pairs),
            head_spec(length, 2 * pairs),
            head_spec(length, 0),
            head_spec(length, 0),
            log_spec(length),
        ]
        + [ANY] * len(carry.ins),
        out_specs=[head_spec(length, 0)] * 3 + [ANY] * len(carry.outs),
        out_shape=[jax.ShapeDtypeStruct((rows, H * HD), bf16)] * 3 + carry.outs,
        scratch_shapes=[pltpu.VMEM((length, PAIR), f32)] * 2 + carry.scratch,
        compiler_params=carry.params(),
        cost_estimate=pl.CostEstimate(
            flops=20 * rows * length * H * HD,
            bytes_accessed=16 * rows * H * HD,
            transcendentals=rows * length * H // 2,
        ),
    )(project, project, project, grad_mixed, mixed, log_total, *carry.ins)
    return outs[:3], carry.result(outs[3:])


TILE = 512
BLOCK = 256
ROOT = 0.7978845608028654
CUBE = 0.044715


def norm_back(hidden, grad, gain):
    center = hidden - jnp.mean(hidden, axis=-1, keepdims=True)
    scale = lax.rsqrt(jnp.mean(center * center, axis=-1, keepdims=True) + norm_eps)
    unit = center * scale
    scaled = grad * gain
    shift = jnp.mean(scaled, axis=-1, keepdims=True)
    tilt = jnp.mean(scaled * unit, axis=-1, keepdims=True)
    return unit, (scaled - shift - unit * tilt) * scale


def whole_spec(shape):
    return pl.BlockSpec(shape, lambda *at: (0,) * len(shape), pipeline_mode=pl.Buffered(1))


def mlp_kernel(
    hidden_ref,
    mixed_ref,
    w_proj_ref,
    w_fc_ref,
    w_out_ref,
    vectors_ref,
    fc_bias_ref,
    after_ref,
    normed_ref,
    inner_ref,
    result_ref,
    total,
):
    step = pl.program_id(0)
    rows = hidden_ref.shape[0]
    for start in range(0, rows, BLOCK):
        here = slice(start, start + BLOCK)

        @pl.when(step == 0)
        def _():
            after = hidden_ref[here].astype(f32) + mm(mixed_ref[here], w_proj_ref[...])
            after = after + vectors_ref[2:3]
            after_ref[here] = after
            normed_ref[here] = layer_norm(after, vectors_ref[0:1], vectors_ref[1:2]).astype(bf16)
            total[here] = after + vectors_ref[3:4]

        inner = mm(normed_ref[here], w_fc_ref[...]) + fc_bias_ref[...]
        inner_ref[here] = inner
        bend = jnp.tanh(ROOT * (inner + CUBE * (inner * inner * inner)))
        active = (inner * (0.5 * (1.0 + bend))).astype(bf16)
        summed = total[here] + mm(active, w_out_ref[...])
        total[here] = summed

        @pl.when(step == pl.num_programs(0) - 1)
        def _():
            result_ref[here] = summed.astype(bf16)


def mlp(weights, smalls, layer_in, mixed, carry):
    _, w_proj, w_fc, w_out = weights
    gains, offsets, _, out_bias, fc_bias = smalls
    rows, width = layer_in.shape
    wide = w_fc.shape[1]
    tile = TILE if wide % TILE == 0 else wide
    grid = (wide // tile,)
    vectors = jnp.stack([gains[1], offsets[1], out_bias[0], out_bias[1]])

    def along(height):
        return pl.BlockSpec((height, tile), lambda i: (0, i))

    outs = pl.pallas_call(
        carry.kernel(mlp_kernel, 7, 4, 1, grid),
        grid=grid,
        in_specs=[
            whole_spec((rows, width)),
            whole_spec((rows, width)),
            whole_spec((width, width)),
            along(width),
            pl.BlockSpec((tile, width), lambda i: (i, 0)),
            whole_spec((4, width)),
            along(1),
        ]
        + [ANY] * len(carry.ins),
        out_specs=[
            whole_spec((rows, width)),
            whole_spec((rows, width)),
            along(rows),
            whole_spec((rows, width)),
        ]
        + [ANY] * len(carry.outs),
        out_shape=[
            jax.ShapeDtypeStruct((rows, width), f32),
            jax.ShapeDtypeStruct((rows, width), bf16),
            jax.ShapeDtypeStruct((rows, wide), f32),
            jax.ShapeDtypeStruct((rows, width), bf16),
        ]
        + carry.outs,
        scratch_shapes=[pltpu.VMEM((rows, width), f32)] + carry.scratch,
        compiler_params=carry.params(),
        cost_estimate=pl.CostEstimate(
            flops=4 * rows * width * wide + 2 * rows * width * width,
            bytes_accessed=4 * rows * wide + 4 * wide * width + 12 * rows * width,
            transcendentals=rows * wide,
        ),
    )(layer_in, mixed, w_proj, w_fc, w_out, vectors, fc_bias[None], *carry.ins)
    return outs[:4], carry.result(outs[4:])


def qkv_back_kernel(
    dq_ref, dk_ref, dv_ref, normed_ref, w_ref, hidden_ref, dafter_ref, gain_ref,
    dw_ref, dx_ref, sums_ref,
):
    rows, width = dq_ref.shape
    parts = (dq_ref, dk_ref, dv_ref)
    for i, part in enumerate(parts):
        columns = slice(i * width, (i + 1) * width)
        dw_ref[:, columns] = mm_tn(normed_ref[...], part[...]).astype(bf16)
    sums_ref[...] = jnp.zeros(sums_ref.shape, f32)
    for start in range(0, rows, BLOCK):
        here = slice(start, start + BLOCK)
        grad = jnp.zeros((BLOCK, width), f32)
        for i, part in enumerate(parts):
            grad = grad + mm_nt(part[here], w_ref[:, i * width : (i + 1) * width])
        unit, back = norm_back(hidden_ref[here].astype(f32), grad, gain_ref[...])
        dx_ref[here] = (dafter_ref[here] + back).astype(bf16)
        sums_ref[0:1] += jnp.sum(grad * unit, axis=0, keepdims=True)
        sums_ref[1:2] += jnp.sum(grad, axis=0, keepdims=True)
        sums_ref[2:3] += jnp.sum(dq_ref[here].astype(f32), axis=0, keepdims=True)
        sums_ref[3:4] += jnp.sum(dv_ref[here].astype(f32), axis=0, keepdims=True)


def qkv_back(w_qkv, gain, kept, grads, grad_after):
    layer_in, normed = kept[:2]
    rows, width = layer_in.shape
    return pl.pallas_call(
        qkv_back_kernel,
        out_shape=[
            jax.ShapeDtypeStruct((width, 3 * width), bf16),
            jax.ShapeDtypeStruct((rows, width), bf16),
            jax.ShapeDtypeStruct((8, width), f32),
        ],
        compiler_params=pltpu.CompilerParams(vmem_limit_bytes=60 * 1024 * 1024),
        cost_estimate=pl.CostEstimate(
            flops=12 * rows * width * width,
            bytes_accessed=18 * rows * width + 12 * width * width,
            transcendentals=0,
        ),
    )(*grads, normed, w_qkv, layer_in, grad_after, gain[None])


def mlp_back_kernel(
    dy_ref,
    normed_ref,
    inner_ref,
    w_fc_ref,
    w_out_ref,
    after_ref,
    mixed_ref,
    w_proj_ref,
    gain_ref,
    dw_out_ref,
    dw_fc_ref,
    dfc_ref,
    dw_proj_ref,
    dmixed_ref,
    dafter_ref,
    sums_ref,
    total,
    active,
    dinner,
    dbranch,
):
    step = pl.program_id(0)
    rows = dy_ref.shape[0]

    @pl.when(step == 0)
    def _():
        total[...] = jnp.zeros(total.shape, f32)

    for start in range(0, rows, BLOCK):
        here = slice(start, start + BLOCK)
        inner = inner_ref[here]
        square = inner * inner
        bend = jnp.tanh(ROOT * (inner + CUBE * (square * inner)))
        half = 0.5 * (1.0 + bend)
        active[here] = (inner * half).astype(bf16)
        slope = half + (0.5 * ROOT) * inner * (1.0 - bend * bend) * (1.0 + (3.0 * CUBE) * square)
        grad = (mm_nt(dy_ref[here], w_out_ref[...]) * slope).astype(bf16)
        dinner[here] = grad
        total[here] += mm_nt(grad, w_fc_ref[...])
    dw_out_ref[...] = mm_tn(active[...], dy_ref[...]).astype(bf16)
    dw_fc_ref[...] = mm_tn(normed_ref[...], dinner[...]).astype(bf16)
    dfc_ref[...] = jnp.sum(dinner[...].astype(f32), axis=0, keepdims=True)

    @pl.when(step == pl.num_programs(0) - 1)
    def _():
        sums_ref[...] = jnp.zeros(sums_ref.shape, f32)
        for start in range(0, rows, BLOCK):
            here = slice(start, start + BLOCK)
            grad = total[here]
            out = dy_ref[here].astype(f32)
            unit, back = norm_back(after_ref[here], grad, gain_ref[...])
            after = out + back
            dafter_ref[here] = after
            branch = after.astype(bf16)
            dbranch[here] = branch
            sums_ref[0:1] += jnp.sum(grad * unit, axis=0, keepdims=True)
            sums_ref[1:2] += jnp.sum(grad, axis=0, keepdims=True)
            sums_ref[2:3] += jnp.sum(branch.astype(f32), axis=0, keepdims=True)
            sums_ref[3:4] += jnp.sum(out, axis=0, keepdims=True)
            dmixed_ref[here] = mm_nt(branch, w_proj_ref[...]).astype(bf16)
        dw_proj_ref[...] = mm_tn(mixed_ref[...], dbranch[...]).astype(bf16)


def mlp_back(weights, gain, kept, grad_out, carry):
    _, w_proj, w_fc, w_out = weights
    _, _, _, mixed, _, after, normed_two, inner = kept
    rows, width = grad_out.shape
    wide = inner.shape[1]
    tile = TILE if wide % TILE == 0 else wide
    grid = (wide // tile,)
    once = pl.Buffered(1)

    def whole(shape):
        return pl.BlockSpec(shape, lambda i: (0, 0), pipeline_mode=once)

    across = pl.BlockSpec((tile, width), lambda i: (i, 0))

    def along(height):
        return pl.BlockSpec((height, tile), lambda i: (0, i))

    outs = pl.pallas_call(
        carry.kernel(mlp_back_kernel, 9, 7, 4, grid),
        grid=grid,
        in_specs=[
            whole((rows, width)),
            whole((rows, width)),
            along(rows),
            along(width),
            across,
            whole((rows, width)),
            whole((rows, width)),
            whole((width, width)),
            whole((1, width)),
        ]
        + [ANY] * len(carry.ins),
        out_specs=[
            across,
            along(width),
            along(1),
            whole((width, width)),
            whole((rows, width)),
            whole((rows, width)),
            whole((8, width)),
        ]
        + [ANY] * len(carry.outs),
        out_shape=[
            jax.ShapeDtypeStruct((wide, width), bf16),
            jax.ShapeDtypeStruct((width, wide), bf16),
            jax.ShapeDtypeStruct((1, wide), f32),
            jax.ShapeDtypeStruct((width, width), bf16),
            jax.ShapeDtypeStruct((rows, width), bf16),
            jax.ShapeDtypeStruct((rows, width), f32),
            jax.ShapeDtypeStruct((8, width), f32),
        ]
        + carry.outs,
        scratch_shapes=[
            pltpu.VMEM((rows, width), f32),
            pltpu.VMEM((rows, tile), bf16),
            pltpu.VMEM((rows, tile), bf16),
            pltpu.VMEM((rows, width), bf16),
        ]
        + carry.scratch,
        compiler_params=carry.params(),
        cost_estimate=pl.CostEstimate(
            flops=8 * rows * width * wide + 4 * rows * width * width,
            bytes_accessed=4 * rows * wide + 8 * wide * width + 16 * rows * width,
            transcendentals=rows * wide,
        ),
    )(
        grad_out,
        normed_two,
        inner,
        w_fc,
        w_out,
        after,
        mixed,
        w_proj,
        gain[None],
        *carry.ins,
    )
    return outs[:7], carry.result(outs[7:])


def layer_forward(weights, smalls, layer_in, attend, carry):
    w_qkv = weights[0]
    gains, offsets, attn_bias, _, _ = smalls
    width = layer_in.shape[-1]
    normed = layer_norm(layer_in.astype(f32), gains[0], offsets[0]).astype(bf16)
    bias = jnp.concatenate([attn_bias[0], jnp.zeros((width,), f32), attn_bias[1]])
    project = (mm(normed, w_qkv) + bias).astype(bf16)
    (mixed, log_total), attended = attend(project)
    if callable(weights[1]):
        weights = weights[1](attended)
    (after, normed_two, inner, result), carried = mlp(weights, smalls, layer_in, mixed, carry)
    kept = (layer_in, normed, project, mixed, log_total, after, normed_two, inner)
    return result, kept, weights, attended, carried


def layer_back(weights, smalls, kept, grad_out, carry, attend_pull):
    w_qkv, w_proj, w_fc, w_out = weights
    gains, offsets, attn_bias, out_bias, fc_bias = smalls
    layer_in, normed, project, mixed, log_total, after, normed_two, inner = kept
    grads, carried = mlp_back(weights, gains[1], kept, grad_out, carry)
    grad_w_out, grad_w_fc, grad_fc_bias, grad_w_proj, grad_mixed, grad_after, sums = grads
    grad_q, grad_k, grad_v = attend_pull(
        (project, grad_mixed, mixed, log_total), (grad_w_fc, grad_w_out)
    )
    grad_w_qkv, grad_input, more = qkv_back(
        w_qkv, gains[0], kept, (grad_q, grad_k, grad_v), grad_after
    )
    vectors = jnp.concatenate([more[:4], sums[:4]], axis=0)
    return grad_input, (grad_w_qkv, grad_w_proj), (vectors, grad_fc_bias[0]), carried


MESH = pl.DeviceIdType.MESH
ANY = pl.BlockSpec(memory_space=pl.ANY)
CHUNK = 768


def greet(groups):
    sides = {side for group in groups for side in group}
    places = lax.axis_size("ctx")
    barrier = pltpu.get_barrier_semaphore()
    for flip, step, bits in sorted(sides):
        device = {
            "section": lax.axis_index("section") ^ flip,
            "ctx": lax.rem(lax.axis_index("ctx") + step, places),
            "fsdp": lax.axis_index("fsdp") ^ bits,
        }
        pl.semaphore_signal(barrier, inc=1, device_id=device, device_id_type=MESH)
    pl.semaphore_wait(barrier, len(sides))


def chip_group():
    return [(1, 0, 0)] + [(flip, 0, bits) for flip in (0, 1) for bits in (1, 2)]


def corner_group():
    return [(0, 0, 3), (1, 0, 3)]


def line_group():
    return [(0, step, 0) for step in range(1, lax.axis_size("ctx"))]


def column_group():
    return [(1, 0, 0)] + [
        (flip, step, 0) for step in range(1, lax.axis_size("ctx")) for flip in (0, 1)
    ]


def remote(source, target, send, recv, device):
    return pltpu.make_async_remote_copy(
        src_ref=source,
        dst_ref=target,
        send_sem=send,
        recv_sem=recv,
        device_id=device,
        device_id_type=MESH,
    )


class Gather:
    def __init__(self, layer, shards, outs, send, recv, local, *bounce):
        self.layer, self.shards, self.outs = layer, shards, outs
        self.bounce = bounce
        self.send, self.recv, self.local = send, recv, local
        self.section = lax.axis_index("section")
        self.index = lax.axis_index("fsdp")
        self.sibling = {"section": 1 - self.section}

    def across(self, bits, section=None):
        where = {"fsdp": self.index ^ bits}
        if section is not None:
            where["section"] = section
        return where

    def copy(self, m, slot, source, target, device):
        return remote(source, target, self.send.at[m, slot], self.recv.at[m, slot], device)

    def first(self, m, bits, half):
        slot = 0 if bits == 1 else 1
        return remote(
            self.shards[m].at[half],
            self.outs[m].at[self.index, half],
            self.send.at[m, slot + 8 * half],
            self.recv.at[m, slot],
            self.across(bits, half),
        )

    def arrived(self, m, bits):
        slot = 0 if bits == 1 else 1
        place = self.outs[m].at[self.index ^ bits, self.section]
        return self.copy(m, slot, place, place, self.across(bits))

    def own(self, m):
        return self.copy(m, 2, self.shards[m], self.outs[m].at[self.index], self.sibling)

    def take(self, m):
        return pltpu.make_async_copy(self.shards[m], self.bounce[m], self.local.at[0, m])

    def keep(self, m):
        return pltpu.make_async_copy(
            self.bounce[m], self.outs[m].at[self.index], self.local.at[1, m]
        )

    def corner(self, m, bits):
        middle = self.outs[m].shape[2] // 2
        rows = pl.ds(0, middle) if bits == 1 else pl.ds(middle, middle)
        place = self.outs[m].at[self.index ^ bits, self.section, rows]
        return self.copy(m, 3 if bits == 1 else 4, place, place, self.across(3 ^ bits))

    def trade(self, m, bits):
        place = self.outs[m].at[self.index ^ bits, self.section]
        return self.copy(m, 4 + bits, place, place, self.sibling)

    def start(self):
        @pl.when(self.section == self.layer)
        def _():
            for m in range(len(self.shards)):
                for half in (1 - self.layer, self.layer):
                    for bits in (1, 2):
                        self.first(m, bits, half).start()
                self.own(m).start()
                self.take(m).start()
            for m in range(len(self.shards)):
                self.take(m).wait()
                self.keep(m).start()

    def middle(self, m):
        for bits in (1, 2):
            self.arrived(m, bits).wait_recv()
            self.corner(m, bits).start()
            self.trade(m, bits).start()

    def last(self, m):
        for bits in (1, 2):
            self.corner(m, bits).wait_recv()
        self.trade(m, 3).start()

    def finish(self, m):
        for bits in (1, 2, 3):
            copy = self.trade(m, bits)
            copy.wait_send()
            copy.wait_recv()
        for bits in (1, 2):
            self.corner(m, bits).wait_send()

        @pl.when(self.section == self.layer)
        def _():
            for half in (0, 1):
                for bits in (1, 2):
                    self.first(m, bits, half).wait_send()
            self.own(m).wait_send()
            self.keep(m).wait()

        @pl.when(self.section != self.layer)
        def _():
            self.own(m).wait_recv()

class Seats:
    def __init__(self, seqs):
        self.sections, self.places = lax.axis_size("section"), lax.axis_size("ctx")
        self.seqs = seqs
        self.per = -(-seqs // (self.sections * self.places))
        self.size = self.places * self.per
        self.real = [min(max(seqs - i * self.size, 0), self.size) for i in range(self.sections)]
        self.skip = [(self.size - real) // 2 for real in self.real]

    def of(self, section, slot):
        real = jnp.where(section == 0, self.real[0], self.real[1])
        skip = jnp.where(section == 0, self.skip[0], self.skip[1])
        taken = (slot >= skip) & (slot < skip + real)
        return taken, jnp.clip(section * self.size + slot - skip, 0, self.seqs - 1)

    def home(self, seq):
        section, slot = seq // self.size, seq % self.size + self.skip[seq // self.size]
        return section, slot // self.per, slot % self.per


class Bring:
    def __init__(self, rows, outs, send, recv, local, zeros):
        self.rows, self.outs = rows, outs
        self.send, self.recv, self.local, self.zeros = send, recv, local, zeros
        self.seats = Seats(rows[0].shape[0])
        self.section, self.z = lax.axis_index("section"), lax.axis_index("ctx")
        self.depth = rows[0].shape[1]

    @staticmethod
    def scratch(rows, per, places):
        return [
            pltpu.SemaphoreType.DMA((len(rows), places * per)),
            pltpu.SemaphoreType.DMA((len(rows), per, places)),
            pltpu.SemaphoreType.DMA((len(rows), per, places)),
            pltpu.VMEM(rows[0].shape[1:], bf16),
        ]

    def span(self, z):
        return pl.ds(z * self.depth, self.depth)

    def copy(self, a, seq, place, p):
        return remote(
            self.rows[a].at[seq],
            self.outs[a].at[p, self.span(self.z)],
            self.send.at[a, place * self.seats.per + p],
            self.recv.at[a, p, self.z],
            {"ctx": place},
        )

    def arrival(self, a, p, place):
        target = self.outs[a].at[p, self.span(place)]
        return remote(target, target, self.send.at[a, 0], self.recv.at[a, p, place], {"ctx": place})

    def stay(self, a, seq, p):
        return pltpu.make_async_copy(
            self.rows[a].at[seq], self.outs[a].at[p, self.span(self.z)], self.local.at[a, p, 0]
        )

    def blank(self, a, p, place):
        return pltpu.make_async_copy(
            self.zeros, self.outs[a].at[p, self.span(place)], self.local.at[a, p, place]
        )

    def each(self, a, going, staying, coming, empty):
        for p in range(self.seats.per):
            for place in range(self.seats.places):
                taken, seq = self.seats.of(self.section, place * self.seats.per + p)

                @pl.when(taken & (place != self.z))
                def _():
                    going(a, seq, place, p)

            taken, seq = self.seats.of(self.section, self.z * self.seats.per + p)

            @pl.when(taken)
            def _():
                staying(a, seq, p)
                for place in range(self.seats.places):

                    @pl.when(place != self.z)
                    def _():
                        coming(a, p, place)

            @pl.when(jnp.logical_not(taken))
            def _():
                for place in range(self.seats.places):
                    empty(a, p, place)

    def clear(self):
        self.zeros[...] = jnp.zeros(self.zeros.shape, bf16)

    def start(self, a):
        self.each(
            a,
            lambda *at: self.copy(*at).start(),
            lambda *at: self.stay(*at).start(),
            lambda *at: None,
            lambda *at: self.blank(*at).start(),
        )

    def finish(self, a):
        self.each(
            a,
            lambda *at: self.copy(*at).wait_send(),
            lambda *at: self.stay(*at).wait(),
            lambda *at: self.arrival(*at).wait_recv(),
            lambda *at: self.blank(*at).wait(),
        )


class Deliver:
    def __init__(self, layer, rows, out, send, recv, local):
        self.layer, self.rows, self.out = layer, rows, out
        self.send, self.recv, self.local = send, recv, local
        self.seats = Seats(out.shape[0])
        self.section, self.z = lax.axis_index("section"), lax.axis_index("ctx")
        self.depth = out.shape[1]

    @staticmethod
    def scratch(seqs, per, places):
        return [
            pltpu.SemaphoreType.DMA((per, places)),
            pltpu.SemaphoreType.DMA((seqs,)),
            pltpu.SemaphoreType.DMA((per,)),
        ]

    def source(self, p, place):
        return self.rows.at[p, pl.ds(place * self.depth, self.depth)]

    def copy(self, p, place, seq):
        return remote(
            self.source(p, place),
            self.out.at[seq],
            self.send.at[p, place],
            self.recv.at[seq],
            {"section": self.layer, "ctx": place},
        )

    def stay(self, p, place, seq):
        return pltpu.make_async_copy(self.source(p, place), self.out.at[seq], self.local.at[p])

    def each(self, going, staying):
        for p in range(self.seats.per):
            taken, seq = self.seats.of(self.section, self.z * self.seats.per + p)
            for place in range(self.seats.places):
                here = (self.section == self.layer) & (self.z == place)

                @pl.when(taken & here)
                def _():
                    staying(p, place, seq)

                @pl.when(taken & jnp.logical_not(here))
                def _():
                    going(p, place, seq)

    def start(self):
        self.each(
            lambda *at: self.copy(*at).start(),
            lambda *at: self.stay(*at).start(),
        )

    def finish(self):
        self.each(
            lambda *at: self.copy(*at).wait_send(),
            lambda *at: self.stay(*at).wait(),
        )
        for seq in range(self.seats.seqs):
            section, place, p = self.seats.home(seq)

            @pl.when(
                (self.section == self.layer)
                & ((self.section != section) | (self.z != place))
            )
            def _():
                target = self.out.at[seq]
                remote(
                    target, target, self.send.at[0, 0], self.recv.at[seq], {"section": 1 - self.section}
                ).wait_recv()


class Spread:
    def __init__(self, block, out, send, recv, local):
        self.block, self.out, self.send, self.recv, self.local = block, out, send, recv, local
        self.section, self.index = lax.axis_index("section"), lax.axis_index("fsdp")

    @staticmethod
    def scratch():
        return [
            pltpu.SemaphoreType.DMA((8,)),
            pltpu.SemaphoreType.DMA((8,)),
            pltpu.SemaphoreType.DMA,
        ]

    def copies(self):
        for flip in (0, 1):
            for bits in range(4):
                if flip or bits:
                    yield remote(
                        self.block,
                        self.out.at[self.section, self.index],
                        self.send.at[4 * flip + bits],
                        self.recv.at[4 * flip + bits],
                        {"section": self.section ^ flip, "fsdp": self.index ^ bits},
                    )

    def stay(self):
        return pltpu.make_async_copy(
            self.block, self.out.at[self.section, self.index], self.local
        )

    def start(self):
        for copy in self.copies():
            copy.start()
        self.stay().start()

    def finish(self):
        for copy in self.copies():
            copy.wait_send()
            copy.wait_recv()
        self.stay().wait()


def gather_scratch(shards):
    count = len(shards)
    return [
        pltpu.SemaphoreType.DMA((count, 10)),
        pltpu.SemaphoreType.DMA((count, 8)),
        pltpu.SemaphoreType.DMA((2, count)),
    ] + [pltpu.VMEM(shard.shape, shard.dtype) for shard in shards]


def gather_shapes(shards):
    return [jax.ShapeDtypeStruct((4,) + shard.shape, shard.dtype) for shard in shards]


def split_shards(shards):
    return [shard.reshape(2, -1, shard.shape[-1]) for shard in shards]


def join_shards(outs):
    return tuple(out.reshape(-1, out.shape[-1]) for out in outs)


class Reduce:
    def __init__(self, line, layer, items, out, scratch):
        self.line, self.layer, self.items, self.out = line, layer, items, out
        (
            self.own,
            self.twin,
            self.near_corner,
            self.far_corner,
            self.near,
            self.far,
            self.outer,
            self.inner,
            self.partial,
            self.total,
            self.send,
            self.recv,
            self.local,
            self.done,
        ) = scratch
        self.section = lax.axis_index("section")
        self.index = lax.axis_index("fsdp")
        self.z = lax.axis_index("ctx")
        self.count = self.own.shape[0]
        self.sibling = {"section": 1 - self.section}
        self.x = {"fsdp": self.index ^ 1}
        self.y = {"fsdp": self.index ^ 2}
        self.is_inner = (self.z == 1) | (self.z == 2)
        self.end = {"ctx": jnp.where(self.z == 1, 0, 3)}
        self.toward = {"ctx": jnp.where(self.z == 0, 1, 2)}
        self.opposite = {"ctx": 3 - self.z}

    def chunks(self):
        k = 0
        for item in self.items:
            rows, columns = item.shape[2:]
            depth = self.own.shape[2]
            for row in range(0, rows, depth):
                for column in range(0, columns, CHUNK):
                    yield k, item, pl.ds(row, depth), pl.ds(column, CHUNK)
                    k += 1

    def copy(self, k, slot, source, target, device):
        return remote(source, target, self.send.at[slot, k], self.recv.at[slot, k], device)

    def swap(self, k):
        return self.copy(k, 0, self.twin.at[k], self.twin.at[k], self.sibling)

    def load(self, k):
        return pltpu.make_async_copy(self.own.at[k], self.own.at[k], self.local.at[k])

    def corner(self, k, near):
        half = self.own.shape[2] // 2
        rows = pl.ds(0, half) if near else pl.ds(half, half)
        source = self.own.at[k, self.index ^ 3, rows]
        target = (self.near_corner if near else self.far_corner).at[k]
        return self.copy(k, 1 if near else 2, source, target, self.x if near else self.y)

    def side(self, k, near):
        source = self.own.at[k, self.index ^ (1 if near else 2)]
        target = (self.near if near else self.far).at[k]
        return self.copy(k, 3 if near else 4, source, target, self.x if near else self.y)

    def inward(self, k):
        return self.copy(k, 5, self.partial.at[k], self.outer.at[k], self.toward)

    def across(self, k):
        return self.copy(k, 6, self.partial.at[k], self.inner.at[k], self.opposite)

    def outward(self, k):
        return self.copy(k, 7, self.total.at[k], self.total.at[k], self.end)

    def start(self):
        for k, item, rows, columns in self.chunks():
            theirs = item.at[:, 1 - self.section, rows, columns]
            mine = item.at[:, self.section, rows, columns]
            self.copy(k, 0, theirs, self.twin.at[k], self.sibling).start()
            pltpu.make_async_copy(mine, self.own.at[k], self.local.at[k]).start()

    def stage(self, number, k):
        half = self.own.shape[2] // 2
        near, far = self.index ^ 1, self.index ^ 2
        if number == 0:
            self.load(k).wait()
            self.swap(k).wait_recv()
            for j in range(4):
                self.own[k, j] = self.own[k, j] + self.twin[k, j]
            self.corner(k, True).start()
            self.corner(k, False).start()
        elif number == 1:
            self.corner(k, True).wait_recv()
            self.corner(k, False).wait_recv()
            self.own[k, far, :half] = self.own[k, far, :half] + self.near_corner[k]
            self.own[k, near, half:] = self.own[k, near, half:] + self.far_corner[k]
            self.side(k, True).start()
            self.side(k, False).start()
        elif number == 2:
            self.side(k, True).wait_recv()
            self.side(k, False).wait_recv()
            summed = (
                self.own[k, self.index].astype(f32)
                + self.near[k].astype(f32)
                + self.far[k].astype(f32)
            ).astype(bf16)
            if not self.line:
                self.total[k] = summed
                return
            self.partial[k] = summed

            @pl.when(jnp.logical_not(self.is_inner))
            def _():
                self.inward(k).start()
        elif number == 3 and self.line:

            @pl.when(self.is_inner)
            def _():
                self.inward(k).wait_recv()
                self.partial[k] = self.partial[k] + self.outer[k]
                self.across(k).start()
        elif number == 4 and self.line:

            @pl.when(self.is_inner)
            def _():
                self.across(k).wait_recv()
                self.total[k] = self.partial[k] + self.inner[k]
                self.outward(k).start()

    def step(self, t, lags):
        for number, lag in enumerate(lags):
            k = t - lag

            @pl.when((k >= 0) & (k < self.count))
            def _():
                self.stage(number, k)

    def finish(self, k):
        self.swap(k).wait_send()
        for near in (True, False):
            self.corner(k, near).wait_send()
            self.side(k, near).wait_send()
        if self.line:

            @pl.when(self.is_inner)
            def _():
                self.across(k).wait_send()
                self.outward(k).wait_send()

            @pl.when(jnp.logical_not(self.is_inner))
            def _():
                self.inward(k).wait_send()
                self.outward(k).wait_recv()

    def write(self):
        return pltpu.make_async_copy(self.total, self.out.at[self.section], self.local.at[0])

    def give(self):
        place = self.out.at[1 - self.layer]
        return remote(self.total, place, self.done.at[0], self.done.at[1], self.sibling)

    def close(self):
        self.write().start()

        @pl.when(self.section != self.layer)
        def _():
            self.give().start()
            self.give().wait_send()

        @pl.when(self.section == self.layer)
        def _():
            self.give().wait_recv()

        self.write().wait()


LAGS = (0, 1, 3, 4, 5)
CARRIED_LAGS = (0, 2, 4, 6, 8)


class ReducePart:
    lags = CARRIED_LAGS

    def __init__(self, layer, grads, line):
        self.layer, self.line = layer, line
        self.ins = [grad.reshape(4, 2, -1, grad.shape[-1]) for grad in grads]
        depth = min(item.shape[2] for item in self.ins)
        self.chunks = sum((item.shape[2] // depth) * (item.shape[3] // CHUNK) for item in self.ins)
        self.outs = [jax.ShapeDtypeStruct((2, self.chunks, depth, CHUNK), bf16)]
        self.scratch = reduce_scratch(self.chunks, depth)

    def groups(self):
        return [column_group(), [(0, 0, 1), (0, 0, 2)]]

    def bind(self, ins, outs, scratch):
        return Reduce(self.line, self.layer, ins, outs[0], scratch)

    def begin(self, reduce):
        reduce.start()

    def tick(self, reduce, step, steps):
        lags = LAGS if steps == 1 else self.lags
        share = -(-(self.chunks + lags[-1]) // steps)

        def advance(t, _):
            reduce.step(step * share + t, lags)
            return 0

        lax.fori_loop(0, share, advance, 0)

    def end(self, reduce):
        def finish(k, _):
            reduce.finish(k)
            return 0

        lax.fori_loop(0, reduce.count, finish, 0)
        reduce.close()

    def result(self, outs):
        return outs[0] if self.line else lax.psum(outs[0], "ctx")


class DeliverPart:
    def __init__(self, layer, rows, stored):
        seats = Seats(stored[0])
        self.layer = layer
        self.ins = [rows.reshape(seats.per, -1, rows.shape[-1])]
        self.outs = [jax.ShapeDtypeStruct(stored, bf16)]
        self.scratch = Deliver.scratch(stored[0], seats.per, seats.places)

    def groups(self):
        return [column_group()]

    def bind(self, ins, outs, scratch):
        return Deliver(self.layer, ins[0], outs[0], *scratch)

    def begin(self, deliver):
        deliver.start()

    def tick(self, deliver, step, steps):
        pass

    def end(self, deliver):
        deliver.finish()

    def result(self, outs):
        return outs[0]


class BringPart:
    def __init__(self, rows):
        seats = Seats(rows.shape[0])
        _, depth, width = rows.shape
        self.ins = [rows]
        self.outs = [jax.ShapeDtypeStruct((seats.per, depth * seats.places, width), bf16)]
        self.scratch = Bring.scratch([rows], seats.per, seats.places)

    def groups(self):
        return [line_group()]

    def bind(self, ins, outs, scratch):
        return Bring(ins, outs, *scratch)

    def begin(self, bring):
        bring.clear()
        bring.start(0)

    def tick(self, bring, step, steps):
        pass

    def end(self, bring):
        bring.finish(0)

    def result(self, outs):
        return outs[0]


class SpreadPart:
    def __init__(self, block):
        self.ins = [block]
        self.outs = [jax.ShapeDtypeStruct((2, 4) + block.shape, bf16)]
        self.scratch = Spread.scratch()

    def groups(self):
        return [chip_group(), corner_group()]

    def bind(self, ins, outs, scratch):
        return Spread(ins[0], outs[0], *scratch)

    def begin(self, spread):
        spread.start()

    def tick(self, spread, step, steps):
        pass

    def end(self, spread):
        spread.finish()

    def result(self, outs):
        return outs[0]


class GatherPart:
    def __init__(self, layer, shards):
        self.layer = layer
        self.ins = split_shards(shards)
        self.outs = gather_shapes(self.ins)
        self.scratch = gather_scratch(self.ins)

    def groups(self):
        return [chip_group()]

    def bind(self, ins, outs, scratch):
        return Gather(self.layer, ins, outs, *scratch)

    def begin(self, gather):
        gather.start()

    def tick(self, gather, step, steps):
        count = len(self.ins)
        if steps == 1:
            for m in range(count):
                gather.middle(m)
                if m > 0:
                    gather.last(m - 1)
            gather.last(count - 1)
            return
        for m in range(count):

            @pl.when(step == steps - 1 - count + m)
            def _():
                gather.middle(m)

            @pl.when(step == steps - 1)
            def _():
                gather.last(m)

    def end(self, gather):
        for m in range(len(self.ins)):
            gather.finish(m)

    def result(self, outs):
        return join_shards(outs)


class Carry:
    def __init__(self, collective, *parts):
        self.collective, self.parts = collective, parts
        self.ins = [array for part in parts for array in part.ins]
        self.outs = [shape for part in parts for shape in part.outs]
        self.scratch = [shape for part in parts for shape in part.scratch]

    def params(self, limit=60):
        return pltpu.CompilerParams(
            collective_id=self.collective,
            has_side_effects=self.collective is not None,
            vmem_limit_bytes=limit * 1024 * 1024,
        )

    def kernel(self, body, ins, outs, scratch, grid):
        if not self.parts:
            return body
        steps = 1
        for size in grid:
            steps *= size

        def run(*refs):
            pieces, at = [], 0
            for size in (ins, len(self.ins), outs, len(self.outs), scratch, len(self.scratch)):
                pieces.append(refs[at : at + size])
                at += size
            bound, at = [], [0, 0, 0]
            for part in self.parts:
                sizes = [len(part.ins), len(part.outs), len(part.scratch)]
                taken = [
                    pieces[2 * i + 1][at[i] : at[i] + sizes[i]] for i in range(3)
                ]
                at = [at[i] + sizes[i] for i in range(3)]
                bound.append((part, part.bind(*taken)))
            step = 0
            for axis in range(len(grid)):
                step = step * grid[axis] + pl.program_id(axis)

            def begin():
                greet([group for part in self.parts for group in part.groups()])
                for part, state in bound:
                    part.begin(state)

            def end():
                for part, state in bound:
                    part.end(state)

            if steps == 1:
                begin()
            else:
                pl.when(step == 0)(begin)
            body(*pieces[0], *pieces[2], *pieces[4])
            for part, state in bound:
                part.tick(state, step, steps)
            if steps == 1:
                end()
            else:
                pl.when(step == steps - 1)(end)

        return run

    def alone(self):
        outs = pl.pallas_call(
            self.kernel(lambda: None, 0, 0, 0, ()),
            in_specs=[ANY] * len(self.ins),
            out_specs=[ANY] * len(self.outs),
            out_shape=self.outs,
            scratch_shapes=self.scratch,
            compiler_params=self.params(),
        )(*self.ins)
        return self.result(outs)

    def result(self, outs):
        results, at = [], 0
        for part in self.parts:
            results.append(part.result(outs[at : at + len(part.outs)]))
            at += len(part.outs)
        return results


def reduce_scratch(count, depth):
    block = (count, depth, CHUNK)
    half = (count, depth // 2, CHUNK)
    return (
        [pltpu.VMEM((count, 4, depth, CHUNK), bf16)] * 2
        + [pltpu.VMEM(half, bf16)] * 2
        + [pltpu.VMEM(block, bf16)] * 6
        + [
            pltpu.SemaphoreType.DMA((8, count)),
            pltpu.SemaphoreType.DMA((8, count)),
            pltpu.SemaphoreType.DMA((count,)),
            pltpu.SemaphoreType.DMA((2,)),
        ]
    )


def unchunk(blocks, shapes):
    depth = blocks.shape[-2]
    parts, k = [], 0
    for rows, columns in shapes:
        high, wide = rows // depth, columns // CHUNK
        part = blocks[..., k : k + high * wide, :, :]
        if wide > 1:
            part = jnp.concatenate([part[..., j, :, :] for j in range(wide)], axis=-1)
        parts.append(part.reshape(blocks.shape[:-3] + (rows, columns)))
        k += high * wide
    return parts


def shards(
    block_input,
    positions,
    cotangent,
    w_qkv,
    w_proj,
    w_fc,
    w_out,
    ln_gain,
    ln_bias,
    attn_bias,
    out_bias,
    fc_bias,
):
    section = lax.axis_index("section")
    first = section == 0
    ctxs = lax.axis_size("ctx")
    fsdps = lax.axis_size("fsdp")
    local_seqs, local_rows, width = block_input.shape
    stored = block_input.shape
    length = positions.shape[1]
    seats = Seats(local_seqs)
    per = seats.per
    shard_width = ln_gain.shape[2]

    pack = jnp.concatenate(
        [ln_gain[0], ln_bias[0], attn_bias[0], out_bias[0], fc_bias[0].reshape(-1, shard_width)]
    )
    pack = jnp.pad(pack, ((0, 16 - pack.shape[0]), (0, 256 - shard_width)))

    def unpack(packed):
        packed = packed[:, :12, :shard_width]
        vectors = jnp.transpose(packed[:, :8], (1, 0, 2)).reshape(8, -1).astype(f32)
        fc = packed[:, 8:].reshape(-1).astype(f32)
        return vectors[0:2], vectors[2:4], vectors[4:6], vectors[6:8], fc

    shards_own = [matrix[0] for matrix in (w_qkv, w_proj, w_fc, w_out)]
    block_rows, packs, first_weights = Carry(
        0, BringPart(block_input), SpreadPart(pack), GatherPart(0, shards_own[:2])
    ).alone()
    smalls = [unpack(packs[layer]) for layer in range(2)]

    places = jnp.stack(
        [
            lax.dynamic_index_in_dim(
                positions, seats.of(section, lax.axis_index("ctx") * per + p)[1], 0, keepdims=False
            )
            for p in range(per)
        ]
    )
    order = (
        lax.broadcasted_iota(jnp.int32, (per, length, length), 1) == places[:, None, :]
    ).astype(bf16)
    order_back = (
        lax.broadcasted_iota(jnp.int32, (per, length, length), 2) == places[:, :, None]
    ).astype(bf16)

    def to_sorted(rows):
        return (
            jnp.einsum("bpt,btd->bpd", order, rows, preferred_element_type=f32)
            .astype(bf16)
            .reshape(per * length, width)
        )

    def to_stored(rows):
        return jnp.einsum(
            "btp,bpd->btd", order_back, rows.reshape(per, length, width), preferred_element_type=f32
        ).astype(bf16)

    start = to_sorted(block_rows)
    line = ctxs == 4

    def attend_zero(project):
        carry = Carry(1, GatherPart(0, shards_own[2:]), BringPart(cotangent))
        return attend_forward(project, length, carry)

    middle, kept_zero, weights_zero, attended, (early,) = layer_forward(
        (first_weights[0], lambda attended: (*first_weights, *attended[0])),
        smalls[0],
        start,
        attend_zero,
        Carry(7, GatherPart(1, shards_own[:2])),
    )
    grad_final = to_sorted(attended[1])

    def attend_one(project):
        carry = Carry(4, GatherPart(1, shards_own[2:]), DeliverPart(0, to_stored(middle), stored))
        return attend_forward(project, length, carry)

    final, kept_one, weights_one, (_, out_zero), _ = layer_forward(
        (early[0], lambda attended: (*early, *attended[0])), smalls[1], middle, attend_one, Carry(None)
    )
    outs = [out_zero]
    halves = []

    def pull_one(kept, grads):
        carry = Carry(5, ReducePart(1, grads, line), DeliverPart(1, to_stored(final), stored))
        pulled, (reduced, out_one) = attend_back(*kept, length, carry)
        outs.append(out_one)
        halves.append(reduced)
        return pulled

    def pull_zero(kept, grads):
        pulled, (reduced,) = attend_back(*kept, length, Carry(6, ReducePart(0, grads, line)))
        halves.append(reduced)
        return pulled

    grad_middle, grads_one, small_one, _ = layer_back(
        weights_one, smalls[1], kept_one, grad_final, Carry(None), pull_one
    )
    carry = Carry(
        2, ReducePart(1, grads_one, line), DeliverPart(1, to_stored(grad_middle), stored)
    )
    grad_start, grads_zero, small_zero, (rest_one, in_one) = layer_back(
        weights_zero, smalls[0], kept_zero, grad_middle, carry, pull_zero
    )

    def repack(small):
        vectors, fc = small
        vectors = jnp.transpose(vectors.reshape(8, fsdps, shard_width), (1, 0, 2))
        packed = jnp.concatenate([vectors, fc.reshape(fsdps, -1, shard_width)], axis=1)
        depth = w_qkv.shape[1] // 2
        return jnp.pad(
            packed.astype(bf16),
            ((0, 0), (0, depth - packed.shape[1]), (0, CHUNK - packed.shape[2])),
        )[:, None]

    pack = jnp.concatenate([repack(small_zero), repack(small_one)], axis=1)
    pack = pack.reshape(-1, CHUNK)
    rest_zero, in_zero = Carry(
        3,
        ReducePart(0, (*grads_zero, pack), line),
        DeliverPart(0, to_stored(grad_start), stored),
    ).alone()
    packed = jnp.where(first, rest_zero[0, -1], rest_zero[1, -1])[:12, :shard_width].astype(f32)
    section_out = jnp.where(first, outs[0], outs[1])[None]
    section_in_grad = jnp.where(first, in_zero, in_one)[None]
    shapes = [(matrix.shape[1] // 2, matrix.shape[2]) for matrix in (w_qkv, w_proj, w_fc, w_out)]
    reduced = [
        jnp.where(first, rest_zero[:, :-1], rest_one),
        jnp.where(first, halves[1], halves[0]),
    ]
    big = [
        block.reshape(-1, block.shape[-1]).astype(f32)[None]
        for some, these in zip(reduced, (shapes[:2], shapes[2:]))
        for block in unchunk(some, these)
    ]

    return (
        section_out,
        section_in_grad,
        *big,
        packed[None, 0:8:4],
        packed[None, 1:8:4],
        packed[None, 2:4],
        packed[None, 6:8],
        packed[8:].reshape(1, -1),
    )


def solution(mesh):
    matrix = P("section", "fsdp", None)
    vectors = P("section", None, "fsdp")
    rows_out = P("section", "fsdp", "ctx", None)
    return jax.shard_map(
        shards,
        mesh=mesh,
        in_specs=(
            P("fsdp", "ctx", None),
            P("fsdp", None),
            P("fsdp", "ctx", None),
            *([matrix] * 4),
            *([vectors] * 4),
            P("section", "fsdp"),
        ),
        out_specs=(
            rows_out,
            rows_out,
            *([matrix] * 4),
            *([vectors] * 4),
            P("section", "fsdp"),
        ),
        check_vma=False,
    )
```

```python
import functools

import jax
import jax.numpy as jnp
from jax import lax
from jax.experimental import pallas as pl
from jax.experimental.pallas import tpu as pltpu
from jax.sharding import PartitionSpec as P

H = 12
HD = 64
PAIR = 2 * HD
SCALE = HD**-0.5

masked_score = -1e30
norm_eps = 1e-05
f32 = jnp.float32
bf16 = jnp.bfloat16


def layer_norm(hidden, gain, offset):
    center = hidden - jnp.mean(hidden, axis=-1, keepdims=True)
    spread = jnp.mean(center * center, axis=-1, keepdims=True)
    return center * lax.rsqrt(spread + norm_eps) * gain + offset


def gelu_tanh(inputs):
    return jax.nn.gelu(inputs, approximate=True)


def mm(left, right):
    return lax.dot_general(left, right, (((1,), (0,)), ((), ())), preferred_element_type=f32)


def mm_nt(left, right):
    return lax.dot_general(left, right, (((1,), (1,)), ((), ())), preferred_element_type=f32)


def mm_tn(left, right):
    return lax.dot_general(left, right, (((0,), (0,)), ((), ())), preferred_element_type=f32)


def masked_scores(keys, queries, start, block):
    scores = mm_nt(keys, queries)
    down = lax.broadcasted_iota(jnp.int32, (block, block), 0)
    across = lax.broadcasted_iota(jnp.int32, (block, block), 1)
    corner = jnp.where(across >= down, scores[start:], masked_score)
    if start == 0:
        return corner
    return jnp.concatenate([scores[:start], corner], axis=0)


def attend_kernel(block, q_ref, k_ref, v_ref, o_ref, log_ref):
    length = q_ref.shape[0]
    for head in range(2):
        cols = slice(head * HD, (head + 1) * HD)
        for start in range(0, length, block):
            end = start + block
            queries = (q_ref[start:end, cols].astype(f32) * SCALE).astype(bf16)
            scores = masked_scores(k_ref[:end, cols], queries, start, block)
            top = jnp.max(scores, axis=0, keepdims=True)
            weights = jnp.exp(scores - top)
            total = jnp.sum(weights, axis=0, keepdims=True)
            mixed = mm_tn(v_ref[:end, cols], weights.astype(bf16)) / total
            o_ref[start:end, cols] = mixed.T.astype(bf16)
            log_ref[0, 0, head : head + 1, start:end] = top + jnp.log(total)


def attend_back_kernel(
    block, q_ref, k_ref, v_ref, do_ref, o_ref, log_ref, dq_ref, dk_ref, dv_ref, dk_sum, dv_sum
):
    length = q_ref.shape[0]
    for head in range(2):
        cols = slice(head * HD, (head + 1) * HD)
        for start in range(length - block, -1, -block):
            end = start + block
            queries = (q_ref[start:end, cols].astype(f32) * SCALE).astype(bf16)
            grads = do_ref[start:end, cols]
            product = grads.astype(f32) * o_ref[start:end, cols].astype(f32)
            delta = jnp.sum(product.T, axis=0, keepdims=True)
            keys = k_ref[:end, cols]
            scores = masked_scores(keys, queries, start, block)
            probs = jnp.exp(scores - log_ref[0, 0, head : head + 1, start:end])
            grad_probs = mm_nt(v_ref[:end, cols], grads)
            grad_scores = (probs * (grad_probs - delta)).astype(bf16)
            dv = mm(probs.astype(bf16), grads)
            dk = mm(grad_scores, queries)
            if end == length:
                dv_sum[:end, cols] = dv
                dk_sum[:end, cols] = dk
            else:
                dv_sum[:end, cols] += dv
                dk_sum[:end, cols] += dk
            dq = mm_tn(keys, grad_scores) * SCALE
            dq_ref[start:end, cols] = dq.T.astype(bf16)
    dk_ref[...] = dk_sum[...].astype(bf16)
    dv_ref[...] = dv_sum[...].astype(bf16)


def query_block(length):
    return 256 if length % 256 == 0 else length


def head_spec(length, offset):
    return pl.BlockSpec((length, PAIR), lambda b, h: (b, offset + h))


def log_spec(length):
    return pl.BlockSpec((1, 1, 2, length), lambda b, h: (b, h, 0, 0))


def attend_forward(project, length, carry):
    rows = project.shape[0]
    count = rows // length
    pairs = H // 2
    grid = (count, pairs)
    body = functools.partial(attend_kernel, query_block(length))
    outs = pl.pallas_call(
        carry.kernel(body, 3, 2, 0, grid),
        grid=grid,
        in_specs=[head_spec(length, 0), head_spec(length, pairs), head_spec(length, 2 * pairs)]
        + [ANY] * len(carry.ins),
        out_specs=[head_spec(length, 0), log_spec(length)] + [ANY] * len(carry.outs),
        out_shape=[
            jax.ShapeDtypeStruct((rows, H * HD), bf16),
            jax.ShapeDtypeStruct((count, pairs, 2, length), f32),
        ]
        + carry.outs,
        scratch_shapes=carry.scratch,
        compiler_params=carry.params(),
        cost_estimate=pl.CostEstimate(
            flops=8 * rows * length * H * HD,
            bytes_accessed=8 * rows * H * HD,
            transcendentals=rows * length * H // 2,
        ),
    )(project, project, project, *carry.ins)
    return outs[:2], carry.result(outs[2:])


def attend_back(project, grad_mixed, mixed, log_total, length, carry):
    rows = project.shape[0]
    count = rows // length
    pairs = H // 2
    grid = (count, pairs)
    body = functools.partial(attend_back_kernel, query_block(length))
    outs = pl.pallas_call(
        carry.kernel(body, 6, 3, 2, grid),
        grid=grid,
        in_specs=[
            head_spec(length, 0),
            head_spec(length, pairs),
            head_spec(length, 2 * pairs),
            head_spec(length, 0),
            head_spec(length, 0),
            log_spec(length),
        ]
        + [ANY] * len(carry.ins),
        out_specs=[head_spec(length, 0)] * 3 + [ANY] * len(carry.outs),
        out_shape=[jax.ShapeDtypeStruct((rows, H * HD), bf16)] * 3 + carry.outs,
        scratch_shapes=[pltpu.VMEM((length, PAIR), f32)] * 2 + carry.scratch,
        compiler_params=carry.params(),
        cost_estimate=pl.CostEstimate(
            flops=20 * rows * length * H * HD,
            bytes_accessed=16 * rows * H * HD,
            transcendentals=rows * length * H // 2,
        ),
    )(project, project, project, grad_mixed, mixed, log_total, *carry.ins)
    return outs[:3], carry.result(outs[3:])


TILE = 512
BLOCK = 256
ROOT = 0.7978845608028654
CUBE = 0.044715


def norm_back(hidden, grad, gain):
    center = hidden - jnp.mean(hidden, axis=-1, keepdims=True)
    scale = lax.rsqrt(jnp.mean(center * center, axis=-1, keepdims=True) + norm_eps)
    unit = center * scale
    scaled = grad * gain
    shift = jnp.mean(scaled, axis=-1, keepdims=True)
    tilt = jnp.mean(scaled * unit, axis=-1, keepdims=True)
    return unit, (scaled - shift - unit * tilt) * scale


def whole_spec(shape):
    return pl.BlockSpec(shape, lambda *at: (0,) * len(shape), pipeline_mode=pl.Buffered(1))


def mlp_kernel(
    hidden_ref,
    mixed_ref,
    w_proj_ref,
    w_fc_ref,
    w_out_ref,
    vectors_ref,
    fc_bias_ref,
    after_ref,
    normed_ref,
    inner_ref,
    result_ref,
    total,
):
    step = pl.program_id(0)
    rows = hidden_ref.shape[0]
    blocks = [slice(start, start + BLOCK) for start in range(0, rows, BLOCK)]

    @pl.when(step == 0)
    def _():
        for here in blocks:
            after = hidden_ref[here].astype(f32) + mm(mixed_ref[here], w_proj_ref[...])
            after = after + vectors_ref[2:3]
            after_ref[here] = after
            normed_ref[here] = layer_norm(after, vectors_ref[0:1], vectors_ref[1:2]).astype(bf16)
            total[here] = after + vectors_ref[3:4]

    for here in blocks:
        inner = mm(normed_ref[here], w_fc_ref[...]) + fc_bias_ref[...]
        inner_ref[here] = inner
        bend = jnp.tanh(inner * (ROOT + (ROOT * CUBE) * (inner * inner)))
        half = 0.5 * inner
        active = (half + half * bend).astype(bf16)
        total[here] += mm(active, w_out_ref[...])

    @pl.when(step == pl.num_programs(0) - 1)
    def _():
        result_ref[...] = total[...].astype(bf16)


def mlp(weights, smalls, layer_in, mixed, carry):
    _, w_proj, w_fc, w_out = weights
    gains, offsets, _, out_bias, fc_bias = smalls
    rows, width = layer_in.shape
    wide = w_fc.shape[1]
    tile = TILE if wide % TILE == 0 else wide
    grid = (wide // tile,)
    vectors = jnp.stack([gains[1], offsets[1], out_bias[0], out_bias[1]])

    def along(height):
        return pl.BlockSpec((height, tile), lambda i: (0, i))

    outs = pl.pallas_call(
        carry.kernel(mlp_kernel, 7, 4, 1, grid),
        grid=grid,
        in_specs=[
            whole_spec((rows, width)),
            whole_spec((rows, width)),
            whole_spec((width, width)),
            along(width),
            pl.BlockSpec((tile, width), lambda i: (i, 0)),
            whole_spec((4, width)),
            along(1),
        ]
        + [ANY] * len(carry.ins),
        out_specs=[
            whole_spec((rows, width)),
            whole_spec((rows, width)),
            along(rows),
            whole_spec((rows, width)),
        ]
        + [ANY] * len(carry.outs),
        out_shape=[
            jax.ShapeDtypeStruct((rows, width), f32),
            jax.ShapeDtypeStruct((rows, width), bf16),
            jax.ShapeDtypeStruct((rows, wide), f32),
            jax.ShapeDtypeStruct((rows, width), bf16),
        ]
        + carry.outs,
        scratch_shapes=[pltpu.VMEM((rows, width), f32)] + carry.scratch,
        compiler_params=carry.params(),
        cost_estimate=pl.CostEstimate(
            flops=4 * rows * width * wide + 2 * rows * width * width,
            bytes_accessed=4 * rows * wide + 4 * wide * width + 12 * rows * width,
            transcendentals=rows * wide,
        ),
    )(layer_in, mixed, w_proj, w_fc, w_out, vectors, fc_bias[None], *carry.ins)
    return outs[:4], carry.result(outs[4:])


def qkv_back_kernel(
    dq_ref, dk_ref, dv_ref, normed_ref, w_ref, hidden_ref, dafter_ref, gain_ref,
    dw_ref, dx_ref, sums_ref,
):
    rows, width = dq_ref.shape
    parts = (dq_ref, dk_ref, dv_ref)

    def weights(i):
        columns = slice(i * width, (i + 1) * width)
        dw_ref[:, columns] = mm_tn(normed_ref[...], parts[i][...]).astype(bf16)

    def inputs():
        sums_ref[...] = jnp.zeros(sums_ref.shape, f32)
        for start in range(0, rows, BLOCK):
            here = slice(start, start + BLOCK)
            grad = jnp.zeros((BLOCK, width), f32)
            for i, part in enumerate(parts):
                grad = grad + mm_nt(part[here], w_ref[:, i * width : (i + 1) * width])
            unit, back = norm_back(hidden_ref[here].astype(f32), grad, gain_ref[...])
            dx_ref[here] = (dafter_ref[here] + back).astype(bf16)
            sums_ref[0:1] += jnp.sum(grad * unit, axis=0, keepdims=True)
            sums_ref[1:2] += jnp.sum(grad, axis=0, keepdims=True)
            sums_ref[2:3] += jnp.sum(dq_ref[here].astype(f32), axis=0, keepdims=True)
            sums_ref[3:4] += jnp.sum(dv_ref[here].astype(f32), axis=0, keepdims=True)

    for i in range(3):
        pl.when(pl.program_id(0) == i)(functools.partial(weights, i))
    pl.when(pl.program_id(0) == 3)(inputs)


def qkv_back(w_qkv, gain, kept, grads, grad_after, carry):
    layer_in, normed = kept[:2]
    rows, width = layer_in.shape
    grid = (4,)
    tall = whole_spec((rows, width))
    wide = whole_spec((width, 3 * width))
    outs = pl.pallas_call(
        carry.kernel(qkv_back_kernel, 8, 3, 0, grid),
        grid=grid,
        in_specs=[tall] * 4
        + [wide, tall, tall, whole_spec((1, width))]
        + [ANY] * len(carry.ins),
        out_specs=[wide, tall, whole_spec((8, width))] + [ANY] * len(carry.outs),
        out_shape=[
            jax.ShapeDtypeStruct((width, 3 * width), bf16),
            jax.ShapeDtypeStruct((rows, width), bf16),
            jax.ShapeDtypeStruct((8, width), f32),
        ]
        + carry.outs,
        scratch_shapes=carry.scratch,
        compiler_params=carry.params(),
        cost_estimate=pl.CostEstimate(
            flops=12 * rows * width * width,
            bytes_accessed=18 * rows * width + 12 * width * width,
            transcendentals=0,
        ),
    )(*grads, normed, w_qkv, layer_in, grad_after, gain[None], *carry.ins)
    return outs[:3], carry.result(outs[3:])


def mlp_back_kernel(
    dy_ref,
    normed_ref,
    inner_ref,
    w_fc_ref,
    w_out_ref,
    after_ref,
    mixed_ref,
    w_proj_ref,
    gain_ref,
    dw_out_ref,
    dw_fc_ref,
    dfc_ref,
    dw_proj_ref,
    dmixed_ref,
    dafter_ref,
    sums_ref,
    total,
    active,
    dinner,
    dbranch,
):
    step = pl.program_id(0)
    rows = dy_ref.shape[0]

    @pl.when(step == 0)
    def _():
        total[...] = jnp.zeros(total.shape, f32)

    for start in range(0, rows, BLOCK):
        here = slice(start, start + BLOCK)
        inner = inner_ref[here]
        square = inner * inner
        bend = jnp.tanh(inner * (ROOT + (ROOT * CUBE) * square))
        half = 0.5 * (1.0 + bend)
        active[here] = (inner * half).astype(bf16)
        slope = half + (0.5 * ROOT) * inner * (1.0 - bend * bend) * (1.0 + (3.0 * CUBE) * square)
        grad = (mm_nt(dy_ref[here], w_out_ref[...]) * slope).astype(bf16)
        dinner[here] = grad
        total[here] += mm_nt(grad, w_fc_ref[...])
    dw_out_ref[...] = mm_tn(active[...], dy_ref[...]).astype(bf16)
    dw_fc_ref[...] = mm_tn(normed_ref[...], dinner[...]).astype(bf16)
    dfc_ref[...] = jnp.sum(dinner[...].astype(f32), axis=0, keepdims=True)

    @pl.when(step == pl.num_programs(0) - 1)
    def _():
        sums_ref[...] = jnp.zeros(sums_ref.shape, f32)
        for start in range(0, rows, BLOCK):
            here = slice(start, start + BLOCK)
            grad = total[here]
            out = dy_ref[here].astype(f32)
            unit, back = norm_back(after_ref[here], grad, gain_ref[...])
            after = out + back
            dafter_ref[here] = after
            branch = after.astype(bf16)
            dbranch[here] = branch
            sums_ref[0:1] += jnp.sum(grad * unit, axis=0, keepdims=True)
            sums_ref[1:2] += jnp.sum(grad, axis=0, keepdims=True)
            sums_ref[2:3] += jnp.sum(branch.astype(f32), axis=0, keepdims=True)
            sums_ref[3:4] += jnp.sum(out, axis=0, keepdims=True)
            dmixed_ref[here] = mm_nt(branch, w_proj_ref[...]).astype(bf16)
        dw_proj_ref[...] = mm_tn(mixed_ref[...], dbranch[...]).astype(bf16)


def mlp_back(weights, gain, kept, grad_out, carry):
    _, w_proj, w_fc, w_out = weights
    _, _, _, mixed, _, after, normed_two, inner = kept
    rows, width = grad_out.shape
    wide = inner.shape[1]
    tile = TILE if wide % TILE == 0 else wide
    grid = (wide // tile,)
    once = pl.Buffered(1)

    def whole(shape):
        return pl.BlockSpec(shape, lambda i: (0, 0), pipeline_mode=once)

    across = pl.BlockSpec((tile, width), lambda i: (i, 0))

    def along(height):
        return pl.BlockSpec((height, tile), lambda i: (0, i))

    outs = pl.pallas_call(
        carry.kernel(mlp_back_kernel, 9, 7, 4, grid),
        grid=grid,
        in_specs=[
            whole((rows, width)),
            whole((rows, width)),
            along(rows),
            along(width),
            across,
            whole((rows, width)),
            whole((rows, width)),
            whole((width, width)),
            whole((1, width)),
        ]
        + [ANY] * len(carry.ins),
        out_specs=[
            across,
            along(width),
            along(1),
            whole((width, width)),
            whole((rows, width)),
            whole((rows, width)),
            whole((8, width)),
        ]
        + [ANY] * len(carry.outs),
        out_shape=[
            jax.ShapeDtypeStruct((wide, width), bf16),
            jax.ShapeDtypeStruct((width, wide), bf16),
            jax.ShapeDtypeStruct((1, wide), f32),
            jax.ShapeDtypeStruct((width, width), bf16),
            jax.ShapeDtypeStruct((rows, width), bf16),
            jax.ShapeDtypeStruct((rows, width), f32),
            jax.ShapeDtypeStruct((8, width), f32),
        ]
        + carry.outs,
        scratch_shapes=[
            pltpu.VMEM((rows, width), f32),
            pltpu.VMEM((rows, tile), bf16),
            pltpu.VMEM((rows, tile), bf16),
            pltpu.VMEM((rows, width), bf16),
        ]
        + carry.scratch,
        compiler_params=carry.params(),
        cost_estimate=pl.CostEstimate(
            flops=8 * rows * width * wide + 4 * rows * width * width,
            bytes_accessed=4 * rows * wide + 8 * wide * width + 16 * rows * width,
            transcendentals=rows * wide,
        ),
    )(
        grad_out,
        normed_two,
        inner,
        w_fc,
        w_out,
        after,
        mixed,
        w_proj,
        gain[None],
        *carry.ins,
    )
    return outs[:7], carry.result(outs[7:])


def layer_forward(weights, smalls, layer_in, attend, carry):
    w_qkv = weights[0]
    gains, offsets, attn_bias, _, _ = smalls
    width = layer_in.shape[-1]
    normed = layer_norm(layer_in.astype(f32), gains[0], offsets[0]).astype(bf16)
    bias = jnp.concatenate([attn_bias[0], jnp.zeros((width,), f32), attn_bias[1]])
    project = (mm(normed, w_qkv) + bias).astype(bf16)
    (mixed, log_total), attended = attend(project)
    if callable(weights[1]):
        weights = weights[1](attended)
    (after, normed_two, inner, result), carried = mlp(weights, smalls, layer_in, mixed, carry)
    kept = (layer_in, normed, project, mixed, log_total, after, normed_two, inner)
    return result, kept, weights, attended, carried


def layer_back(weights, smalls, kept, grad_out, carry, attend_pull, last):
    w_qkv, w_proj, w_fc, w_out = weights
    gains, offsets, attn_bias, out_bias, fc_bias = smalls
    layer_in, normed, project, mixed, log_total, after, normed_two, inner = kept
    grads, carried = mlp_back(weights, gains[1], kept, grad_out, carry)
    grad_w_out, grad_w_fc, grad_fc_bias, grad_w_proj, grad_mixed, grad_after, sums = grads
    grad_q, grad_k, grad_v = attend_pull(
        (project, grad_mixed, mixed, log_total), (grad_w_proj, grad_w_fc, grad_w_out), carried
    )
    carry, done = last(grad_w_fc)
    (grad_w_qkv, grad_input, more), carried = qkv_back(
        w_qkv, gains[0], kept, (grad_q, grad_k, grad_v), grad_after, carry
    )
    done(carried)
    vectors = jnp.concatenate([more[:4], sums[:4]], axis=0)
    grads = (grad_w_qkv, grad_w_proj, grad_w_fc)
    return grad_input, grads, (vectors, grad_fc_bias[0])


MESH = pl.DeviceIdType.MESH
ANY = pl.BlockSpec(memory_space=pl.ANY)
CHUNK = 768
DEPTH = 96


def greet(groups):
    sides = {side for group in groups for side in group}
    places = lax.axis_size("ctx")
    barrier = pltpu.get_barrier_semaphore()
    for flip, step, bits in sorted(sides):
        device = {
            "section": lax.axis_index("section") ^ flip,
            "ctx": lax.rem(lax.axis_index("ctx") + step, places),
            "fsdp": lax.axis_index("fsdp") ^ bits,
        }
        pl.semaphore_signal(barrier, inc=1, device_id=device, device_id_type=MESH)
    pl.semaphore_wait(barrier, len(sides))


def chip_group():
    return [(1, 0, 0)] + [(flip, 0, bits) for flip in (0, 1) for bits in (1, 2)]


def corner_group():
    return [(0, 0, 3), (1, 0, 3)]


def line_group():
    return [(0, step, 0) for step in range(1, lax.axis_size("ctx"))]


def column_group():
    return [(1, 0, 0)] + [
        (flip, step, 0) for step in range(1, lax.axis_size("ctx")) for flip in (0, 1)
    ]


def remote(source, target, send, recv, device):
    return pltpu.make_async_remote_copy(
        src_ref=source,
        dst_ref=target,
        send_sem=send,
        recv_sem=recv,
        device_id=device,
        device_id_type=MESH,
    )


class Gather:
    def __init__(self, layer, shards, outs, send, recv, local, *bounce):
        self.layer, self.shards, self.outs = layer, shards, outs
        self.bounce = bounce
        self.send, self.recv, self.local = send, recv, local
        self.section = lax.axis_index("section")
        self.index = lax.axis_index("fsdp")
        self.sibling = {"section": 1 - self.section}

    def across(self, bits, section=None):
        where = {"fsdp": self.index ^ bits}
        if section is not None:
            where["section"] = section
        return where

    def copy(self, m, slot, source, target, device):
        return remote(source, target, self.send.at[m, slot], self.recv.at[m, slot], device)

    def first(self, m, bits, half):
        slot = 0 if bits == 1 else 1
        return remote(
            self.shards[m].at[half],
            self.outs[m].at[self.index, half],
            self.send.at[m, slot + 8 * half],
            self.recv.at[m, slot],
            self.across(bits, half),
        )

    def arrived(self, m, bits):
        slot = 0 if bits == 1 else 1
        place = self.outs[m].at[self.index ^ bits, self.section]
        return self.copy(m, slot, place, place, self.across(bits))

    def own(self, m):
        return self.copy(m, 2, self.shards[m], self.outs[m].at[self.index], self.sibling)

    def take(self, m):
        return pltpu.make_async_copy(self.shards[m], self.bounce[m], self.local.at[0, m])

    def keep(self, m):
        return pltpu.make_async_copy(
            self.bounce[m], self.outs[m].at[self.index], self.local.at[1, m]
        )

    def corner(self, m, bits):
        middle = self.outs[m].shape[2] // 2
        rows = pl.ds(0, middle) if bits == 1 else pl.ds(middle, middle)
        place = self.outs[m].at[self.index ^ bits, self.section, rows]
        return self.copy(m, 3 if bits == 1 else 4, place, place, self.across(3 ^ bits))

    def trade(self, m, bits):
        place = self.outs[m].at[self.index ^ bits, self.section]
        return self.copy(m, 4 + bits, place, place, self.sibling)

    def start(self):
        @pl.when(self.section == self.layer)
        def _():
            for m in range(len(self.shards)):
                for half in (1 - self.layer, self.layer):
                    for bits in (1, 2):
                        self.first(m, bits, half).start()
                self.own(m).start()
                self.take(m).start()
            for m in range(len(self.shards)):
                self.take(m).wait()
                self.keep(m).start()

    def middle(self, m):
        for bits in (1, 2):
            self.arrived(m, bits).wait_recv()
            self.corner(m, bits).start()
            self.trade(m, bits).start()

    def last(self, m):
        for bits in (1, 2):
            self.corner(m, bits).wait_recv()
        self.trade(m, 3).start()

    def finish(self, m):
        for bits in (1, 2, 3):
            copy = self.trade(m, bits)
            copy.wait_send()
            copy.wait_recv()
        for bits in (1, 2):
            self.corner(m, bits).wait_send()

        @pl.when(self.section == self.layer)
        def _():
            for half in (0, 1):
                for bits in (1, 2):
                    self.first(m, bits, half).wait_send()
            self.own(m).wait_send()
            self.keep(m).wait()

        @pl.when(self.section != self.layer)
        def _():
            self.own(m).wait_recv()

class Seats:
    def __init__(self, seqs):
        self.sections, self.places = lax.axis_size("section"), lax.axis_size("ctx")
        self.seqs = seqs
        self.per = -(-seqs // (self.sections * self.places))
        self.size = self.places * self.per
        self.real = [min(max(seqs - i * self.size, 0), self.size) for i in range(self.sections)]
        self.skip = [(self.size - real) // 2 for real in self.real]

    def of(self, section, slot):
        real = jnp.where(section == 0, self.real[0], self.real[1])
        skip = jnp.where(section == 0, self.skip[0], self.skip[1])
        taken = (slot >= skip) & (slot < skip + real)
        return taken, jnp.clip(section * self.size + slot - skip, 0, self.seqs - 1)

    def home(self, seq):
        section, slot = seq // self.size, seq % self.size + self.skip[seq // self.size]
        return section, slot // self.per, slot % self.per


class Bring:
    def __init__(self, rows, outs, send, recv, local, zeros):
        self.rows, self.outs = rows, outs
        self.send, self.recv, self.local, self.zeros = send, recv, local, zeros
        self.seats = Seats(rows[0].shape[0])
        self.section, self.z = lax.axis_index("section"), lax.axis_index("ctx")
        self.depth = rows[0].shape[1]

    @staticmethod
    def scratch(rows, per, places):
        return [
            pltpu.SemaphoreType.DMA((len(rows), places * per)),
            pltpu.SemaphoreType.DMA((len(rows), per, places)),
            pltpu.SemaphoreType.DMA((len(rows), per, places)),
            pltpu.VMEM(rows[0].shape[1:], bf16),
        ]

    def span(self, z):
        return pl.ds(z * self.depth, self.depth)

    def copy(self, a, seq, place, p):
        return remote(
            self.rows[a].at[seq],
            self.outs[a].at[p, self.span(self.z)],
            self.send.at[a, place * self.seats.per + p],
            self.recv.at[a, p, self.z],
            {"ctx": place},
        )

    def arrival(self, a, p, place):
        target = self.outs[a].at[p, self.span(place)]
        return remote(target, target, self.send.at[a, 0], self.recv.at[a, p, place], {"ctx": place})

    def stay(self, a, seq, p):
        return pltpu.make_async_copy(
            self.rows[a].at[seq], self.outs[a].at[p, self.span(self.z)], self.local.at[a, p, 0]
        )

    def blank(self, a, p, place):
        return pltpu.make_async_copy(
            self.zeros, self.outs[a].at[p, self.span(place)], self.local.at[a, p, place]
        )

    def each(self, a, going, staying, coming, empty):
        for p in range(self.seats.per):
            for place in range(self.seats.places):
                taken, seq = self.seats.of(self.section, place * self.seats.per + p)

                @pl.when(taken & (place != self.z))
                def _():
                    going(a, seq, place, p)

            taken, seq = self.seats.of(self.section, self.z * self.seats.per + p)

            @pl.when(taken)
            def _():
                staying(a, seq, p)
                for place in range(self.seats.places):

                    @pl.when(place != self.z)
                    def _():
                        coming(a, p, place)

            @pl.when(jnp.logical_not(taken))
            def _():
                for place in range(self.seats.places):
                    empty(a, p, place)

    def clear(self):
        self.zeros[...] = jnp.zeros(self.zeros.shape, bf16)

    def start(self, a):
        self.each(
            a,
            lambda *at: self.copy(*at).start(),
            lambda *at: self.stay(*at).start(),
            lambda *at: None,
            lambda *at: self.blank(*at).start(),
        )

    def finish(self, a):
        self.each(
            a,
            lambda *at: self.copy(*at).wait_send(),
            lambda *at: self.stay(*at).wait(),
            lambda *at: self.arrival(*at).wait_recv(),
            lambda *at: self.blank(*at).wait(),
        )


class Deliver:
    def __init__(self, layer, rows, out, send, recv, local):
        self.layer, self.rows, self.out = layer, rows, out
        self.send, self.recv, self.local = send, recv, local
        self.seats = Seats(out.shape[0])
        self.section, self.z = lax.axis_index("section"), lax.axis_index("ctx")
        self.depth = out.shape[1]

    @staticmethod
    def scratch(seqs, per, places):
        return [
            pltpu.SemaphoreType.DMA((per, places)),
            pltpu.SemaphoreType.DMA((seqs,)),
            pltpu.SemaphoreType.DMA((per,)),
        ]

    def source(self, p, place):
        return self.rows.at[p, pl.ds(place * self.depth, self.depth)]

    def copy(self, p, place, seq):
        return remote(
            self.source(p, place),
            self.out.at[seq],
            self.send.at[p, place],
            self.recv.at[seq],
            {"section": self.layer, "ctx": place},
        )

    def stay(self, p, place, seq):
        return pltpu.make_async_copy(self.source(p, place), self.out.at[seq], self.local.at[p])

    def each(self, going, staying):
        for p in range(self.seats.per):
            taken, seq = self.seats.of(self.section, self.z * self.seats.per + p)
            for place in range(self.seats.places):
                here = (self.section == self.layer) & (self.z == place)

                @pl.when(taken & here)
                def _():
                    staying(p, place, seq)

                @pl.when(taken & jnp.logical_not(here))
                def _():
                    going(p, place, seq)

    def start(self):
        self.each(
            lambda *at: self.copy(*at).start(),
            lambda *at: self.stay(*at).start(),
        )

    def finish(self):
        self.each(
            lambda *at: self.copy(*at).wait_send(),
            lambda *at: self.stay(*at).wait(),
        )
        for seq in range(self.seats.seqs):
            section, place, p = self.seats.home(seq)

            @pl.when(
                (self.section == self.layer)
                & ((self.section != section) | (self.z != place))
            )
            def _():
                target = self.out.at[seq]
                remote(
                    target, target, self.send.at[0, 0], self.recv.at[seq], {"section": 1 - self.section}
                ).wait_recv()


class Spread:
    def __init__(self, block, out, send, recv, local):
        self.block, self.out, self.send, self.recv, self.local = block, out, send, recv, local
        self.section, self.index = lax.axis_index("section"), lax.axis_index("fsdp")

    @staticmethod
    def scratch():
        return [
            pltpu.SemaphoreType.DMA((8,)),
            pltpu.SemaphoreType.DMA((8,)),
            pltpu.SemaphoreType.DMA,
        ]

    def copies(self):
        for flip in (0, 1):
            for bits in range(4):
                if flip or bits:
                    yield remote(
                        self.block,
                        self.out.at[self.section, self.index],
                        self.send.at[4 * flip + bits],
                        self.recv.at[4 * flip + bits],
                        {"section": self.section ^ flip, "fsdp": self.index ^ bits},
                    )

    def stay(self):
        return pltpu.make_async_copy(
            self.block, self.out.at[self.section, self.index], self.local
        )

    def start(self):
        for copy in self.copies():
            copy.start()
        self.stay().start()

    def finish(self):
        for copy in self.copies():
            copy.wait_send()
            copy.wait_recv()
        self.stay().wait()


def gather_scratch(shards):
    count = len(shards)
    return [
        pltpu.SemaphoreType.DMA((count, 10)),
        pltpu.SemaphoreType.DMA((count, 8)),
        pltpu.SemaphoreType.DMA((2, count)),
    ] + [pltpu.VMEM(shard.shape, shard.dtype) for shard in shards]


def gather_shapes(shards):
    return [jax.ShapeDtypeStruct((4,) + shard.shape, shard.dtype) for shard in shards]


def split_shards(shards):
    return [shard.reshape(2, -1, shard.shape[-1]) for shard in shards]


def join_shards(outs):
    return tuple(out.reshape(-1, out.shape[-1]) for out in outs)


class Reduce:
    base = 5

    def __init__(self, line, alone, layer, items, ranges, out, scratch):
        self.line, self.alone, self.layer, self.out = line, alone, layer, out
        self.items, self.ranges = items, ranges
        (
            self.own,
            self.twin,
            self.near_corner,
            self.far_corner,
            self.near,
            self.far,
            self.outer,
            self.inner,
            self.partial,
            self.total,
            self.send,
            self.recv,
            self.local,
            self.done,
        ) = scratch
        self.place()

    def place(self):
        self.section = lax.axis_index("section")
        self.index = lax.axis_index("fsdp")
        self.z = lax.axis_index("ctx")
        self.count = self.total.shape[0]
        self.sibling = {"section": 1 - self.section}
        self.x = {"fsdp": self.index ^ 1}
        self.y = {"fsdp": self.index ^ 2}
        self.is_inner = (self.z == 1) | (self.z == 2)
        self.end = {"ctx": jnp.where(self.z == 1, 0, 3)}
        self.toward = {"ctx": jnp.where(self.z == 0, 1, 2)}
        self.opposite = {"ctx": 3 - self.z}

    def chunks(self):
        k = 0
        for item, some in zip(self.items, self.ranges):
            rows, columns = item.shape[2:]
            depth = self.own.shape[2]
            places = [
                (pl.ds(row, depth), pl.ds(column, CHUNK))
                for row in range(0, rows, depth)
                for column in range(0, columns, CHUNK)
            ]
            for place in places[some]:
                yield k, item, *place
                k += 1

    def copy(self, k, slot, source, target, device):
        return remote(source, target, self.send.at[slot, k], self.recv.at[slot, k], device)

    def swap(self, k):
        return self.copy(k, 0, self.twin.at[k], self.twin.at[k], self.sibling)

    def load(self, k):
        return pltpu.make_async_copy(self.own.at[k], self.own.at[k], self.local.at[k])

    def corner(self, k, near):
        half = self.own.shape[2] // 2
        rows = pl.ds(0, half) if near else pl.ds(half, half)
        source = self.own.at[k, self.index ^ 3, rows]
        target = (self.near_corner if near else self.far_corner).at[k]
        return self.copy(k, 1 if near else 2, source, target, self.x if near else self.y)

    def side(self, k, near):
        source = self.own.at[k, self.index ^ (1 if near else 2)]
        target = (self.near if near else self.far).at[k]
        return self.copy(k, 3 if near else 4, source, target, self.x if near else self.y)

    def inward(self, k):
        return self.copy(k, self.base + 0, self.partial.at[k], self.outer.at[k], self.toward)

    def across(self, k):
        return self.copy(k, self.base + 1, self.partial.at[k], self.inner.at[k], self.opposite)

    def outward(self, k):
        return self.copy(k, self.base + 2, self.total.at[k], self.total.at[k], self.end)

    def start(self):
        for k, item, rows, columns in self.chunks():
            theirs = item.at[:, 1 - self.section, rows, columns]
            mine = item.at[:, self.section, rows, columns]
            self.copy(k, 0, theirs, self.twin.at[k], self.sibling).start()
            pltpu.make_async_copy(mine, self.own.at[k], self.local.at[k]).start()

    def stage(self, number, k):
        half = self.total.shape[1] // 2
        near, far = self.index ^ 1, self.index ^ 2
        if number == 0:
            self.load(k).wait()
            self.swap(k).wait_recv()
            for j in range(4):
                self.own[k, j] = self.own[k, j] + self.twin[k, j]
            self.corner(k, True).start()
            self.corner(k, False).start()
        elif number == 1:
            self.corner(k, True).wait_recv()
            self.corner(k, False).wait_recv()
            self.own[k, far, :half] = self.own[k, far, :half] + self.near_corner[k]
            self.own[k, near, half:] = self.own[k, near, half:] + self.far_corner[k]
            self.side(k, True).start()
            self.side(k, False).start()
        elif number == 2:
            self.side(k, True).wait_recv()
            self.side(k, False).wait_recv()
            summed = (
                self.own[k, self.index].astype(f32)
                + self.near[k].astype(f32)
                + self.far[k].astype(f32)
            ).astype(bf16)
            if not self.line:
                self.total[k] = summed
                return
            self.partial[k] = summed

            @pl.when(jnp.logical_not(self.is_inner))
            def _():
                self.inward(k).start()
        elif number == 3 and self.line:

            @pl.when(self.is_inner)
            def _():
                self.inward(k).wait_recv()
                self.partial[k] = self.partial[k] + self.outer[k]
                self.across(k).start()
        elif number == 4 and self.line:

            @pl.when(self.is_inner)
            def _():
                self.across(k).wait_recv()
                self.total[k] = self.partial[k] + self.inner[k]
                self.outward(k).start()

    def step(self, t, lags):
        for number, lag in enumerate(lags):
            k = t - lag

            @pl.when((k >= 0) & (k < self.count))
            def _():
                self.stage(number, k)

    def finish(self, k):
        self.swap(k).wait_send()
        for near in (True, False):
            self.corner(k, near).wait_send()
            self.side(k, near).wait_send()
        if self.line:
            self.line_sent(k)

    def line_sent(self, k):
        @pl.when(self.is_inner)
        def _():
            self.across(k).wait_send()
            self.outward(k).wait_send()

        @pl.when(jnp.logical_not(self.is_inner))
        def _():
            self.inward(k).wait_send()
            self.outward(k).wait_recv()

    def write(self):
        return pltpu.make_async_copy(self.total, self.out.at[self.section], self.local.at[0])

    def give(self):
        place = self.out.at[1 - self.layer]
        return remote(self.total, place, self.done.at[0], self.done.at[1], self.sibling)

    def close(self):
        if self.alone:
            copy = pltpu.make_async_copy(self.total, self.out, self.local.at[0])
            copy.start()
            copy.wait()
            return
        self.write().start()

        @pl.when(self.section != self.layer)
        def _():
            self.give().start()
            self.give().wait_send()

        @pl.when(self.section == self.layer)
        def _():
            self.give().wait_recv()

        self.write().wait()


class Line(Reduce):
    base = 0

    def __init__(self, layer, source, out, scratch):
        self.line, self.alone, self.layer, self.source, self.out = True, False, layer, source, out
        (
            self.partial,
            self.outer,
            self.inner,
            self.total,
            self.send,
            self.recv,
            self.local,
            self.done,
        ) = scratch
        self.place()

    def load(self, k):
        return pltpu.make_async_copy(self.source.at[k], self.partial.at[k], self.local.at[k])

    def start(self):
        for k in range(self.count):
            self.load(k).start()

    def stage(self, number, k):
        if number == 0:
            self.load(k).wait()

            @pl.when(jnp.logical_not(self.is_inner))
            def _():
                self.inward(k).start()
        else:
            super().stage(number + 2, k)

    def finish(self, k):
        self.line_sent(k)


LAGS = (0, 1, 3, 4, 5)
CARRIED_LAGS = (0, 2, 4, 6, 8)


class ReducePart:
    lags = CARRIED_LAGS

    def __init__(self, layer, grads, line, alone=False):
        self.layer, self.line, self.alone = layer, line and not alone, line and alone
        self.ins = [grad.reshape(4, 2, -1, grad.shape[-1]) for grad, _ in grads]
        self.ranges = [slice(*some) for _, some in grads]
        self.chunks = sum(stop - start for _, (start, stop) in grads)
        depth = DEPTH
        whole = (self.chunks, depth, CHUNK)
        self.outs = [jax.ShapeDtypeStruct(whole if self.alone else (2,) + whole, bf16)]
        self.scratch = reduce_scratch(self.chunks, depth, self.line)

    def groups(self):
        return [column_group(), [(0, 0, 1), (0, 0, 2)]]

    def bind(self, ins, outs, scratch):
        return Reduce(self.line, self.alone, self.layer, ins, self.ranges, outs[0], scratch)

    def begin(self, reduce):
        reduce.start()

    def tick(self, reduce, step, steps):
        lags = LAGS[: len(self.lags)] if steps == 1 else self.lags
        share = -(-(self.chunks + lags[-1]) // steps)

        def advance(t, _):
            reduce.step(step * share + t, lags)
            return 0

        lax.fori_loop(0, share, advance, 0)

    def end(self, reduce):
        def finish(k, _):
            reduce.finish(k)
            return 0

        lax.fori_loop(0, reduce.count, finish, 0)
        reduce.close()

    def result(self, outs):
        return outs[0] if self.line or self.alone else lax.psum(outs[0], "ctx")


class LinePart(ReducePart):
    lags = (0, 2, 4)

    def __init__(self, layer, source):
        self.layer, self.line = layer, True
        self.chunks = source.shape[0]
        self.ins = [source]
        self.outs = [jax.ShapeDtypeStruct((2,) + source.shape, bf16)]
        self.scratch = [pltpu.VMEM(source.shape, bf16)] * 4 + [
            pltpu.SemaphoreType.DMA((3, self.chunks)),
            pltpu.SemaphoreType.DMA((3, self.chunks)),
            pltpu.SemaphoreType.DMA((self.chunks,)),
            pltpu.SemaphoreType.DMA((2,)),
        ]

    def groups(self):
        return [column_group()]

    def bind(self, ins, outs, scratch):
        return Line(self.layer, ins[0], outs[0], scratch)


class DeliverPart:
    def __init__(self, layer, rows, stored):
        seats = Seats(stored[0])
        self.layer = layer
        self.ins = [rows.reshape(seats.per, -1, rows.shape[-1])]
        self.outs = [jax.ShapeDtypeStruct(stored, bf16)]
        self.scratch = Deliver.scratch(stored[0], seats.per, seats.places)

    def groups(self):
        return [column_group()]

    def bind(self, ins, outs, scratch):
        return Deliver(self.layer, ins[0], outs[0], *scratch)

    def begin(self, deliver):
        deliver.start()

    def tick(self, deliver, step, steps):
        pass

    def end(self, deliver):
        deliver.finish()

    def result(self, outs):
        return outs[0]


class BringPart:
    def __init__(self, rows):
        seats = Seats(rows.shape[0])
        _, depth, width = rows.shape
        self.ins = [rows]
        self.outs = [jax.ShapeDtypeStruct((seats.per, depth * seats.places, width), bf16)]
        self.scratch = Bring.scratch([rows], seats.per, seats.places)

    def groups(self):
        return [line_group()]

    def bind(self, ins, outs, scratch):
        return Bring(ins, outs, *scratch)

    def begin(self, bring):
        bring.clear()
        bring.start(0)

    def tick(self, bring, step, steps):
        pass

    def end(self, bring):
        bring.finish(0)

    def result(self, outs):
        return outs[0]


class SpreadPart:
    def __init__(self, block):
        self.ins = [block]
        self.outs = [jax.ShapeDtypeStruct((2, 4) + block.shape, bf16)]
        self.scratch = Spread.scratch()

    def groups(self):
        return [chip_group(), corner_group()]

    def bind(self, ins, outs, scratch):
        return Spread(ins[0], outs[0], *scratch)

    def begin(self, spread):
        spread.start()

    def tick(self, spread, step, steps):
        pass

    def end(self, spread):
        spread.finish()

    def result(self, outs):
        return outs[0]


class GatherPart:
    def __init__(self, layer, shards):
        self.layer = layer
        self.ins = split_shards(shards)
        self.outs = gather_shapes(self.ins)
        self.scratch = gather_scratch(self.ins)

    def groups(self):
        return [chip_group()]

    def bind(self, ins, outs, scratch):
        return Gather(self.layer, ins, outs, *scratch)

    def begin(self, gather):
        gather.start()

    def tick(self, gather, step, steps):
        count = len(self.ins)
        if steps == 1:
            for m in range(count):
                gather.middle(m)
                if m > 0:
                    gather.last(m - 1)
            gather.last(count - 1)
            return
        for m in range(count):

            @pl.when(step == steps - 1 - count + m)
            def _():
                gather.middle(m)

            @pl.when(step == steps - 1)
            def _():
                gather.last(m)

    def end(self, gather):
        for m in range(len(self.ins)):
            gather.finish(m)

    def result(self, outs):
        return join_shards(outs)


class Carry:
    def __init__(self, collective, *parts):
        self.collective, self.parts = collective, parts
        self.ins = [array for part in parts for array in part.ins]
        self.outs = [shape for part in parts for shape in part.outs]
        self.scratch = [shape for part in parts for shape in part.scratch]

    def params(self, limit=60):
        return pltpu.CompilerParams(
            collective_id=self.collective,
            has_side_effects=self.collective is not None,
            vmem_limit_bytes=limit * 1024 * 1024,
        )

    def kernel(self, body, ins, outs, scratch, grid):
        if not self.parts:
            return body
        steps = 1
        for size in grid:
            steps *= size

        def run(*refs):
            pieces, at = [], 0
            for size in (ins, len(self.ins), outs, len(self.outs), scratch, len(self.scratch)):
                pieces.append(refs[at : at + size])
                at += size
            bound, at = [], [0, 0, 0]
            for part in self.parts:
                sizes = [len(part.ins), len(part.outs), len(part.scratch)]
                taken = [
                    pieces[2 * i + 1][at[i] : at[i] + sizes[i]] for i in range(3)
                ]
                at = [at[i] + sizes[i] for i in range(3)]
                bound.append((part, part.bind(*taken)))
            step = 0
            for axis in range(len(grid)):
                step = step * grid[axis] + pl.program_id(axis)

            def begin():
                greet([group for part in self.parts for group in part.groups()])
                for part, state in bound:
                    part.begin(state)

            def end():
                for part, state in bound:
                    part.end(state)

            if steps == 1:
                begin()
            else:
                pl.when(step == 0)(begin)
            body(*pieces[0], *pieces[2], *pieces[4])
            for part, state in bound:
                part.tick(state, step, steps)
            if steps == 1:
                end()
            else:
                pl.when(step == steps - 1)(end)

        return run

    def alone(self):
        outs = pl.pallas_call(
            self.kernel(lambda: None, 0, 0, 0, ()),
            in_specs=[ANY] * len(self.ins),
            out_specs=[ANY] * len(self.outs),
            out_shape=self.outs,
            scratch_shapes=self.scratch,
            compiler_params=self.params(),
        )(*self.ins)
        return self.result(outs)

    def result(self, outs):
        results, at = [], 0
        for part in self.parts:
            results.append(part.result(outs[at : at + len(part.outs)]))
            at += len(part.outs)
        return results


def reduce_scratch(count, depth, line):
    block = (count, depth, CHUNK)
    half = (count, depth // 2, CHUNK)
    return (
        [pltpu.VMEM((count, 4, depth, CHUNK), bf16)] * 2
        + [pltpu.VMEM(half, bf16)] * 2
        + [pltpu.VMEM(block, bf16)] * 2
        + [pltpu.VMEM(block if line else (1, 16, 128), bf16)] * 3
        + [pltpu.VMEM(block, bf16)]
        + [
            pltpu.SemaphoreType.DMA((8, count)),
            pltpu.SemaphoreType.DMA((8, count)),
            pltpu.SemaphoreType.DMA((count,)),
            pltpu.SemaphoreType.DMA((2,)),
        ]
    )


def unchunk(blocks, shapes):
    depth = blocks.shape[-2]
    parts, k = [], 0
    for rows, columns in shapes:
        high, wide = rows // depth, columns // CHUNK
        part = blocks[..., k : k + high * wide, :, :]
        part = part.reshape(blocks.shape[:-3] + (high, wide) + blocks.shape[-2:])
        part = jnp.concatenate([part[..., j, :, :] for j in range(wide)], axis=-1)
        parts.append(part.reshape(blocks.shape[:-3] + (rows, columns)))
        k += high * wide
    return parts


def shards(
    block_input,
    positions,
    cotangent,
    w_qkv,
    w_proj,
    w_fc,
    w_out,
    ln_gain,
    ln_bias,
    attn_bias,
    out_bias,
    fc_bias,
):
    section = lax.axis_index("section")
    first = section == 0
    ctxs = lax.axis_size("ctx")
    fsdps = lax.axis_size("fsdp")
    local_seqs, local_rows, width = block_input.shape
    stored = block_input.shape
    length = positions.shape[1]
    seats = Seats(local_seqs)
    per = seats.per
    shard_width = ln_gain.shape[2]

    pack = jnp.concatenate(
        [ln_gain[0], ln_bias[0], attn_bias[0], out_bias[0], fc_bias[0].reshape(-1, shard_width)]
    )
    pack = jnp.pad(pack, ((0, 16 - pack.shape[0]), (0, 256 - shard_width)))

    def unpack(packed):
        packed = packed[:, :12, :shard_width]
        vectors = jnp.transpose(packed[:, :8], (1, 0, 2)).reshape(8, -1).astype(f32)
        fc = packed[:, 8:].reshape(-1).astype(f32)
        return vectors[0:2], vectors[2:4], vectors[4:6], vectors[6:8], fc

    shards_own = [matrix[0] for matrix in (w_qkv, w_proj, w_fc, w_out)]
    block_rows, packs, first_weights = Carry(
        0, BringPart(block_input), SpreadPart(pack), GatherPart(0, shards_own[:2])
    ).alone()
    smalls = [unpack(packs[layer]) for layer in range(2)]

    places = jnp.stack(
        [
            lax.dynamic_index_in_dim(
                positions, seats.of(section, lax.axis_index("ctx") * per + p)[1], 0, keepdims=False
            )
            for p in range(per)
        ]
    )
    order = (
        lax.broadcasted_iota(jnp.int32, (per, length, length), 1) == places[:, None, :]
    ).astype(bf16)
    order_back = (
        lax.broadcasted_iota(jnp.int32, (per, length, length), 2) == places[:, :, None]
    ).astype(bf16)

    def to_sorted(rows):
        return (
            jnp.einsum("bpt,btd->bpd", order, rows, preferred_element_type=f32)
            .astype(bf16)
            .reshape(per * length, width)
        )

    def to_stored(rows):
        return jnp.einsum(
            "btp,bpd->btd", order_back, rows.reshape(per, length, width), preferred_element_type=f32
        ).astype(bf16)

    start = to_sorted(block_rows)
    line = ctxs == 4

    def attend_zero(project):
        carry = Carry(1, GatherPart(0, shards_own[2:]), BringPart(cotangent))
        return attend_forward(project, length, carry)

    middle, kept_zero, weights_zero, attended, (early,) = layer_forward(
        (first_weights[0], lambda attended: (*first_weights, *attended[0])),
        smalls[0],
        start,
        attend_zero,
        Carry(7, GatherPart(1, shards_own[:2])),
    )
    grad_final = to_sorted(attended[1])

    def attend_one(project):
        carry = Carry(4, GatherPart(1, shards_own[2:]), DeliverPart(0, to_stored(middle), stored))
        return attend_forward(project, length, carry)

    final, kept_one, weights_one, (_, out_zero), _ = layer_forward(
        (early[0], lambda attended: (*early, *attended[0])), smalls[1], middle, attend_one, Carry(None)
    )
    outs = [out_zero]
    sums = {}
    fc_chunks = w_fc.shape[2] // CHUNK
    qkv_chunks = w_qkv.shape[2] // CHUNK
    proj_chunks = w_proj.shape[2] // CHUNK
    out_chunks = w_out.shape[1] // (2 * DEPTH)

    def lines(*waiting):
        names = [name for name in waiting if name in sums]
        return names if line else [], [LinePart(l, sums[l, n]) for l, n in names] if line else []

    def pull_one(kept, grads, _):
        chosen = [(grads[2], (0, out_chunks)), (grads[1], (0, 1))]
        carry = Carry(
            5, ReducePart(1, chosen, line, True), DeliverPart(1, to_stored(final), stored)
        )
        pulled, (sums[1, "a"], out_one) = attend_back(*kept, length, carry)
        outs.append(out_one)
        return pulled

    grad_middle, grads_one, small_one = layer_back(
        weights_one,
        smalls[1],
        kept_one,
        grad_final,
        Carry(None),
        pull_one,
        lambda grad: (Carry(None), lambda carried: None),
    )
    names, parts = lines((1, "a"))
    chosen = [
        (grads_one[2], (1, fc_chunks)),
        (grads_one[0], (0, qkv_chunks)),
        (grads_one[1], (0, proj_chunks)),
    ]
    carry = Carry(
        2,
        ReducePart(1, chosen, line, True),
        *parts,
        DeliverPart(1, to_stored(grad_middle), stored),
    )

    def pull_zero(kept, grads, carried):
        sums[1, "b"], *summed, sums["in"] = carried
        sums.update(zip(names, summed))
        later, parts = lines((1, "b"))
        chosen = [(grads[2], (0, out_chunks)), (grads[0], (0, proj_chunks))]
        pulled, (sums[0, "a"], *summed) = attend_back(
            *kept, length, Carry(6, ReducePart(0, chosen, line, True), *parts)
        )
        sums.update(zip(later, summed))
        return pulled

    def last_zero(grad_w_fc):
        later, parts = lines((0, "a"))

        def done(carried):
            sums[0, "b"], *summed = carried
            sums.update(zip(later, summed))

        return Carry(8, ReducePart(0, [(grad_w_fc, (0, fc_chunks))], line, True), *parts), done

    grad_start, grads_zero, small_zero = layer_back(
        weights_zero, smalls[0], kept_zero, grad_middle, carry, pull_zero, last_zero
    )
    in_one = sums["in"]

    def repack(small):
        vectors, fc = small
        vectors = jnp.transpose(vectors.reshape(8, fsdps, shard_width), (1, 0, 2))
        packed = jnp.concatenate([vectors, fc.reshape(fsdps, -1, shard_width)], axis=1)
        depth = w_qkv.shape[1] // 2
        return jnp.pad(
            packed.astype(bf16),
            ((0, 0), (0, depth - packed.shape[1]), (0, CHUNK - packed.shape[2])),
        )[:, None]

    pack = jnp.concatenate([repack(small_zero), repack(small_one)], axis=1)
    pack = pack.reshape(-1, CHUNK)
    names, parts = lines((0, "b"))
    chosen = [(grads_zero[0], (0, qkv_chunks)), (pack, (0, 1))]
    sums[0, "c"], *summed, in_zero = Carry(
        3,
        ReducePart(0, chosen, line),
        *parts,
        DeliverPart(0, to_stored(grad_start), stored),
    ).alone()
    sums.update(zip(names, summed))
    packed = jnp.where(first, sums[0, "c"][0, -1], sums[0, "c"][1, -1])
    packed = packed[:12, :shard_width].astype(f32)
    section_out = jnp.where(first, outs[0], outs[1])[None]
    section_in_grad = jnp.where(first, in_zero, in_one)[None]
    one = jnp.concatenate([sums[1, "a"], sums[1, "b"]], axis=1)
    edge = out_chunks + fc_chunks
    whole = [
        (sums[0, "c"][:, :qkv_chunks], one[:, edge : edge + qkv_chunks], w_qkv),
        (sums[0, "a"][:, out_chunks:], one[:, edge + qkv_chunks :], w_proj),
        (sums[0, "b"], one[:, out_chunks:edge], w_fc),
        (sums[0, "a"][:, :out_chunks], one[:, :out_chunks], w_out),
    ]
    big = []
    for low, high, matrix in whole:
        shape = (matrix.shape[1] // 2, matrix.shape[2])
        (block,) = unchunk(jnp.where(first, low, high), [shape])
        big.append(block.reshape(-1, block.shape[-1]).astype(f32)[None])

    return (
        section_out,
        section_in_grad,
        *big,
        packed[None, 0:8:4],
        packed[None, 1:8:4],
        packed[None, 2:4],
        packed[None, 6:8],
        packed[8:].reshape(1, -1),
    )


def solution(mesh):
    matrix = P("section", "fsdp", None)
    vectors = P("section", None, "fsdp")
    rows_out = P("section", "fsdp", "ctx", None)
    return jax.shard_map(
        shards,
        mesh=mesh,
        in_specs=(
            P("fsdp", "ctx", None),
            P("fsdp", None),
            P("fsdp", "ctx", None),
            *([matrix] * 4),
            *([vectors] * 4),
            P("section", "fsdp"),
        ),
        out_specs=(
            rows_out,
            rows_out,
            *([matrix] * 4),
            *([vectors] * 4),
            P("section", "fsdp"),
        ),
        check_vma=False,
    )
```

```python
import functools

import jax
import jax.numpy as jnp
from jax import lax
from jax.experimental import pallas as pl
from jax.experimental.pallas import tpu as pltpu
from jax.sharding import PartitionSpec as P

H = 12
HD = 64
PAIR = 2 * HD
SCALE = HD**-0.5

masked_score = -1e30
norm_eps = 1e-05
f32 = jnp.float32
bf16 = jnp.bfloat16


def layer_norm(hidden, gain, offset):
    center = hidden - jnp.mean(hidden, axis=-1, keepdims=True)
    spread = jnp.mean(center * center, axis=-1, keepdims=True)
    return center * lax.rsqrt(spread + norm_eps) * gain + offset


def gelu_tanh(inputs):
    return jax.nn.gelu(inputs, approximate=True)


def mm(left, right):
    return lax.dot_general(left, right, (((1,), (0,)), ((), ())), preferred_element_type=f32)


def mm_nt(left, right):
    return lax.dot_general(left, right, (((1,), (1,)), ((), ())), preferred_element_type=f32)


def mm_tn(left, right):
    return lax.dot_general(left, right, (((0,), (0,)), ((), ())), preferred_element_type=f32)


def masked_scores(keys, queries, start, block):
    scores = mm_nt(keys, queries)
    down = lax.broadcasted_iota(jnp.int32, (block, block), 0)
    across = lax.broadcasted_iota(jnp.int32, (block, block), 1)
    corner = jnp.where(across >= down, scores[start:], masked_score)
    if start == 0:
        return corner
    return jnp.concatenate([scores[:start], corner], axis=0)


def attend_kernel(block, q_ref, k_ref, v_ref, o_ref, log_ref):
    length = q_ref.shape[0]
    for head in range(2):
        cols = slice(head * HD, (head + 1) * HD)
        for start in range(0, length, block):
            end = start + block
            queries = (q_ref[start:end, cols].astype(f32) * SCALE).astype(bf16)
            scores = masked_scores(k_ref[:end, cols], queries, start, block)
            top = jnp.max(scores, axis=0, keepdims=True)
            weights = jnp.exp(scores - top)
            total = jnp.sum(weights, axis=0, keepdims=True)
            mixed = mm_tn(v_ref[:end, cols], weights.astype(bf16)) / total
            o_ref[start:end, cols] = mixed.T.astype(bf16)
            log_ref[0, 0, head : head + 1, start:end] = top + jnp.log(total)


def attend_back_kernel(
    block, q_ref, k_ref, v_ref, do_ref, o_ref, log_ref, dq_ref, dk_ref, dv_ref, dk_sum, dv_sum
):
    length = q_ref.shape[0]
    for head in range(2):
        cols = slice(head * HD, (head + 1) * HD)
        for start in range(length - block, -1, -block):
            end = start + block
            queries = (q_ref[start:end, cols].astype(f32) * SCALE).astype(bf16)
            grads = do_ref[start:end, cols]
            product = grads.astype(f32) * o_ref[start:end, cols].astype(f32)
            delta = jnp.sum(product.T, axis=0, keepdims=True)
            keys = k_ref[:end, cols]
            scores = masked_scores(keys, queries, start, block)
            probs = jnp.exp(scores - log_ref[0, 0, head : head + 1, start:end])
            grad_probs = mm_nt(v_ref[:end, cols], grads)
            grad_scores = (probs * (grad_probs - delta)).astype(bf16)
            dv = mm(probs.astype(bf16), grads)
            dk = mm(grad_scores, queries)
            if end == length:
                dv_sum[:end, cols] = dv
                dk_sum[:end, cols] = dk
            else:
                dv_sum[:end, cols] += dv
                dk_sum[:end, cols] += dk
            dq = mm_tn(keys, grad_scores) * SCALE
            dq_ref[start:end, cols] = dq.T.astype(bf16)
    dk_ref[...] = dk_sum[...].astype(bf16)
    dv_ref[...] = dv_sum[...].astype(bf16)


def query_block(length):
    return 256 if length % 256 == 0 else length


def head_spec(length, offset):
    return pl.BlockSpec((length, PAIR), lambda b, h: (b, offset + h))


def log_spec(length):
    return pl.BlockSpec((1, 1, 2, length), lambda b, h: (b, h, 0, 0))


def attend_forward(project, length, carry):
    rows = project.shape[0]
    count = rows // length
    pairs = H // 2
    grid = (count, pairs)
    body = functools.partial(attend_kernel, query_block(length))
    outs = pl.pallas_call(
        carry.kernel(body, 3, 2, 0, grid),
        grid=grid,
        in_specs=[head_spec(length, 0), head_spec(length, pairs), head_spec(length, 2 * pairs)]
        + [ANY] * len(carry.ins),
        out_specs=[head_spec(length, 0), log_spec(length)] + [ANY] * len(carry.outs),
        out_shape=[
            jax.ShapeDtypeStruct((rows, H * HD), bf16),
            jax.ShapeDtypeStruct((count, pairs, 2, length), f32),
        ]
        + carry.outs,
        scratch_shapes=carry.scratch,
        compiler_params=carry.params(),
        cost_estimate=pl.CostEstimate(
            flops=8 * rows * length * H * HD,
            bytes_accessed=8 * rows * H * HD,
            transcendentals=rows * length * H // 2,
        ),
    )(project, project, project, *carry.ins)
    return outs[:2], carry.result(outs[2:])


def attend_back(project, grad_mixed, mixed, log_total, length, carry):
    rows = project.shape[0]
    count = rows // length
    pairs = H // 2
    grid = (count, pairs)
    body = functools.partial(attend_back_kernel, query_block(length))
    outs = pl.pallas_call(
        carry.kernel(body, 6, 3, 2, grid),
        grid=grid,
        in_specs=[
            head_spec(length, 0),
            head_spec(length, pairs),
            head_spec(length, 2 * pairs),
            head_spec(length, 0),
            head_spec(length, 0),
            log_spec(length),
        ]
        + [ANY] * len(carry.ins),
        out_specs=[head_spec(length, 0)] * 3 + [ANY] * len(carry.outs),
        out_shape=[jax.ShapeDtypeStruct((rows, H * HD), bf16)] * 3 + carry.outs,
        scratch_shapes=[pltpu.VMEM((length, PAIR), f32)] * 2 + carry.scratch,
        compiler_params=carry.params(),
        cost_estimate=pl.CostEstimate(
            flops=20 * rows * length * H * HD,
            bytes_accessed=16 * rows * H * HD,
            transcendentals=rows * length * H // 2,
        ),
    )(project, project, project, grad_mixed, mixed, log_total, *carry.ins)
    return outs[:3], carry.result(outs[3:])


TILE = 512
BLOCK = 256
ROOT = 0.7978845608028654
CUBE = 0.044715


def norm_back(hidden, grad, gain):
    center = hidden - jnp.mean(hidden, axis=-1, keepdims=True)
    scale = lax.rsqrt(jnp.mean(center * center, axis=-1, keepdims=True) + norm_eps)
    unit = center * scale
    scaled = grad * gain
    shift = jnp.mean(scaled, axis=-1, keepdims=True)
    tilt = jnp.mean(scaled * unit, axis=-1, keepdims=True)
    return unit, (scaled - shift - unit * tilt) * scale


def whole_spec(shape):
    return pl.BlockSpec(shape, lambda *at: (0,) * len(shape), pipeline_mode=pl.Buffered(1))


def mlp_kernel(
    hidden_ref,
    mixed_ref,
    w_proj_ref,
    w_fc_ref,
    w_out_ref,
    vectors_ref,
    fc_bias_ref,
    after_ref,
    normed_ref,
    inner_ref,
    result_ref,
    total,
):
    step = pl.program_id(0)
    rows = hidden_ref.shape[0]
    blocks = [slice(start, start + BLOCK) for start in range(0, rows, BLOCK)]

    @pl.when(step == 0)
    def _():
        for here in blocks:
            after = hidden_ref[here].astype(f32) + mm(mixed_ref[here], w_proj_ref[...])
            after = after + vectors_ref[2:3]
            after_ref[here] = after
            normed_ref[here] = layer_norm(after, vectors_ref[0:1], vectors_ref[1:2]).astype(bf16)
            total[here] = after + vectors_ref[3:4]

    for here in blocks:
        inner = mm(normed_ref[here], w_fc_ref[...]) + fc_bias_ref[...]
        inner_ref[here] = inner
        bend = jnp.tanh(inner * (ROOT + (ROOT * CUBE) * (inner * inner)))
        half = 0.5 * inner
        active = (half + half * bend).astype(bf16)
        total[here] += mm(active, w_out_ref[...])

    @pl.when(step == pl.num_programs(0) - 1)
    def _():
        result_ref[...] = total[...].astype(bf16)


def mlp(weights, smalls, layer_in, mixed, carry):
    _, w_proj, w_fc, w_out = weights
    gains, offsets, _, out_bias, fc_bias = smalls
    rows, width = layer_in.shape
    wide = w_fc.shape[1]
    tile = TILE if wide % TILE == 0 else wide
    grid = (wide // tile,)
    vectors = jnp.stack([gains[1], offsets[1], out_bias[0], out_bias[1]])

    def along(height):
        return pl.BlockSpec((height, tile), lambda i: (0, i))

    outs = pl.pallas_call(
        carry.kernel(mlp_kernel, 7, 4, 1, grid),
        grid=grid,
        in_specs=[
            whole_spec((rows, width)),
            whole_spec((rows, width)),
            whole_spec((width, width)),
            along(width),
            pl.BlockSpec((tile, width), lambda i: (i, 0)),
            whole_spec((4, width)),
            along(1),
        ]
        + [ANY] * len(carry.ins),
        out_specs=[
            whole_spec((rows, width)),
            whole_spec((rows, width)),
            along(rows),
            whole_spec((rows, width)),
        ]
        + [ANY] * len(carry.outs),
        out_shape=[
            jax.ShapeDtypeStruct((rows, width), f32),
            jax.ShapeDtypeStruct((rows, width), bf16),
            jax.ShapeDtypeStruct((rows, wide), f32),
            jax.ShapeDtypeStruct((rows, width), bf16),
        ]
        + carry.outs,
        scratch_shapes=[pltpu.VMEM((rows, width), f32)] + carry.scratch,
        compiler_params=carry.params(),
        cost_estimate=pl.CostEstimate(
            flops=4 * rows * width * wide + 2 * rows * width * width,
            bytes_accessed=4 * rows * wide + 4 * wide * width + 12 * rows * width,
            transcendentals=rows * wide,
        ),
    )(layer_in, mixed, w_proj, w_fc, w_out, vectors, fc_bias[None], *carry.ins)
    return outs[:4], carry.result(outs[4:])


def qkv_back_kernel(
    dq_ref, dk_ref, dv_ref, normed_ref, w_ref, hidden_ref, dafter_ref, gain_ref,
    dw_ref, dx_ref, sums_ref,
):
    rows, width = dq_ref.shape
    parts = (dq_ref, dk_ref, dv_ref)
    for i, part in enumerate(parts):
        columns = slice(i * width, (i + 1) * width)
        dw_ref[:, columns] = mm_tn(normed_ref[...], part[...]).astype(bf16)
    sums_ref[...] = jnp.zeros(sums_ref.shape, f32)
    for start in range(0, rows, BLOCK):
        here = slice(start, start + BLOCK)
        grad = jnp.zeros((BLOCK, width), f32)
        for i, part in enumerate(parts):
            grad = grad + mm_nt(part[here], w_ref[:, i * width : (i + 1) * width])
        unit, back = norm_back(hidden_ref[here].astype(f32), grad, gain_ref[...])
        dx_ref[here] = (dafter_ref[here] + back).astype(bf16)
        sums_ref[0:1] += jnp.sum(grad * unit, axis=0, keepdims=True)
        sums_ref[1:2] += jnp.sum(grad, axis=0, keepdims=True)
        sums_ref[2:3] += jnp.sum(dq_ref[here].astype(f32), axis=0, keepdims=True)
        sums_ref[3:4] += jnp.sum(dv_ref[here].astype(f32), axis=0, keepdims=True)


def qkv_back(w_qkv, gain, kept, grads, grad_after):
    layer_in, normed = kept[:2]
    rows, width = layer_in.shape
    return pl.pallas_call(
        qkv_back_kernel,
        out_shape=[
            jax.ShapeDtypeStruct((width, 3 * width), bf16),
            jax.ShapeDtypeStruct((rows, width), bf16),
            jax.ShapeDtypeStruct((8, width), f32),
        ],
        compiler_params=pltpu.CompilerParams(vmem_limit_bytes=60 * 1024 * 1024),
        cost_estimate=pl.CostEstimate(
            flops=12 * rows * width * width,
            bytes_accessed=18 * rows * width + 12 * width * width,
            transcendentals=0,
        ),
    )(*grads, normed, w_qkv, layer_in, grad_after, gain[None])


def mlp_back_kernel(
    dy_ref,
    normed_ref,
    inner_ref,
    w_fc_ref,
    w_out_ref,
    after_ref,
    mixed_ref,
    w_proj_ref,
    gain_ref,
    dw_out_ref,
    dw_fc_ref,
    dfc_ref,
    dw_proj_ref,
    dmixed_ref,
    dafter_ref,
    sums_ref,
    total,
    active,
    dinner,
    dbranch,
):
    step = pl.program_id(0)
    rows = dy_ref.shape[0]

    @pl.when(step == 0)
    def _():
        total[...] = jnp.zeros(total.shape, f32)

    for start in range(0, rows, BLOCK):
        here = slice(start, start + BLOCK)
        inner = inner_ref[here]
        square = inner * inner
        bend = jnp.tanh(inner * (ROOT + (ROOT * CUBE) * square))
        half = 0.5 * (1.0 + bend)
        active[here] = (inner * half).astype(bf16)
        slope = half + (0.5 * ROOT) * inner * (1.0 - bend * bend) * (1.0 + (3.0 * CUBE) * square)
        grad = (mm_nt(dy_ref[here], w_out_ref[...]) * slope).astype(bf16)
        dinner[here] = grad
        total[here] += mm_nt(grad, w_fc_ref[...])
    dw_out_ref[...] = mm_tn(active[...], dy_ref[...]).astype(bf16)
    dw_fc_ref[...] = mm_tn(normed_ref[...], dinner[...]).astype(bf16)
    dfc_ref[...] = jnp.sum(dinner[...].astype(f32), axis=0, keepdims=True)

    @pl.when(step == pl.num_programs(0) - 1)
    def _():
        sums_ref[...] = jnp.zeros(sums_ref.shape, f32)
        for start in range(0, rows, BLOCK):
            here = slice(start, start + BLOCK)
            grad = total[here]
            out = dy_ref[here].astype(f32)
            unit, back = norm_back(after_ref[here], grad, gain_ref[...])
            after = out + back
            dafter_ref[here] = after
            branch = after.astype(bf16)
            dbranch[here] = branch
            sums_ref[0:1] += jnp.sum(grad * unit, axis=0, keepdims=True)
            sums_ref[1:2] += jnp.sum(grad, axis=0, keepdims=True)
            sums_ref[2:3] += jnp.sum(branch.astype(f32), axis=0, keepdims=True)
            sums_ref[3:4] += jnp.sum(out, axis=0, keepdims=True)
            dmixed_ref[here] = mm_nt(branch, w_proj_ref[...]).astype(bf16)
        dw_proj_ref[...] = mm_tn(mixed_ref[...], dbranch[...]).astype(bf16)


def mlp_back(weights, gain, kept, grad_out, carry):
    _, w_proj, w_fc, w_out = weights
    _, _, _, mixed, _, after, normed_two, inner = kept
    rows, width = grad_out.shape
    wide = inner.shape[1]
    tile = TILE if wide % TILE == 0 else wide
    grid = (wide // tile,)
    once = pl.Buffered(1)

    def whole(shape):
        return pl.BlockSpec(shape, lambda i: (0, 0), pipeline_mode=once)

    across = pl.BlockSpec((tile, width), lambda i: (i, 0))

    def along(height):
        return pl.BlockSpec((height, tile), lambda i: (0, i))

    outs = pl.pallas_call(
        carry.kernel(mlp_back_kernel, 9, 7, 4, grid),
        grid=grid,
        in_specs=[
            whole((rows, width)),
            whole((rows, width)),
            along(rows),
            along(width),
            across,
            whole((rows, width)),
            whole((rows, width)),
            whole((width, width)),
            whole((1, width)),
        ]
        + [ANY] * len(carry.ins),
        out_specs=[
            across,
            along(width),
            along(1),
            whole((width, width)),
            whole((rows, width)),
            whole((rows, width)),
            whole((8, width)),
        ]
        + [ANY] * len(carry.outs),
        out_shape=[
            jax.ShapeDtypeStruct((wide, width), bf16),
            jax.ShapeDtypeStruct((width, wide), bf16),
            jax.ShapeDtypeStruct((1, wide), f32),
            jax.ShapeDtypeStruct((width, width), bf16),
            jax.ShapeDtypeStruct((rows, width), bf16),
            jax.ShapeDtypeStruct((rows, width), f32),
            jax.ShapeDtypeStruct((8, width), f32),
        ]
        + carry.outs,
        scratch_shapes=[
            pltpu.VMEM((rows, width), f32),
            pltpu.VMEM((rows, tile), bf16),
            pltpu.VMEM((rows, tile), bf16),
            pltpu.VMEM((rows, width), bf16),
        ]
        + carry.scratch,
        compiler_params=carry.params(),
        cost_estimate=pl.CostEstimate(
            flops=8 * rows * width * wide + 4 * rows * width * width,
            bytes_accessed=4 * rows * wide + 8 * wide * width + 16 * rows * width,
            transcendentals=rows * wide,
        ),
    )(
        grad_out,
        normed_two,
        inner,
        w_fc,
        w_out,
        after,
        mixed,
        w_proj,
        gain[None],
        *carry.ins,
    )
    return outs[:7], carry.result(outs[7:])


def layer_forward(weights, smalls, layer_in, attend, carry):
    w_qkv = weights[0]
    gains, offsets, attn_bias, _, _ = smalls
    width = layer_in.shape[-1]
    normed = layer_norm(layer_in.astype(f32), gains[0], offsets[0]).astype(bf16)
    bias = jnp.concatenate([attn_bias[0], jnp.zeros((width,), f32), attn_bias[1]])
    project = (mm(normed, w_qkv) + bias).astype(bf16)
    (mixed, log_total), attended = attend(project)
    if callable(weights[1]):
        weights = weights[1](attended)
    (after, normed_two, inner, result), carried = mlp(weights, smalls, layer_in, mixed, carry)
    kept = (layer_in, normed, project, mixed, log_total, after, normed_two, inner)
    return result, kept, weights, attended, carried


def layer_back(weights, smalls, kept, grad_out, carry, attend_pull):
    w_qkv, w_proj, w_fc, w_out = weights
    gains, offsets, attn_bias, out_bias, fc_bias = smalls
    layer_in, normed, project, mixed, log_total, after, normed_two, inner = kept
    grads, carried = mlp_back(weights, gains[1], kept, grad_out, carry)
    grad_w_out, grad_w_fc, grad_fc_bias, grad_w_proj, grad_mixed, grad_after, sums = grads
    grad_q, grad_k, grad_v = attend_pull(
        (project, grad_mixed, mixed, log_total), (grad_w_fc, grad_w_out)
    )
    grad_w_qkv, grad_input, more = qkv_back(
        w_qkv, gains[0], kept, (grad_q, grad_k, grad_v), grad_after
    )
    vectors = jnp.concatenate([more[:4], sums[:4]], axis=0)
    return grad_input, (grad_w_qkv, grad_w_proj), (vectors, grad_fc_bias[0]), carried


MESH = pl.DeviceIdType.MESH
ANY = pl.BlockSpec(memory_space=pl.ANY)
CHUNK = 768


def greet(groups):
    sides = {side for group in groups for side in group}
    places = lax.axis_size("ctx")
    barrier = pltpu.get_barrier_semaphore()
    for flip, step, bits in sorted(sides):
        device = {
            "section": lax.axis_index("section") ^ flip,
            "ctx": lax.rem(lax.axis_index("ctx") + step, places),
            "fsdp": lax.axis_index("fsdp") ^ bits,
        }
        pl.semaphore_signal(barrier, inc=1, device_id=device, device_id_type=MESH)
    pl.semaphore_wait(barrier, len(sides))


def chip_group():
    return [(1, 0, 0)] + [(flip, 0, bits) for flip in (0, 1) for bits in (1, 2)]


def corner_group():
    return [(0, 0, 3), (1, 0, 3)]


def line_group():
    return [(0, step, 0) for step in range(1, lax.axis_size("ctx"))]


def column_group():
    return [(1, 0, 0)] + [
        (flip, step, 0) for step in range(1, lax.axis_size("ctx")) for flip in (0, 1)
    ]


def remote(source, target, send, recv, device):
    return pltpu.make_async_remote_copy(
        src_ref=source,
        dst_ref=target,
        send_sem=send,
        recv_sem=recv,
        device_id=device,
        device_id_type=MESH,
    )


class Gather:
    def __init__(self, layer, shards, outs, send, recv, local, *bounce):
        self.layer, self.shards, self.outs = layer, shards, outs
        self.bounce = bounce
        self.send, self.recv, self.local = send, recv, local
        self.section = lax.axis_index("section")
        self.index = lax.axis_index("fsdp")
        self.sibling = {"section": 1 - self.section}

    def across(self, bits, section=None):
        where = {"fsdp": self.index ^ bits}
        if section is not None:
            where["section"] = section
        return where

    def copy(self, m, slot, source, target, device):
        return remote(source, target, self.send.at[m, slot], self.recv.at[m, slot], device)

    def first(self, m, bits, half):
        slot = 0 if bits == 1 else 1
        return remote(
            self.shards[m].at[half],
            self.outs[m].at[self.index, half],
            self.send.at[m, slot + 8 * half],
            self.recv.at[m, slot],
            self.across(bits, half),
        )

    def arrived(self, m, bits):
        slot = 0 if bits == 1 else 1
        place = self.outs[m].at[self.index ^ bits, self.section]
        return self.copy(m, slot, place, place, self.across(bits))

    def own(self, m):
        return self.copy(m, 2, self.shards[m], self.outs[m].at[self.index], self.sibling)

    def take(self, m):
        return pltpu.make_async_copy(self.shards[m], self.bounce[m], self.local.at[0, m])

    def keep(self, m):
        return pltpu.make_async_copy(
            self.bounce[m], self.outs[m].at[self.index], self.local.at[1, m]
        )

    def corner(self, m, bits):
        middle = self.outs[m].shape[2] // 2
        rows = pl.ds(0, middle) if bits == 1 else pl.ds(middle, middle)
        place = self.outs[m].at[self.index ^ bits, self.section, rows]
        return self.copy(m, 3 if bits == 1 else 4, place, place, self.across(3 ^ bits))

    def trade(self, m, bits):
        place = self.outs[m].at[self.index ^ bits, self.section]
        return self.copy(m, 4 + bits, place, place, self.sibling)

    def start(self):
        @pl.when(self.section == self.layer)
        def _():
            for m in range(len(self.shards)):
                for half in (1 - self.layer, self.layer):
                    for bits in (1, 2):
                        self.first(m, bits, half).start()
                self.own(m).start()
                self.take(m).start()
            for m in range(len(self.shards)):
                self.take(m).wait()
                self.keep(m).start()

    def middle(self, m):
        for bits in (1, 2):
            self.arrived(m, bits).wait_recv()
            self.corner(m, bits).start()
            self.trade(m, bits).start()

    def last(self, m):
        for bits in (1, 2):
            self.corner(m, bits).wait_recv()
        self.trade(m, 3).start()

    def finish(self, m):
        for bits in (1, 2, 3):
            copy = self.trade(m, bits)
            copy.wait_send()
            copy.wait_recv()
        for bits in (1, 2):
            self.corner(m, bits).wait_send()

        @pl.when(self.section == self.layer)
        def _():
            for half in (0, 1):
                for bits in (1, 2):
                    self.first(m, bits, half).wait_send()
            self.own(m).wait_send()
            self.keep(m).wait()

        @pl.when(self.section != self.layer)
        def _():
            self.own(m).wait_recv()

class Seats:
    def __init__(self, seqs):
        self.sections, self.places = lax.axis_size("section"), lax.axis_size("ctx")
        self.seqs = seqs
        self.per = -(-seqs // (self.sections * self.places))
        self.size = self.places * self.per
        self.real = [min(max(seqs - i * self.size, 0), self.size) for i in range(self.sections)]
        self.skip = [(self.size - real) // 2 for real in self.real]

    def of(self, section, slot):
        real = jnp.where(section == 0, self.real[0], self.real[1])
        skip = jnp.where(section == 0, self.skip[0], self.skip[1])
        taken = (slot >= skip) & (slot < skip + real)
        return taken, jnp.clip(section * self.size + slot - skip, 0, self.seqs - 1)

    def home(self, seq):
        section, slot = seq // self.size, seq % self.size + self.skip[seq // self.size]
        return section, slot // self.per, slot % self.per


class Bring:
    def __init__(self, rows, outs, send, recv, local, zeros):
        self.rows, self.outs = rows, outs
        self.send, self.recv, self.local, self.zeros = send, recv, local, zeros
        self.seats = Seats(rows[0].shape[0])
        self.section, self.z = lax.axis_index("section"), lax.axis_index("ctx")
        self.depth = rows[0].shape[1]

    @staticmethod
    def scratch(rows, per, places):
        return [
            pltpu.SemaphoreType.DMA((len(rows), places * per)),
            pltpu.SemaphoreType.DMA((len(rows), per, places)),
            pltpu.SemaphoreType.DMA((len(rows), per, places)),
            pltpu.VMEM(rows[0].shape[1:], bf16),
        ]

    def span(self, z):
        return pl.ds(z * self.depth, self.depth)

    def copy(self, a, seq, place, p):
        return remote(
            self.rows[a].at[seq],
            self.outs[a].at[p, self.span(self.z)],
            self.send.at[a, place * self.seats.per + p],
            self.recv.at[a, p, self.z],
            {"ctx": place},
        )

    def arrival(self, a, p, place):
        target = self.outs[a].at[p, self.span(place)]
        return remote(target, target, self.send.at[a, 0], self.recv.at[a, p, place], {"ctx": place})

    def stay(self, a, seq, p):
        return pltpu.make_async_copy(
            self.rows[a].at[seq], self.outs[a].at[p, self.span(self.z)], self.local.at[a, p, 0]
        )

    def blank(self, a, p, place):
        return pltpu.make_async_copy(
            self.zeros, self.outs[a].at[p, self.span(place)], self.local.at[a, p, place]
        )

    def each(self, a, going, staying, coming, empty):
        for p in range(self.seats.per):
            for place in range(self.seats.places):
                taken, seq = self.seats.of(self.section, place * self.seats.per + p)

                @pl.when(taken & (place != self.z))
                def _():
                    going(a, seq, place, p)

            taken, seq = self.seats.of(self.section, self.z * self.seats.per + p)

            @pl.when(taken)
            def _():
                staying(a, seq, p)
                for place in range(self.seats.places):

                    @pl.when(place != self.z)
                    def _():
                        coming(a, p, place)

            @pl.when(jnp.logical_not(taken))
            def _():
                for place in range(self.seats.places):
                    empty(a, p, place)

    def clear(self):
        self.zeros[...] = jnp.zeros(self.zeros.shape, bf16)

    def start(self, a):
        self.each(
            a,
            lambda *at: self.copy(*at).start(),
            lambda *at: self.stay(*at).start(),
            lambda *at: None,
            lambda *at: self.blank(*at).start(),
        )

    def finish(self, a):
        self.each(
            a,
            lambda *at: self.copy(*at).wait_send(),
            lambda *at: self.stay(*at).wait(),
            lambda *at: self.arrival(*at).wait_recv(),
            lambda *at: self.blank(*at).wait(),
        )


class Deliver:
    def __init__(self, layer, rows, out, send, recv, local):
        self.layer, self.rows, self.out = layer, rows, out
        self.send, self.recv, self.local = send, recv, local
        self.seats = Seats(out.shape[0])
        self.section, self.z = lax.axis_index("section"), lax.axis_index("ctx")
        self.depth = out.shape[1]

    @staticmethod
    def scratch(seqs, per, places):
        return [
            pltpu.SemaphoreType.DMA((per, places)),
            pltpu.SemaphoreType.DMA((seqs,)),
            pltpu.SemaphoreType.DMA((per,)),
        ]

    def source(self, p, place):
        return self.rows.at[p, pl.ds(place * self.depth, self.depth)]

    def copy(self, p, place, seq):
        return remote(
            self.source(p, place),
            self.out.at[seq],
            self.send.at[p, place],
            self.recv.at[seq],
            {"section": self.layer, "ctx": place},
        )

    def stay(self, p, place, seq):
        return pltpu.make_async_copy(self.source(p, place), self.out.at[seq], self.local.at[p])

    def each(self, going, staying):
        for p in range(self.seats.per):
            taken, seq = self.seats.of(self.section, self.z * self.seats.per + p)
            for place in range(self.seats.places):
                here = (self.section == self.layer) & (self.z == place)

                @pl.when(taken & here)
                def _():
                    staying(p, place, seq)

                @pl.when(taken & jnp.logical_not(here))
                def _():
                    going(p, place, seq)

    def start(self):
        self.each(
            lambda *at: self.copy(*at).start(),
            lambda *at: self.stay(*at).start(),
        )

    def finish(self):
        self.each(
            lambda *at: self.copy(*at).wait_send(),
            lambda *at: self.stay(*at).wait(),
        )
        for seq in range(self.seats.seqs):
            section, place, p = self.seats.home(seq)

            @pl.when(
                (self.section == self.layer)
                & ((self.section != section) | (self.z != place))
            )
            def _():
                target = self.out.at[seq]
                remote(
                    target, target, self.send.at[0, 0], self.recv.at[seq], {"section": 1 - self.section}
                ).wait_recv()


class Spread:
    def __init__(self, block, out, send, recv, local):
        self.block, self.out, self.send, self.recv, self.local = block, out, send, recv, local
        self.section, self.index = lax.axis_index("section"), lax.axis_index("fsdp")

    @staticmethod
    def scratch():
        return [
            pltpu.SemaphoreType.DMA((8,)),
            pltpu.SemaphoreType.DMA((8,)),
            pltpu.SemaphoreType.DMA,
        ]

    def copies(self):
        for flip in (0, 1):
            for bits in range(4):
                if flip or bits:
                    yield remote(
                        self.block,
                        self.out.at[self.section, self.index],
                        self.send.at[4 * flip + bits],
                        self.recv.at[4 * flip + bits],
                        {"section": self.section ^ flip, "fsdp": self.index ^ bits},
                    )

    def stay(self):
        return pltpu.make_async_copy(
            self.block, self.out.at[self.section, self.index], self.local
        )

    def start(self):
        for copy in self.copies():
            copy.start()
        self.stay().start()

    def finish(self):
        for copy in self.copies():
            copy.wait_send()
            copy.wait_recv()
        self.stay().wait()


def gather_scratch(shards):
    count = len(shards)
    return [
        pltpu.SemaphoreType.DMA((count, 10)),
        pltpu.SemaphoreType.DMA((count, 8)),
        pltpu.SemaphoreType.DMA((2, count)),
    ] + [pltpu.VMEM(shard.shape, shard.dtype) for shard in shards]


def gather_shapes(shards):
    return [jax.ShapeDtypeStruct((4,) + shard.shape, shard.dtype) for shard in shards]


def split_shards(shards):
    return [shard.reshape(2, -1, shard.shape[-1]) for shard in shards]


def join_shards(outs):
    return tuple(out.reshape(-1, out.shape[-1]) for out in outs)


class Reduce:
    def __init__(self, line, layer, items, out, scratch):
        self.line, self.layer, self.items, self.out = line, layer, items, out
        (
            self.own,
            self.twin,
            self.near_corner,
            self.far_corner,
            self.near,
            self.far,
            self.outer,
            self.inner,
            self.partial,
            self.total,
            self.send,
            self.recv,
            self.local,
            self.done,
        ) = scratch
        self.section = lax.axis_index("section")
        self.index = lax.axis_index("fsdp")
        self.z = lax.axis_index("ctx")
        self.count = self.own.shape[0]
        self.sibling = {"section": 1 - self.section}
        self.x = {"fsdp": self.index ^ 1}
        self.y = {"fsdp": self.index ^ 2}
        self.is_inner = (self.z == 1) | (self.z == 2)
        self.end = {"ctx": jnp.where(self.z == 1, 0, 3)}
        self.toward = {"ctx": jnp.where(self.z == 0, 1, 2)}
        self.opposite = {"ctx": 3 - self.z}

    def chunks(self):
        k = 0
        for item in self.items:
            rows, columns = item.shape[2:]
            depth = self.own.shape[2]
            for row in range(0, rows, depth):
                for column in range(0, columns, CHUNK):
                    yield k, item, pl.ds(row, depth), pl.ds(column, CHUNK)
                    k += 1

    def copy(self, k, slot, source, target, device):
        return remote(source, target, self.send.at[slot, k], self.recv.at[slot, k], device)

    def swap(self, k):
        return self.copy(k, 0, self.twin.at[k], self.twin.at[k], self.sibling)

    def load(self, k):
        return pltpu.make_async_copy(self.own.at[k], self.own.at[k], self.local.at[k])

    def corner(self, k, near):
        half = self.own.shape[2] // 2
        rows = pl.ds(0, half) if near else pl.ds(half, half)
        source = self.own.at[k, self.index ^ 3, rows]
        target = (self.near_corner if near else self.far_corner).at[k]
        return self.copy(k, 1 if near else 2, source, target, self.x if near else self.y)

    def side(self, k, near):
        source = self.own.at[k, self.index ^ (1 if near else 2)]
        target = (self.near if near else self.far).at[k]
        return self.copy(k, 3 if near else 4, source, target, self.x if near else self.y)

    def inward(self, k):
        return self.copy(k, 5, self.partial.at[k], self.outer.at[k], self.toward)

    def across(self, k):
        return self.copy(k, 6, self.partial.at[k], self.inner.at[k], self.opposite)

    def outward(self, k):
        return self.copy(k, 7, self.total.at[k], self.total.at[k], self.end)

    def start(self):
        for k, item, rows, columns in self.chunks():
            theirs = item.at[:, 1 - self.section, rows, columns]
            mine = item.at[:, self.section, rows, columns]
            self.copy(k, 0, theirs, self.twin.at[k], self.sibling).start()
            pltpu.make_async_copy(mine, self.own.at[k], self.local.at[k]).start()

    def stage(self, number, k):
        half = self.own.shape[2] // 2
        near, far = self.index ^ 1, self.index ^ 2
        if number == 0:
            self.load(k).wait()
            self.swap(k).wait_recv()
            for j in range(4):
                self.own[k, j] = self.own[k, j] + self.twin[k, j]
            self.corner(k, True).start()
            self.corner(k, False).start()
        elif number == 1:
            self.corner(k, True).wait_recv()
            self.corner(k, False).wait_recv()
            self.own[k, far, :half] = self.own[k, far, :half] + self.near_corner[k]
            self.own[k, near, half:] = self.own[k, near, half:] + self.far_corner[k]
            self.side(k, True).start()
            self.side(k, False).start()
        elif number == 2:
            self.side(k, True).wait_recv()
            self.side(k, False).wait_recv()
            summed = (
                self.own[k, self.index].astype(f32)
                + self.near[k].astype(f32)
                + self.far[k].astype(f32)
            ).astype(bf16)
            if not self.line:
                self.total[k] = summed
                return
            self.partial[k] = summed

            @pl.when(jnp.logical_not(self.is_inner))
            def _():
                self.inward(k).start()
        elif number == 3 and self.line:

            @pl.when(self.is_inner)
            def _():
                self.inward(k).wait_recv()
                self.partial[k] = self.partial[k] + self.outer[k]
                self.across(k).start()
        elif number == 4 and self.line:

            @pl.when(self.is_inner)
            def _():
                self.across(k).wait_recv()
                self.total[k] = self.partial[k] + self.inner[k]
                self.outward(k).start()

    def step(self, t, lags):
        for number, lag in enumerate(lags):
            k = t - lag

            @pl.when((k >= 0) & (k < self.count))
            def _():
                self.stage(number, k)

    def finish(self, k):
        self.swap(k).wait_send()
        for near in (True, False):
            self.corner(k, near).wait_send()
            self.side(k, near).wait_send()
        if self.line:

            @pl.when(self.is_inner)
            def _():
                self.across(k).wait_send()
                self.outward(k).wait_send()

            @pl.when(jnp.logical_not(self.is_inner))
            def _():
                self.inward(k).wait_send()
                self.outward(k).wait_recv()

    def write(self):
        return pltpu.make_async_copy(self.total, self.out.at[self.section], self.local.at[0])

    def give(self):
        place = self.out.at[1 - self.layer]
        return remote(self.total, place, self.done.at[0], self.done.at[1], self.sibling)

    def close(self):
        self.write().start()

        @pl.when(self.section != self.layer)
        def _():
            self.give().start()
            self.give().wait_send()

        @pl.when(self.section == self.layer)
        def _():
            self.give().wait_recv()

        self.write().wait()


LAGS = (0, 1, 3, 4, 5)
CARRIED_LAGS = (0, 2, 4, 6, 8)


class ReducePart:
    lags = CARRIED_LAGS

    def __init__(self, layer, grads, line):
        self.layer, self.line = layer, line
        self.ins = [grad.reshape(4, 2, -1, grad.shape[-1]) for grad in grads]
        depth = min(item.shape[2] for item in self.ins)
        self.chunks = sum((item.shape[2] // depth) * (item.shape[3] // CHUNK) for item in self.ins)
        self.outs = [jax.ShapeDtypeStruct((2, self.chunks, depth, CHUNK), bf16)]
        self.scratch = reduce_scratch(self.chunks, depth)

    def groups(self):
        return [column_group(), [(0, 0, 1), (0, 0, 2)]]

    def bind(self, ins, outs, scratch):
        return Reduce(self.line, self.layer, ins, outs[0], scratch)

    def begin(self, reduce):
        reduce.start()

    def tick(self, reduce, step, steps):
        lags = LAGS if steps == 1 else self.lags
        share = -(-(self.chunks + lags[-1]) // steps)

        def advance(t, _):
            reduce.step(step * share + t, lags)
            return 0

        lax.fori_loop(0, share, advance, 0)

    def end(self, reduce):
        def finish(k, _):
            reduce.finish(k)
            return 0

        lax.fori_loop(0, reduce.count, finish, 0)
        reduce.close()

    def result(self, outs):
        return outs[0] if self.line else lax.psum(outs[0], "ctx")


class DeliverPart:
    def __init__(self, layer, rows, stored):
        seats = Seats(stored[0])
        self.layer = layer
        self.ins = [rows.reshape(seats.per, -1, rows.shape[-1])]
        self.outs = [jax.ShapeDtypeStruct(stored, bf16)]
        self.scratch = Deliver.scratch(stored[0], seats.per, seats.places)

    def groups(self):
        return [column_group()]

    def bind(self, ins, outs, scratch):
        return Deliver(self.layer, ins[0], outs[0], *scratch)

    def begin(self, deliver):
        deliver.start()

    def tick(self, deliver, step, steps):
        pass

    def end(self, deliver):
        deliver.finish()

    def result(self, outs):
        return outs[0]


class BringPart:
    def __init__(self, rows):
        seats = Seats(rows.shape[0])
        _, depth, width = rows.shape
        self.ins = [rows]
        self.outs = [jax.ShapeDtypeStruct((seats.per, depth * seats.places, width), bf16)]
        self.scratch = Bring.scratch([rows], seats.per, seats.places)

    def groups(self):
        return [line_group()]

    def bind(self, ins, outs, scratch):
        return Bring(ins, outs, *scratch)

    def begin(self, bring):
        bring.clear()
        bring.start(0)

    def tick(self, bring, step, steps):
        pass

    def end(self, bring):
        bring.finish(0)

    def result(self, outs):
        return outs[0]


class SpreadPart:
    def __init__(self, block):
        self.ins = [block]
        self.outs = [jax.ShapeDtypeStruct((2, 4) + block.shape, bf16)]
        self.scratch = Spread.scratch()

    def groups(self):
        return [chip_group(), corner_group()]

    def bind(self, ins, outs, scratch):
        return Spread(ins[0], outs[0], *scratch)

    def begin(self, spread):
        spread.start()

    def tick(self, spread, step, steps):
        pass

    def end(self, spread):
        spread.finish()

    def result(self, outs):
        return outs[0]


class GatherPart:
    def __init__(self, layer, shards):
        self.layer = layer
        self.ins = split_shards(shards)
        self.outs = gather_shapes(self.ins)
        self.scratch = gather_scratch(self.ins)

    def groups(self):
        return [chip_group()]

    def bind(self, ins, outs, scratch):
        return Gather(self.layer, ins, outs, *scratch)

    def begin(self, gather):
        gather.start()

    def tick(self, gather, step, steps):
        count = len(self.ins)
        if steps == 1:
            for m in range(count):
                gather.middle(m)
                if m > 0:
                    gather.last(m - 1)
            gather.last(count - 1)
            return
        for m in range(count):

            @pl.when(step == steps - 1 - count + m)
            def _():
                gather.middle(m)

            @pl.when(step == steps - 1)
            def _():
                gather.last(m)

    def end(self, gather):
        for m in range(len(self.ins)):
            gather.finish(m)

    def result(self, outs):
        return join_shards(outs)


class Carry:
    def __init__(self, collective, *parts):
        self.collective, self.parts = collective, parts
        self.ins = [array for part in parts for array in part.ins]
        self.outs = [shape for part in parts for shape in part.outs]
        self.scratch = [shape for part in parts for shape in part.scratch]

    def params(self, limit=60):
        return pltpu.CompilerParams(
            collective_id=self.collective,
            has_side_effects=self.collective is not None,
            vmem_limit_bytes=limit * 1024 * 1024,
        )

    def kernel(self, body, ins, outs, scratch, grid):
        if not self.parts:
            return body
        steps = 1
        for size in grid:
            steps *= size

        def run(*refs):
            pieces, at = [], 0
            for size in (ins, len(self.ins), outs, len(self.outs), scratch, len(self.scratch)):
                pieces.append(refs[at : at + size])
                at += size
            bound, at = [], [0, 0, 0]
            for part in self.parts:
                sizes = [len(part.ins), len(part.outs), len(part.scratch)]
                taken = [
                    pieces[2 * i + 1][at[i] : at[i] + sizes[i]] for i in range(3)
                ]
                at = [at[i] + sizes[i] for i in range(3)]
                bound.append((part, part.bind(*taken)))
            step = 0
            for axis in range(len(grid)):
                step = step * grid[axis] + pl.program_id(axis)

            def begin():
                greet([group for part in self.parts for group in part.groups()])
                for part, state in bound:
                    part.begin(state)

            def end():
                for part, state in bound:
                    part.end(state)

            if steps == 1:
                begin()
            else:
                pl.when(step == 0)(begin)
            body(*pieces[0], *pieces[2], *pieces[4])
            for part, state in bound:
                part.tick(state, step, steps)
            if steps == 1:
                end()
            else:
                pl.when(step == steps - 1)(end)

        return run

    def alone(self):
        outs = pl.pallas_call(
            self.kernel(lambda: None, 0, 0, 0, ()),
            in_specs=[ANY] * len(self.ins),
            out_specs=[ANY] * len(self.outs),
            out_shape=self.outs,
            scratch_shapes=self.scratch,
            compiler_params=self.params(),
        )(*self.ins)
        return self.result(outs)

    def result(self, outs):
        results, at = [], 0
        for part in self.parts:
            results.append(part.result(outs[at : at + len(part.outs)]))
            at += len(part.outs)
        return results


def reduce_scratch(count, depth):
    block = (count, depth, CHUNK)
    half = (count, depth // 2, CHUNK)
    return (
        [pltpu.VMEM((count, 4, depth, CHUNK), bf16)] * 2
        + [pltpu.VMEM(half, bf16)] * 2
        + [pltpu.VMEM(block, bf16)] * 6
        + [
            pltpu.SemaphoreType.DMA((8, count)),
            pltpu.SemaphoreType.DMA((8, count)),
            pltpu.SemaphoreType.DMA((count,)),
            pltpu.SemaphoreType.DMA((2,)),
        ]
    )


def unchunk(blocks, shapes):
    depth = blocks.shape[-2]
    parts, k = [], 0
    for rows, columns in shapes:
        high, wide = rows // depth, columns // CHUNK
        part = blocks[..., k : k + high * wide, :, :]
        part = part.reshape(blocks.shape[:-3] + (high, wide) + blocks.shape[-2:])
        part = jnp.concatenate([part[..., j, :, :] for j in range(wide)], axis=-1)
        parts.append(part.reshape(blocks.shape[:-3] + (rows, columns)))
        k += high * wide
    return parts


def shards(
    block_input,
    positions,
    cotangent,
    w_qkv,
    w_proj,
    w_fc,
    w_out,
    ln_gain,
    ln_bias,
    attn_bias,
    out_bias,
    fc_bias,
):
    section = lax.axis_index("section")
    first = section == 0
    ctxs = lax.axis_size("ctx")
    fsdps = lax.axis_size("fsdp")
    local_seqs, local_rows, width = block_input.shape
    stored = block_input.shape
    length = positions.shape[1]
    seats = Seats(local_seqs)
    per = seats.per
    shard_width = ln_gain.shape[2]

    pack = jnp.concatenate(
        [ln_gain[0], ln_bias[0], attn_bias[0], out_bias[0], fc_bias[0].reshape(-1, shard_width)]
    )
    pack = jnp.pad(pack, ((0, 16 - pack.shape[0]), (0, 256 - shard_width)))

    def unpack(packed):
        packed = packed[:, :12, :shard_width]
        vectors = jnp.transpose(packed[:, :8], (1, 0, 2)).reshape(8, -1).astype(f32)
        fc = packed[:, 8:].reshape(-1).astype(f32)
        return vectors[0:2], vectors[2:4], vectors[4:6], vectors[6:8], fc

    shards_own = [matrix[0] for matrix in (w_qkv, w_proj, w_fc, w_out)]
    block_rows, packs, first_weights = Carry(
        0, BringPart(block_input), SpreadPart(pack), GatherPart(0, shards_own[:2])
    ).alone()
    smalls = [unpack(packs[layer]) for layer in range(2)]

    places = jnp.stack(
        [
            lax.dynamic_index_in_dim(
                positions, seats.of(section, lax.axis_index("ctx") * per + p)[1], 0, keepdims=False
            )
            for p in range(per)
        ]
    )
    order = (
        lax.broadcasted_iota(jnp.int32, (per, length, length), 1) == places[:, None, :]
    ).astype(bf16)
    order_back = (
        lax.broadcasted_iota(jnp.int32, (per, length, length), 2) == places[:, :, None]
    ).astype(bf16)

    def to_sorted(rows):
        return (
            jnp.einsum("bpt,btd->bpd", order, rows, preferred_element_type=f32)
            .astype(bf16)
            .reshape(per * length, width)
        )

    def to_stored(rows):
        return jnp.einsum(
            "btp,bpd->btd", order_back, rows.reshape(per, length, width), preferred_element_type=f32
        ).astype(bf16)

    start = to_sorted(block_rows)
    line = ctxs == 4

    def attend_zero(project):
        carry = Carry(1, GatherPart(0, shards_own[2:]), BringPart(cotangent))
        return attend_forward(project, length, carry)

    middle, kept_zero, weights_zero, attended, (early,) = layer_forward(
        (first_weights[0], lambda attended: (*first_weights, *attended[0])),
        smalls[0],
        start,
        attend_zero,
        Carry(7, GatherPart(1, shards_own[:2])),
    )
    grad_final = to_sorted(attended[1])

    def attend_one(project):
        carry = Carry(4, GatherPart(1, shards_own[2:]), DeliverPart(0, to_stored(middle), stored))
        return attend_forward(project, length, carry)

    final, kept_one, weights_one, (_, out_zero), _ = layer_forward(
        (early[0], lambda attended: (*early, *attended[0])), smalls[1], middle, attend_one, Carry(None)
    )
    outs = [out_zero]
    halves = []

    def pull_one(kept, grads):
        carry = Carry(5, ReducePart(1, grads, line), DeliverPart(1, to_stored(final), stored))
        pulled, (reduced, out_one) = attend_back(*kept, length, carry)
        outs.append(out_one)
        halves.append(reduced)
        return pulled

    def pull_zero(kept, grads):
        pulled, (reduced,) = attend_back(*kept, length, Carry(6, ReducePart(0, grads, line)))
        halves.append(reduced)
        return pulled

    grad_middle, grads_one, small_one, _ = layer_back(
        weights_one, smalls[1], kept_one, grad_final, Carry(None), pull_one
    )
    carry = Carry(
        2, ReducePart(1, grads_one, line), DeliverPart(1, to_stored(grad_middle), stored)
    )
    grad_start, grads_zero, small_zero, (rest_one, in_one) = layer_back(
        weights_zero, smalls[0], kept_zero, grad_middle, carry, pull_zero
    )

    def repack(small):
        vectors, fc = small
        vectors = jnp.transpose(vectors.reshape(8, fsdps, shard_width), (1, 0, 2))
        packed = jnp.concatenate([vectors, fc.reshape(fsdps, -1, shard_width)], axis=1)
        depth = w_qkv.shape[1] // 2
        return jnp.pad(
            packed.astype(bf16),
            ((0, 0), (0, depth - packed.shape[1]), (0, CHUNK - packed.shape[2])),
        )[:, None]

    pack = jnp.concatenate([repack(small_zero), repack(small_one)], axis=1)
    pack = pack.reshape(-1, CHUNK)
    rest_zero, in_zero = Carry(
        3,
        ReducePart(0, (*grads_zero, pack), line),
        DeliverPart(0, to_stored(grad_start), stored),
    ).alone()
    packed = jnp.where(first, rest_zero[0, -1], rest_zero[1, -1])[:12, :shard_width].astype(f32)
    section_out = jnp.where(first, outs[0], outs[1])[None]
    section_in_grad = jnp.where(first, in_zero, in_one)[None]
    shapes = [(matrix.shape[1] // 2, matrix.shape[2]) for matrix in (w_qkv, w_proj, w_fc, w_out)]
    reduced = [
        jnp.where(first, rest_zero[:, :-1], rest_one),
        jnp.where(first, halves[1], halves[0]),
    ]
    big = [
        block.reshape(-1, block.shape[-1]).astype(f32)[None]
        for some, these in zip(reduced, (shapes[:2], shapes[2:]))
        for block in unchunk(some, these)
    ]

    return (
        section_out,
        section_in_grad,
        *big,
        packed[None, 0:8:4],
        packed[None, 1:8:4],
        packed[None, 2:4],
        packed[None, 6:8],
        packed[8:].reshape(1, -1),
    )


def solution(mesh):
    matrix = P("section", "fsdp", None)
    vectors = P("section", None, "fsdp")
    rows_out = P("section", "fsdp", "ctx", None)
    return jax.shard_map(
        shards,
        mesh=mesh,
        in_specs=(
            P("fsdp", "ctx", None),
            P("fsdp", None),
            P("fsdp", "ctx", None),
            *([matrix] * 4),
            *([vectors] * 4),
            P("section", "fsdp"),
        ),
        out_specs=(
            rows_out,
            rows_out,
            *([matrix] * 4),
            *([vectors] * 4),
            P("section", "fsdp"),
        ),
        check_vma=False,
    )
```

```python
import functools

import jax
import jax.numpy as jnp
from jax import lax
from jax.experimental import pallas as pl
from jax.experimental.pallas import tpu as pltpu
from jax.sharding import PartitionSpec as P

H = 12
HD = 64
PAIR = 2 * HD
SCALE = HD**-0.5

masked_score = -1e30
norm_eps = 1e-05
f32 = jnp.float32
bf16 = jnp.bfloat16


def layer_norm(hidden, gain, offset):
    center = hidden - jnp.mean(hidden, axis=-1, keepdims=True)
    spread = jnp.mean(center * center, axis=-1, keepdims=True)
    return center * lax.rsqrt(spread + norm_eps) * gain + offset


def gelu_tanh(inputs):
    return jax.nn.gelu(inputs, approximate=True)


def mm(left, right):
    return lax.dot_general(left, right, (((1,), (0,)), ((), ())), preferred_element_type=f32)


def mm_nt(left, right):
    return lax.dot_general(left, right, (((1,), (1,)), ((), ())), preferred_element_type=f32)


def mm_tn(left, right):
    return lax.dot_general(left, right, (((0,), (0,)), ((), ())), preferred_element_type=f32)


def masked_scores(keys, queries, start, block):
    scores = mm_nt(keys, queries)
    down = lax.broadcasted_iota(jnp.int32, (block, block), 0)
    across = lax.broadcasted_iota(jnp.int32, (block, block), 1)
    corner = jnp.where(across >= down, scores[start:], masked_score)
    if start == 0:
        return corner
    return jnp.concatenate([scores[:start], corner], axis=0)


def attend_kernel(block, q_ref, k_ref, v_ref, o_ref, log_ref):
    length = q_ref.shape[0]
    for head in range(2):
        cols = slice(head * HD, (head + 1) * HD)
        for start in range(0, length, block):
            end = start + block
            queries = (q_ref[start:end, cols].astype(f32) * SCALE).astype(bf16)
            scores = masked_scores(k_ref[:end, cols], queries, start, block)
            top = jnp.max(scores, axis=0, keepdims=True)
            weights = jnp.exp(scores - top)
            total = jnp.sum(weights, axis=0, keepdims=True)
            mixed = mm_tn(v_ref[:end, cols], weights.astype(bf16)) / total
            o_ref[start:end, cols] = mixed.T.astype(bf16)
            log_ref[0, 0, head : head + 1, start:end] = top + jnp.log(total)


def attend_back_kernel(
    block, q_ref, k_ref, v_ref, do_ref, o_ref, log_ref, dq_ref, dk_ref, dv_ref, dk_sum, dv_sum
):
    length = q_ref.shape[0]
    for head in range(2):
        cols = slice(head * HD, (head + 1) * HD)
        for start in range(length - block, -1, -block):
            end = start + block
            queries = (q_ref[start:end, cols].astype(f32) * SCALE).astype(bf16)
            grads = do_ref[start:end, cols]
            product = grads.astype(f32) * o_ref[start:end, cols].astype(f32)
            delta = jnp.sum(product.T, axis=0, keepdims=True)
            keys = k_ref[:end, cols]
            scores = masked_scores(keys, queries, start, block)
            probs = jnp.exp(scores - log_ref[0, 0, head : head + 1, start:end])
            grad_probs = mm_nt(v_ref[:end, cols], grads)
            grad_scores = (probs * (grad_probs - delta)).astype(bf16)
            dv = mm(probs.astype(bf16), grads)
            dk = mm(grad_scores, queries)
            if end == length:
                dv_sum[:end, cols] = dv
                dk_sum[:end, cols] = dk
            else:
                dv_sum[:end, cols] += dv
                dk_sum[:end, cols] += dk
            dq = mm_tn(keys, grad_scores) * SCALE
            dq_ref[start:end, cols] = dq.T.astype(bf16)
    dk_ref[...] = dk_sum[...].astype(bf16)
    dv_ref[...] = dv_sum[...].astype(bf16)


def query_block(length):
    return 256 if length % 256 == 0 else length


def head_spec(length, offset):
    return pl.BlockSpec((length, PAIR), lambda b, h: (b, offset + h))


def log_spec(length):
    return pl.BlockSpec((1, 1, 2, length), lambda b, h: (b, h, 0, 0))


def attend_forward(project, length, carry):
    rows = project.shape[0]
    count = rows // length
    pairs = H // 2
    grid = (count, pairs)
    body = functools.partial(attend_kernel, query_block(length))
    outs = pl.pallas_call(
        carry.kernel(body, 3, 2, 0, grid),
        grid=grid,
        in_specs=[head_spec(length, 0), head_spec(length, pairs), head_spec(length, 2 * pairs)]
        + [ANY] * len(carry.ins),
        out_specs=[head_spec(length, 0), log_spec(length)] + [ANY] * len(carry.outs),
        out_shape=[
            jax.ShapeDtypeStruct((rows, H * HD), bf16),
            jax.ShapeDtypeStruct((count, pairs, 2, length), f32),
        ]
        + carry.outs,
        scratch_shapes=carry.scratch,
        compiler_params=carry.params(),
        cost_estimate=pl.CostEstimate(
            flops=8 * rows * length * H * HD,
            bytes_accessed=8 * rows * H * HD,
            transcendentals=rows * length * H // 2,
        ),
    )(project, project, project, *carry.ins)
    return outs[:2], carry.result(outs[2:])


def attend_back(project, grad_mixed, mixed, log_total, length, carry):
    rows = project.shape[0]
    count = rows // length
    pairs = H // 2
    grid = (count, pairs)
    body = functools.partial(attend_back_kernel, query_block(length))
    outs = pl.pallas_call(
        carry.kernel(body, 6, 3, 2, grid),
        grid=grid,
        in_specs=[
            head_spec(length, 0),
            head_spec(length, pairs),
            head_spec(length, 2 * pairs),
            head_spec(length, 0),
            head_spec(length, 0),
            log_spec(length),
        ]
        + [ANY] * len(carry.ins),
        out_specs=[head_spec(length, 0)] * 3 + [ANY] * len(carry.outs),
        out_shape=[jax.ShapeDtypeStruct((rows, H * HD), bf16)] * 3 + carry.outs,
        scratch_shapes=[pltpu.VMEM((length, PAIR), f32)] * 2 + carry.scratch,
        compiler_params=carry.params(),
        cost_estimate=pl.CostEstimate(
            flops=20 * rows * length * H * HD,
            bytes_accessed=16 * rows * H * HD,
            transcendentals=rows * length * H // 2,
        ),
    )(project, project, project, grad_mixed, mixed, log_total, *carry.ins)
    return outs[:3], carry.result(outs[3:])


TILE = 512
BLOCK = 256
ROOT = 0.7978845608028654
CUBE = 0.044715


def norm_back(hidden, grad, gain):
    center = hidden - jnp.mean(hidden, axis=-1, keepdims=True)
    scale = lax.rsqrt(jnp.mean(center * center, axis=-1, keepdims=True) + norm_eps)
    unit = center * scale
    scaled = grad * gain
    shift = jnp.mean(scaled, axis=-1, keepdims=True)
    tilt = jnp.mean(scaled * unit, axis=-1, keepdims=True)
    return unit, (scaled - shift - unit * tilt) * scale


def whole_spec(shape):
    return pl.BlockSpec(shape, lambda *at: (0,) * len(shape), pipeline_mode=pl.Buffered(1))


def mlp_kernel(
    hidden_ref,
    mixed_ref,
    w_proj_ref,
    w_fc_ref,
    w_out_ref,
    vectors_ref,
    fc_bias_ref,
    after_ref,
    normed_ref,
    inner_ref,
    result_ref,
    total,
):
    step = pl.program_id(0)
    rows = hidden_ref.shape[0]
    blocks = [slice(start, start + BLOCK) for start in range(0, rows, BLOCK)]

    @pl.when(step == 0)
    def _():
        for here in blocks:
            after = hidden_ref[here].astype(f32) + mm(mixed_ref[here], w_proj_ref[...])
            after = after + vectors_ref[2:3]
            after_ref[here] = after
            normed_ref[here] = layer_norm(after, vectors_ref[0:1], vectors_ref[1:2]).astype(bf16)
            total[here] = after + vectors_ref[3:4]

    for here in blocks:
        inner = mm(normed_ref[here], w_fc_ref[...]) + fc_bias_ref[...]
        inner_ref[here] = inner
        bend = jnp.tanh(inner * (ROOT + (ROOT * CUBE) * (inner * inner)))
        half = 0.5 * inner
        active = (half + half * bend).astype(bf16)
        total[here] += mm(active, w_out_ref[...])

    @pl.when(step == pl.num_programs(0) - 1)
    def _():
        result_ref[...] = total[...].astype(bf16)


def mlp(weights, smalls, layer_in, mixed, carry):
    _, w_proj, w_fc, w_out = weights
    gains, offsets, _, out_bias, fc_bias = smalls
    rows, width = layer_in.shape
    wide = w_fc.shape[1]
    tile = TILE if wide % TILE == 0 else wide
    grid = (wide // tile,)
    vectors = jnp.stack([gains[1], offsets[1], out_bias[0], out_bias[1]])

    def along(height):
        return pl.BlockSpec((height, tile), lambda i: (0, i))

    outs = pl.pallas_call(
        carry.kernel(mlp_kernel, 7, 4, 1, grid),
        grid=grid,
        in_specs=[
            whole_spec((rows, width)),
            whole_spec((rows, width)),
            whole_spec((width, width)),
            along(width),
            pl.BlockSpec((tile, width), lambda i: (i, 0)),
            whole_spec((4, width)),
            along(1),
        ]
        + [ANY] * len(carry.ins),
        out_specs=[
            whole_spec((rows, width)),
            whole_spec((rows, width)),
            along(rows),
            whole_spec((rows, width)),
        ]
        + [ANY] * len(carry.outs),
        out_shape=[
            jax.ShapeDtypeStruct((rows, width), f32),
            jax.ShapeDtypeStruct((rows, width), bf16),
            jax.ShapeDtypeStruct((rows, wide), f32),
            jax.ShapeDtypeStruct((rows, width), bf16),
        ]
        + carry.outs,
        scratch_shapes=[pltpu.VMEM((rows, width), f32)] + carry.scratch,
        compiler_params=carry.params(),
        cost_estimate=pl.CostEstimate(
            flops=4 * rows * width * wide + 2 * rows * width * width,
            bytes_accessed=4 * rows * wide + 4 * wide * width + 12 * rows * width,
            transcendentals=rows * wide,
        ),
    )(layer_in, mixed, w_proj, w_fc, w_out, vectors, fc_bias[None], *carry.ins)
    return outs[:4], carry.result(outs[4:])


def qkv_back_kernel(
    dq_ref, dk_ref, dv_ref, normed_ref, w_ref, hidden_ref, dafter_ref, gain_ref,
    dw_ref, dx_ref, sums_ref,
):
    rows, width = dq_ref.shape
    parts = (dq_ref, dk_ref, dv_ref)
    for i, part in enumerate(parts):
        columns = slice(i * width, (i + 1) * width)
        dw_ref[:, columns] = mm_tn(normed_ref[...], part[...]).astype(bf16)
    sums_ref[...] = jnp.zeros(sums_ref.shape, f32)
    for start in range(0, rows, BLOCK):
        here = slice(start, start + BLOCK)
        grad = jnp.zeros((BLOCK, width), f32)
        for i, part in enumerate(parts):
            grad = grad + mm_nt(part[here], w_ref[:, i * width : (i + 1) * width])
        unit, back = norm_back(hidden_ref[here].astype(f32), grad, gain_ref[...])
        dx_ref[here] = (dafter_ref[here] + back).astype(bf16)
        sums_ref[0:1] += jnp.sum(grad * unit, axis=0, keepdims=True)
        sums_ref[1:2] += jnp.sum(grad, axis=0, keepdims=True)
        sums_ref[2:3] += jnp.sum(dq_ref[here].astype(f32), axis=0, keepdims=True)
        sums_ref[3:4] += jnp.sum(dv_ref[here].astype(f32), axis=0, keepdims=True)


def qkv_back(w_qkv, gain, kept, grads, grad_after):
    layer_in, normed = kept[:2]
    rows, width = layer_in.shape
    return pl.pallas_call(
        qkv_back_kernel,
        out_shape=[
            jax.ShapeDtypeStruct((width, 3 * width), bf16),
            jax.ShapeDtypeStruct((rows, width), bf16),
            jax.ShapeDtypeStruct((8, width), f32),
        ],
        compiler_params=pltpu.CompilerParams(vmem_limit_bytes=60 * 1024 * 1024),
        cost_estimate=pl.CostEstimate(
            flops=12 * rows * width * width,
            bytes_accessed=18 * rows * width + 12 * width * width,
            transcendentals=0,
        ),
    )(*grads, normed, w_qkv, layer_in, grad_after, gain[None])


def mlp_back_kernel(
    dy_ref,
    normed_ref,
    inner_ref,
    w_fc_ref,
    w_out_ref,
    after_ref,
    mixed_ref,
    w_proj_ref,
    gain_ref,
    dw_out_ref,
    dw_fc_ref,
    dfc_ref,
    dw_proj_ref,
    dmixed_ref,
    dafter_ref,
    sums_ref,
    total,
    active,
    dinner,
    dbranch,
):
    step = pl.program_id(0)
    rows = dy_ref.shape[0]

    @pl.when(step == 0)
    def _():
        total[...] = jnp.zeros(total.shape, f32)

    for start in range(0, rows, BLOCK):
        here = slice(start, start + BLOCK)
        inner = inner_ref[here]
        square = inner * inner
        bend = jnp.tanh(inner * (ROOT + (ROOT * CUBE) * square))
        half = 0.5 * (1.0 + bend)
        active[here] = (inner * half).astype(bf16)
        slope = half + (0.5 * ROOT) * inner * (1.0 - bend * bend) * (1.0 + (3.0 * CUBE) * square)
        grad = (mm_nt(dy_ref[here], w_out_ref[...]) * slope).astype(bf16)
        dinner[here] = grad
        total[here] += mm_nt(grad, w_fc_ref[...])
    dw_out_ref[...] = mm_tn(active[...], dy_ref[...]).astype(bf16)
    dw_fc_ref[...] = mm_tn(normed_ref[...], dinner[...]).astype(bf16)
    dfc_ref[...] = jnp.sum(dinner[...].astype(f32), axis=0, keepdims=True)

    @pl.when(step == pl.num_programs(0) - 1)
    def _():
        sums_ref[...] = jnp.zeros(sums_ref.shape, f32)
        for start in range(0, rows, BLOCK):
            here = slice(start, start + BLOCK)
            grad = total[here]
            out = dy_ref[here].astype(f32)
            unit, back = norm_back(after_ref[here], grad, gain_ref[...])
            after = out + back
            dafter_ref[here] = after
            branch = after.astype(bf16)
            dbranch[here] = branch
            sums_ref[0:1] += jnp.sum(grad * unit, axis=0, keepdims=True)
            sums_ref[1:2] += jnp.sum(grad, axis=0, keepdims=True)
            sums_ref[2:3] += jnp.sum(branch.astype(f32), axis=0, keepdims=True)
            sums_ref[3:4] += jnp.sum(out, axis=0, keepdims=True)
            dmixed_ref[here] = mm_nt(branch, w_proj_ref[...]).astype(bf16)
        dw_proj_ref[...] = mm_tn(mixed_ref[...], dbranch[...]).astype(bf16)


def mlp_back(weights, gain, kept, grad_out, carry):
    _, w_proj, w_fc, w_out = weights
    _, _, _, mixed, _, after, normed_two, inner = kept
    rows, width = grad_out.shape
    wide = inner.shape[1]
    tile = TILE if wide % TILE == 0 else wide
    grid = (wide // tile,)
    once = pl.Buffered(1)

    def whole(shape):
        return pl.BlockSpec(shape, lambda i: (0, 0), pipeline_mode=once)

    across = pl.BlockSpec((tile, width), lambda i: (i, 0))

    def along(height):
        return pl.BlockSpec((height, tile), lambda i: (0, i))

    outs = pl.pallas_call(
        carry.kernel(mlp_back_kernel, 9, 7, 4, grid),
        grid=grid,
        in_specs=[
            whole((rows, width)),
            whole((rows, width)),
            along(rows),
            along(width),
            across,
            whole((rows, width)),
            whole((rows, width)),
            whole((width, width)),
            whole((1, width)),
        ]
        + [ANY] * len(carry.ins),
        out_specs=[
            across,
            along(width),
            along(1),
            whole((width, width)),
            whole((rows, width)),
            whole((rows, width)),
            whole((8, width)),
        ]
        + [ANY] * len(carry.outs),
        out_shape=[
            jax.ShapeDtypeStruct((wide, width), bf16),
            jax.ShapeDtypeStruct((width, wide), bf16),
            jax.ShapeDtypeStruct((1, wide), f32),
            jax.ShapeDtypeStruct((width, width), bf16),
            jax.ShapeDtypeStruct((rows, width), bf16),
            jax.ShapeDtypeStruct((rows, width), f32),
            jax.ShapeDtypeStruct((8, width), f32),
        ]
        + carry.outs,
        scratch_shapes=[
            pltpu.VMEM((rows, width), f32),
            pltpu.VMEM((rows, tile), bf16),
            pltpu.VMEM((rows, tile), bf16),
            pltpu.VMEM((rows, width), bf16),
        ]
        + carry.scratch,
        compiler_params=carry.params(),
        cost_estimate=pl.CostEstimate(
            flops=8 * rows * width * wide + 4 * rows * width * width,
            bytes_accessed=4 * rows * wide + 8 * wide * width + 16 * rows * width,
            transcendentals=rows * wide,
        ),
    )(
        grad_out,
        normed_two,
        inner,
        w_fc,
        w_out,
        after,
        mixed,
        w_proj,
        gain[None],
        *carry.ins,
    )
    return outs[:7], carry.result(outs[7:])


def layer_forward(weights, smalls, layer_in, attend, carry):
    w_qkv = weights[0]
    gains, offsets, attn_bias, _, _ = smalls
    width = layer_in.shape[-1]
    normed = layer_norm(layer_in.astype(f32), gains[0], offsets[0]).astype(bf16)
    bias = jnp.concatenate([attn_bias[0], jnp.zeros((width,), f32), attn_bias[1]])
    project = (mm(normed, w_qkv) + bias).astype(bf16)
    (mixed, log_total), attended = attend(project)
    if callable(weights[1]):
        weights = weights[1](attended)
    (after, normed_two, inner, result), carried = mlp(weights, smalls, layer_in, mixed, carry)
    kept = (layer_in, normed, project, mixed, log_total, after, normed_two, inner)
    return result, kept, weights, attended, carried


def layer_back(weights, smalls, kept, grad_out, carry, attend_pull):
    w_qkv, w_proj, w_fc, w_out = weights
    gains, offsets, attn_bias, out_bias, fc_bias = smalls
    layer_in, normed, project, mixed, log_total, after, normed_two, inner = kept
    grads, carried = mlp_back(weights, gains[1], kept, grad_out, carry)
    grad_w_out, grad_w_fc, grad_fc_bias, grad_w_proj, grad_mixed, grad_after, sums = grads
    grad_q, grad_k, grad_v = attend_pull(
        (project, grad_mixed, mixed, log_total), (grad_w_fc, grad_w_out)
    )
    grad_w_qkv, grad_input, more = qkv_back(
        w_qkv, gains[0], kept, (grad_q, grad_k, grad_v), grad_after
    )
    vectors = jnp.concatenate([more[:4], sums[:4]], axis=0)
    return grad_input, (grad_w_qkv, grad_w_proj), (vectors, grad_fc_bias[0]), carried


MESH = pl.DeviceIdType.MESH
ANY = pl.BlockSpec(memory_space=pl.ANY)
CHUNK = 768
DEPTH = 96


def greet(groups):
    sides = {side for group in groups for side in group}
    places = lax.axis_size("ctx")
    barrier = pltpu.get_barrier_semaphore()
    for flip, step, bits in sorted(sides):
        device = {
            "section": lax.axis_index("section") ^ flip,
            "ctx": lax.rem(lax.axis_index("ctx") + step, places),
            "fsdp": lax.axis_index("fsdp") ^ bits,
        }
        pl.semaphore_signal(barrier, inc=1, device_id=device, device_id_type=MESH)
    pl.semaphore_wait(barrier, len(sides))


def chip_group():
    return [(1, 0, 0)] + [(flip, 0, bits) for flip in (0, 1) for bits in (1, 2)]


def corner_group():
    return [(0, 0, 3), (1, 0, 3)]


def line_group():
    return [(0, step, 0) for step in range(1, lax.axis_size("ctx"))]


def column_group():
    return [(1, 0, 0)] + [
        (flip, step, 0) for step in range(1, lax.axis_size("ctx")) for flip in (0, 1)
    ]


def remote(source, target, send, recv, device):
    return pltpu.make_async_remote_copy(
        src_ref=source,
        dst_ref=target,
        send_sem=send,
        recv_sem=recv,
        device_id=device,
        device_id_type=MESH,
    )


class Gather:
    def __init__(self, layer, shards, outs, send, recv, local, *bounce):
        self.layer, self.shards, self.outs = layer, shards, outs
        self.bounce = bounce
        self.send, self.recv, self.local = send, recv, local
        self.section = lax.axis_index("section")
        self.index = lax.axis_index("fsdp")
        self.sibling = {"section": 1 - self.section}

    def across(self, bits, section=None):
        where = {"fsdp": self.index ^ bits}
        if section is not None:
            where["section"] = section
        return where

    def copy(self, m, slot, source, target, device):
        return remote(source, target, self.send.at[m, slot], self.recv.at[m, slot], device)

    def first(self, m, bits, half):
        slot = 0 if bits == 1 else 1
        return remote(
            self.shards[m].at[half],
            self.outs[m].at[self.index, half],
            self.send.at[m, slot + 8 * half],
            self.recv.at[m, slot],
            self.across(bits, half),
        )

    def arrived(self, m, bits):
        slot = 0 if bits == 1 else 1
        place = self.outs[m].at[self.index ^ bits, self.section]
        return self.copy(m, slot, place, place, self.across(bits))

    def own(self, m):
        return self.copy(m, 2, self.shards[m], self.outs[m].at[self.index], self.sibling)

    def take(self, m):
        return pltpu.make_async_copy(self.shards[m], self.bounce[m], self.local.at[0, m])

    def keep(self, m):
        return pltpu.make_async_copy(
            self.bounce[m], self.outs[m].at[self.index], self.local.at[1, m]
        )

    def corner(self, m, bits):
        middle = self.outs[m].shape[2] // 2
        rows = pl.ds(0, middle) if bits == 1 else pl.ds(middle, middle)
        place = self.outs[m].at[self.index ^ bits, self.section, rows]
        return self.copy(m, 3 if bits == 1 else 4, place, place, self.across(3 ^ bits))

    def trade(self, m, bits):
        place = self.outs[m].at[self.index ^ bits, self.section]
        return self.copy(m, 4 + bits, place, place, self.sibling)

    def start(self):
        @pl.when(self.section == self.layer)
        def _():
            for m in range(len(self.shards)):
                for half in (1 - self.layer, self.layer):
                    for bits in (1, 2):
                        self.first(m, bits, half).start()
                self.own(m).start()
                self.take(m).start()
            for m in range(len(self.shards)):
                self.take(m).wait()
                self.keep(m).start()

    def middle(self, m):
        for bits in (1, 2):
            self.arrived(m, bits).wait_recv()
            self.corner(m, bits).start()
            self.trade(m, bits).start()

    def last(self, m):
        for bits in (1, 2):
            self.corner(m, bits).wait_recv()
        self.trade(m, 3).start()

    def finish(self, m):
        for bits in (1, 2, 3):
            copy = self.trade(m, bits)
            copy.wait_send()
            copy.wait_recv()
        for bits in (1, 2):
            self.corner(m, bits).wait_send()

        @pl.when(self.section == self.layer)
        def _():
            for half in (0, 1):
                for bits in (1, 2):
                    self.first(m, bits, half).wait_send()
            self.own(m).wait_send()
            self.keep(m).wait()

        @pl.when(self.section != self.layer)
        def _():
            self.own(m).wait_recv()

class Seats:
    def __init__(self, seqs):
        self.sections, self.places = lax.axis_size("section"), lax.axis_size("ctx")
        self.seqs = seqs
        self.per = -(-seqs // (self.sections * self.places))
        self.size = self.places * self.per
        self.real = [min(max(seqs - i * self.size, 0), self.size) for i in range(self.sections)]
        self.skip = [(self.size - real) // 2 for real in self.real]

    def of(self, section, slot):
        real = jnp.where(section == 0, self.real[0], self.real[1])
        skip = jnp.where(section == 0, self.skip[0], self.skip[1])
        taken = (slot >= skip) & (slot < skip + real)
        return taken, jnp.clip(section * self.size + slot - skip, 0, self.seqs - 1)

    def home(self, seq):
        section, slot = seq // self.size, seq % self.size + self.skip[seq // self.size]
        return section, slot // self.per, slot % self.per


class Bring:
    def __init__(self, rows, outs, send, recv, local, zeros):
        self.rows, self.outs = rows, outs
        self.send, self.recv, self.local, self.zeros = send, recv, local, zeros
        self.seats = Seats(rows[0].shape[0])
        self.section, self.z = lax.axis_index("section"), lax.axis_index("ctx")
        self.depth = rows[0].shape[1]

    @staticmethod
    def scratch(rows, per, places):
        return [
            pltpu.SemaphoreType.DMA((len(rows), places * per)),
            pltpu.SemaphoreType.DMA((len(rows), per, places)),
            pltpu.SemaphoreType.DMA((len(rows), per, places)),
            pltpu.VMEM(rows[0].shape[1:], bf16),
        ]

    def span(self, z):
        return pl.ds(z * self.depth, self.depth)

    def copy(self, a, seq, place, p):
        return remote(
            self.rows[a].at[seq],
            self.outs[a].at[p, self.span(self.z)],
            self.send.at[a, place * self.seats.per + p],
            self.recv.at[a, p, self.z],
            {"ctx": place},
        )

    def arrival(self, a, p, place):
        target = self.outs[a].at[p, self.span(place)]
        return remote(target, target, self.send.at[a, 0], self.recv.at[a, p, place], {"ctx": place})

    def stay(self, a, seq, p):
        return pltpu.make_async_copy(
            self.rows[a].at[seq], self.outs[a].at[p, self.span(self.z)], self.local.at[a, p, 0]
        )

    def blank(self, a, p, place):
        return pltpu.make_async_copy(
            self.zeros, self.outs[a].at[p, self.span(place)], self.local.at[a, p, place]
        )

    def each(self, a, going, staying, coming, empty):
        for p in range(self.seats.per):
            for place in range(self.seats.places):
                taken, seq = self.seats.of(self.section, place * self.seats.per + p)

                @pl.when(taken & (place != self.z))
                def _():
                    going(a, seq, place, p)

            taken, seq = self.seats.of(self.section, self.z * self.seats.per + p)

            @pl.when(taken)
            def _():
                staying(a, seq, p)
                for place in range(self.seats.places):

                    @pl.when(place != self.z)
                    def _():
                        coming(a, p, place)

            @pl.when(jnp.logical_not(taken))
            def _():
                for place in range(self.seats.places):
                    empty(a, p, place)

    def clear(self):
        self.zeros[...] = jnp.zeros(self.zeros.shape, bf16)

    def start(self, a):
        self.each(
            a,
            lambda *at: self.copy(*at).start(),
            lambda *at: self.stay(*at).start(),
            lambda *at: None,
            lambda *at: self.blank(*at).start(),
        )

    def finish(self, a):
        self.each(
            a,
            lambda *at: self.copy(*at).wait_send(),
            lambda *at: self.stay(*at).wait(),
            lambda *at: self.arrival(*at).wait_recv(),
            lambda *at: self.blank(*at).wait(),
        )


class Deliver:
    def __init__(self, layer, rows, out, send, recv, local):
        self.layer, self.rows, self.out = layer, rows, out
        self.send, self.recv, self.local = send, recv, local
        self.seats = Seats(out.shape[0])
        self.section, self.z = lax.axis_index("section"), lax.axis_index("ctx")
        self.depth = out.shape[1]

    @staticmethod
    def scratch(seqs, per, places):
        return [
            pltpu.SemaphoreType.DMA((per, places)),
            pltpu.SemaphoreType.DMA((seqs,)),
            pltpu.SemaphoreType.DMA((per,)),
        ]

    def source(self, p, place):
        return self.rows.at[p, pl.ds(place * self.depth, self.depth)]

    def copy(self, p, place, seq):
        return remote(
            self.source(p, place),
            self.out.at[seq],
            self.send.at[p, place],
            self.recv.at[seq],
            {"section": self.layer, "ctx": place},
        )

    def stay(self, p, place, seq):
        return pltpu.make_async_copy(self.source(p, place), self.out.at[seq], self.local.at[p])

    def each(self, going, staying):
        for p in range(self.seats.per):
            taken, seq = self.seats.of(self.section, self.z * self.seats.per + p)
            for place in range(self.seats.places):
                here = (self.section == self.layer) & (self.z == place)

                @pl.when(taken & here)
                def _():
                    staying(p, place, seq)

                @pl.when(taken & jnp.logical_not(here))
                def _():
                    going(p, place, seq)

    def start(self):
        self.each(
            lambda *at: self.copy(*at).start(),
            lambda *at: self.stay(*at).start(),
        )

    def finish(self):
        self.each(
            lambda *at: self.copy(*at).wait_send(),
            lambda *at: self.stay(*at).wait(),
        )
        for seq in range(self.seats.seqs):
            section, place, p = self.seats.home(seq)

            @pl.when(
                (self.section == self.layer)
                & ((self.section != section) | (self.z != place))
            )
            def _():
                target = self.out.at[seq]
                remote(
                    target, target, self.send.at[0, 0], self.recv.at[seq], {"section": 1 - self.section}
                ).wait_recv()


class Spread:
    def __init__(self, block, out, send, recv, local):
        self.block, self.out, self.send, self.recv, self.local = block, out, send, recv, local
        self.section, self.index = lax.axis_index("section"), lax.axis_index("fsdp")

    @staticmethod
    def scratch():
        return [
            pltpu.SemaphoreType.DMA((8,)),
            pltpu.SemaphoreType.DMA((8,)),
            pltpu.SemaphoreType.DMA,
        ]

    def copies(self):
        for flip in (0, 1):
            for bits in range(4):
                if flip or bits:
                    yield remote(
                        self.block,
                        self.out.at[self.section, self.index],
                        self.send.at[4 * flip + bits],
                        self.recv.at[4 * flip + bits],
                        {"section": self.section ^ flip, "fsdp": self.index ^ bits},
                    )

    def stay(self):
        return pltpu.make_async_copy(
            self.block, self.out.at[self.section, self.index], self.local
        )

    def start(self):
        for copy in self.copies():
            copy.start()
        self.stay().start()

    def finish(self):
        for copy in self.copies():
            copy.wait_send()
            copy.wait_recv()
        self.stay().wait()


def gather_scratch(shards):
    count = len(shards)
    return [
        pltpu.SemaphoreType.DMA((count, 10)),
        pltpu.SemaphoreType.DMA((count, 8)),
        pltpu.SemaphoreType.DMA((2, count)),
    ] + [pltpu.VMEM(shard.shape, shard.dtype) for shard in shards]


def gather_shapes(shards):
    return [jax.ShapeDtypeStruct((4,) + shard.shape, shard.dtype) for shard in shards]


def split_shards(shards):
    return [shard.reshape(2, -1, shard.shape[-1]) for shard in shards]


def join_shards(outs):
    return tuple(out.reshape(-1, out.shape[-1]) for out in outs)


class Reduce:
    def __init__(self, line, layer, items, out, scratch):
        self.line, self.layer, self.items, self.out = line, layer, items, out
        (
            self.own,
            self.twin,
            self.near_corner,
            self.far_corner,
            self.near,
            self.far,
            self.outer,
            self.inner,
            self.partial,
            self.total,
            self.send,
            self.recv,
            self.local,
            self.done,
        ) = scratch
        self.section = lax.axis_index("section")
        self.index = lax.axis_index("fsdp")
        self.z = lax.axis_index("ctx")
        self.count = self.own.shape[0]
        self.sibling = {"section": 1 - self.section}
        self.x = {"fsdp": self.index ^ 1}
        self.y = {"fsdp": self.index ^ 2}
        self.is_inner = (self.z == 1) | (self.z == 2)
        self.end = {"ctx": jnp.where(self.z == 1, 0, 3)}
        self.toward = {"ctx": jnp.where(self.z == 0, 1, 2)}
        self.opposite = {"ctx": 3 - self.z}

    def chunks(self):
        k = 0
        for item in self.items:
            rows, columns = item.shape[2:]
            depth = self.own.shape[2]
            for row in range(0, rows, depth):
                for column in range(0, columns, CHUNK):
                    yield k, item, pl.ds(row, depth), pl.ds(column, CHUNK)
                    k += 1

    def copy(self, k, slot, source, target, device):
        return remote(source, target, self.send.at[slot, k], self.recv.at[slot, k], device)

    def swap(self, k):
        return self.copy(k, 0, self.twin.at[k], self.twin.at[k], self.sibling)

    def load(self, k):
        return pltpu.make_async_copy(self.own.at[k], self.own.at[k], self.local.at[k])

    def corner(self, k, near):
        half = self.own.shape[2] // 2
        rows = pl.ds(0, half) if near else pl.ds(half, half)
        source = self.own.at[k, self.index ^ 3, rows]
        target = (self.near_corner if near else self.far_corner).at[k]
        return self.copy(k, 1 if near else 2, source, target, self.x if near else self.y)

    def side(self, k, near):
        source = self.own.at[k, self.index ^ (1 if near else 2)]
        target = (self.near if near else self.far).at[k]
        return self.copy(k, 3 if near else 4, source, target, self.x if near else self.y)

    def inward(self, k):
        return self.copy(k, 5, self.partial.at[k], self.outer.at[k], self.toward)

    def across(self, k):
        return self.copy(k, 6, self.partial.at[k], self.inner.at[k], self.opposite)

    def outward(self, k):
        return self.copy(k, 7, self.total.at[k], self.total.at[k], self.end)

    def start(self):
        for k, item, rows, columns in self.chunks():
            theirs = item.at[:, 1 - self.section, rows, columns]
            mine = item.at[:, self.section, rows, columns]
            self.copy(k, 0, theirs, self.twin.at[k], self.sibling).start()
            pltpu.make_async_copy(mine, self.own.at[k], self.local.at[k]).start()

    def stage(self, number, k):
        half = self.own.shape[2] // 2
        near, far = self.index ^ 1, self.index ^ 2
        if number == 0:
            self.load(k).wait()
            self.swap(k).wait_recv()
            for j in range(4):
                self.own[k, j] = self.own[k, j] + self.twin[k, j]
            self.corner(k, True).start()
            self.corner(k, False).start()
        elif number == 1:
            self.corner(k, True).wait_recv()
            self.corner(k, False).wait_recv()
            self.own[k, far, :half] = self.own[k, far, :half] + self.near_corner[k]
            self.own[k, near, half:] = self.own[k, near, half:] + self.far_corner[k]
            self.side(k, True).start()
            self.side(k, False).start()
        elif number == 2:
            self.side(k, True).wait_recv()
            self.side(k, False).wait_recv()
            summed = (
                self.own[k, self.index].astype(f32)
                + self.near[k].astype(f32)
                + self.far[k].astype(f32)
            ).astype(bf16)
            if not self.line:
                self.total[k] = summed
                return
            self.partial[k] = summed

            @pl.when(jnp.logical_not(self.is_inner))
            def _():
                self.inward(k).start()
        elif number == 3 and self.line:

            @pl.when(self.is_inner)
            def _():
                self.inward(k).wait_recv()
                self.partial[k] = self.partial[k] + self.outer[k]
                self.across(k).start()
        elif number == 4 and self.line:

            @pl.when(self.is_inner)
            def _():
                self.across(k).wait_recv()
                self.total[k] = self.partial[k] + self.inner[k]
                self.outward(k).start()

    def step(self, t, lags):
        for number, lag in enumerate(lags):
            k = t - lag

            @pl.when((k >= 0) & (k < self.count))
            def _():
                self.stage(number, k)

    def finish(self, k):
        self.swap(k).wait_send()
        for near in (True, False):
            self.corner(k, near).wait_send()
            self.side(k, near).wait_send()
        if self.line:

            @pl.when(self.is_inner)
            def _():
                self.across(k).wait_send()
                self.outward(k).wait_send()

            @pl.when(jnp.logical_not(self.is_inner))
            def _():
                self.inward(k).wait_send()
                self.outward(k).wait_recv()

    def write(self):
        return pltpu.make_async_copy(self.total, self.out.at[self.section], self.local.at[0])

    def give(self):
        place = self.out.at[1 - self.layer]
        return remote(self.total, place, self.done.at[0], self.done.at[1], self.sibling)

    def close(self):
        self.write().start()

        @pl.when(self.section != self.layer)
        def _():
            self.give().start()
            self.give().wait_send()

        @pl.when(self.section == self.layer)
        def _():
            self.give().wait_recv()

        self.write().wait()


LAGS = (0, 1, 3, 4, 5)
CARRIED_LAGS = (0, 2, 4, 6, 8)


class ReducePart:
    lags = CARRIED_LAGS

    def __init__(self, layer, grads, line):
        self.layer, self.line = layer, line
        self.ins = [grad.reshape(4, 2, -1, grad.shape[-1]) for grad in grads]
        depth = min([DEPTH] + [item.shape[2] for item in self.ins])
        self.chunks = sum((item.shape[2] // depth) * (item.shape[3] // CHUNK) for item in self.ins)
        self.outs = [jax.ShapeDtypeStruct((2, self.chunks, depth, CHUNK), bf16)]
        self.scratch = reduce_scratch(self.chunks, depth)

    def groups(self):
        return [column_group(), [(0, 0, 1), (0, 0, 2)]]

    def bind(self, ins, outs, scratch):
        return Reduce(self.line, self.layer, ins, outs[0], scratch)

    def begin(self, reduce):
        reduce.start()

    def tick(self, reduce, step, steps):
        lags = LAGS if steps == 1 else self.lags
        share = -(-(self.chunks + lags[-1]) // steps)

        def advance(t, _):
            reduce.step(step * share + t, lags)
            return 0

        lax.fori_loop(0, share, advance, 0)

    def end(self, reduce):
        def finish(k, _):
            reduce.finish(k)
            return 0

        lax.fori_loop(0, reduce.count, finish, 0)
        reduce.close()

    def result(self, outs):
        return outs[0] if self.line else lax.psum(outs[0], "ctx")


class DeliverPart:
    def __init__(self, layer, rows, stored):
        seats = Seats(stored[0])
        self.layer = layer
        self.ins = [rows.reshape(seats.per, -1, rows.shape[-1])]
        self.outs = [jax.ShapeDtypeStruct(stored, bf16)]
        self.scratch = Deliver.scratch(stored[0], seats.per, seats.places)

    def groups(self):
        return [column_group()]

    def bind(self, ins, outs, scratch):
        return Deliver(self.layer, ins[0], outs[0], *scratch)

    def begin(self, deliver):
        deliver.start()

    def tick(self, deliver, step, steps):
        pass

    def end(self, deliver):
        deliver.finish()

    def result(self, outs):
        return outs[0]


class BringPart:
    def __init__(self, rows):
        seats = Seats(rows.shape[0])
        _, depth, width = rows.shape
        self.ins = [rows]
        self.outs = [jax.ShapeDtypeStruct((seats.per, depth * seats.places, width), bf16)]
        self.scratch = Bring.scratch([rows], seats.per, seats.places)

    def groups(self):
        return [line_group()]

    def bind(self, ins, outs, scratch):
        return Bring(ins, outs, *scratch)

    def begin(self, bring):
        bring.clear()
        bring.start(0)

    def tick(self, bring, step, steps):
        pass

    def end(self, bring):
        bring.finish(0)

    def result(self, outs):
        return outs[0]


class SpreadPart:
    def __init__(self, block):
        self.ins = [block]
        self.outs = [jax.ShapeDtypeStruct((2, 4) + block.shape, bf16)]
        self.scratch = Spread.scratch()

    def groups(self):
        return [chip_group(), corner_group()]

    def bind(self, ins, outs, scratch):
        return Spread(ins[0], outs[0], *scratch)

    def begin(self, spread):
        spread.start()

    def tick(self, spread, step, steps):
        pass

    def end(self, spread):
        spread.finish()

    def result(self, outs):
        return outs[0]


class GatherPart:
    def __init__(self, layer, shards):
        self.layer = layer
        self.ins = split_shards(shards)
        self.outs = gather_shapes(self.ins)
        self.scratch = gather_scratch(self.ins)

    def groups(self):
        return [chip_group()]

    def bind(self, ins, outs, scratch):
        return Gather(self.layer, ins, outs, *scratch)

    def begin(self, gather):
        gather.start()

    def tick(self, gather, step, steps):
        count = len(self.ins)
        if steps == 1:
            for m in range(count):
                gather.middle(m)
                if m > 0:
                    gather.last(m - 1)
            gather.last(count - 1)
            return
        for m in range(count):

            @pl.when(step == steps - 1 - count + m)
            def _():
                gather.middle(m)

            @pl.when(step == steps - 1)
            def _():
                gather.last(m)

    def end(self, gather):
        for m in range(len(self.ins)):
            gather.finish(m)

    def result(self, outs):
        return join_shards(outs)


class Carry:
    def __init__(self, collective, *parts):
        self.collective, self.parts = collective, parts
        self.ins = [array for part in parts for array in part.ins]
        self.outs = [shape for part in parts for shape in part.outs]
        self.scratch = [shape for part in parts for shape in part.scratch]

    def params(self, limit=60):
        return pltpu.CompilerParams(
            collective_id=self.collective,
            has_side_effects=self.collective is not None,
            vmem_limit_bytes=limit * 1024 * 1024,
        )

    def kernel(self, body, ins, outs, scratch, grid):
        if not self.parts:
            return body
        steps = 1
        for size in grid:
            steps *= size

        def run(*refs):
            pieces, at = [], 0
            for size in (ins, len(self.ins), outs, len(self.outs), scratch, len(self.scratch)):
                pieces.append(refs[at : at + size])
                at += size
            bound, at = [], [0, 0, 0]
            for part in self.parts:
                sizes = [len(part.ins), len(part.outs), len(part.scratch)]
                taken = [
                    pieces[2 * i + 1][at[i] : at[i] + sizes[i]] for i in range(3)
                ]
                at = [at[i] + sizes[i] for i in range(3)]
                bound.append((part, part.bind(*taken)))
            step = 0
            for axis in range(len(grid)):
                step = step * grid[axis] + pl.program_id(axis)

            def begin():
                greet([group for part in self.parts for group in part.groups()])
                for part, state in bound:
                    part.begin(state)

            def end():
                for part, state in bound:
                    part.end(state)

            if steps == 1:
                begin()
            else:
                pl.when(step == 0)(begin)
            body(*pieces[0], *pieces[2], *pieces[4])
            for part, state in bound:
                part.tick(state, step, steps)
            if steps == 1:
                end()
            else:
                pl.when(step == steps - 1)(end)

        return run

    def alone(self):
        outs = pl.pallas_call(
            self.kernel(lambda: None, 0, 0, 0, ()),
            in_specs=[ANY] * len(self.ins),
            out_specs=[ANY] * len(self.outs),
            out_shape=self.outs,
            scratch_shapes=self.scratch,
            compiler_params=self.params(),
        )(*self.ins)
        return self.result(outs)

    def result(self, outs):
        results, at = [], 0
        for part in self.parts:
            results.append(part.result(outs[at : at + len(part.outs)]))
            at += len(part.outs)
        return results


def reduce_scratch(count, depth):
    block = (count, depth, CHUNK)
    half = (count, depth // 2, CHUNK)
    return (
        [pltpu.VMEM((count, 4, depth, CHUNK), bf16)] * 2
        + [pltpu.VMEM(half, bf16)] * 2
        + [pltpu.VMEM(block, bf16)] * 6
        + [
            pltpu.SemaphoreType.DMA((8, count)),
            pltpu.SemaphoreType.DMA((8, count)),
            pltpu.SemaphoreType.DMA((count,)),
            pltpu.SemaphoreType.DMA((2,)),
        ]
    )


def unchunk(blocks, shapes):
    depth = blocks.shape[-2]
    parts, k = [], 0
    for rows, columns in shapes:
        high, wide = rows // depth, columns // CHUNK
        part = blocks[..., k : k + high * wide, :, :]
        part = part.reshape(blocks.shape[:-3] + (high, wide) + blocks.shape[-2:])
        part = jnp.concatenate([part[..., j, :, :] for j in range(wide)], axis=-1)
        parts.append(part.reshape(blocks.shape[:-3] + (rows, columns)))
        k += high * wide
    return parts


def shards(
    block_input,
    positions,
    cotangent,
    w_qkv,
    w_proj,
    w_fc,
    w_out,
    ln_gain,
    ln_bias,
    attn_bias,
    out_bias,
    fc_bias,
):
    section = lax.axis_index("section")
    first = section == 0
    ctxs = lax.axis_size("ctx")
    fsdps = lax.axis_size("fsdp")
    local_seqs, local_rows, width = block_input.shape
    stored = block_input.shape
    length = positions.shape[1]
    seats = Seats(local_seqs)
    per = seats.per
    shard_width = ln_gain.shape[2]

    pack = jnp.concatenate(
        [ln_gain[0], ln_bias[0], attn_bias[0], out_bias[0], fc_bias[0].reshape(-1, shard_width)]
    )
    pack = jnp.pad(pack, ((0, 16 - pack.shape[0]), (0, 256 - shard_width)))

    def unpack(packed):
        packed = packed[:, :12, :shard_width]
        vectors = jnp.transpose(packed[:, :8], (1, 0, 2)).reshape(8, -1).astype(f32)
        fc = packed[:, 8:].reshape(-1).astype(f32)
        return vectors[0:2], vectors[2:4], vectors[4:6], vectors[6:8], fc

    shards_own = [matrix[0] for matrix in (w_qkv, w_proj, w_fc, w_out)]
    block_rows, packs, first_weights = Carry(
        0, BringPart(block_input), SpreadPart(pack), GatherPart(0, shards_own[:2])
    ).alone()
    smalls = [unpack(packs[layer]) for layer in range(2)]

    places = jnp.stack(
        [
            lax.dynamic_index_in_dim(
                positions, seats.of(section, lax.axis_index("ctx") * per + p)[1], 0, keepdims=False
            )
            for p in range(per)
        ]
    )
    order = (
        lax.broadcasted_iota(jnp.int32, (per, length, length), 1) == places[:, None, :]
    ).astype(bf16)
    order_back = (
        lax.broadcasted_iota(jnp.int32, (per, length, length), 2) == places[:, :, None]
    ).astype(bf16)

    def to_sorted(rows):
        return (
            jnp.einsum("bpt,btd->bpd", order, rows, preferred_element_type=f32)
            .astype(bf16)
            .reshape(per * length, width)
        )

    def to_stored(rows):
        return jnp.einsum(
            "btp,bpd->btd", order_back, rows.reshape(per, length, width), preferred_element_type=f32
        ).astype(bf16)

    start = to_sorted(block_rows)
    line = ctxs == 4

    def attend_zero(project):
        carry = Carry(1, GatherPart(0, shards_own[2:]), BringPart(cotangent))
        return attend_forward(project, length, carry)

    middle, kept_zero, weights_zero, attended, (early,) = layer_forward(
        (first_weights[0], lambda attended: (*first_weights, *attended[0])),
        smalls[0],
        start,
        attend_zero,
        Carry(7, GatherPart(1, shards_own[:2])),
    )
    grad_final = to_sorted(attended[1])

    def attend_one(project):
        carry = Carry(4, GatherPart(1, shards_own[2:]), DeliverPart(0, to_stored(middle), stored))
        return attend_forward(project, length, carry)

    final, kept_one, weights_one, (_, out_zero), _ = layer_forward(
        (early[0], lambda attended: (*early, *attended[0])), smalls[1], middle, attend_one, Carry(None)
    )
    outs = [out_zero]
    halves = []
    held = []

    def pull_one(kept, grads):
        held.append(grads[0])
        carry = Carry(
            5, ReducePart(1, grads[1:], line), DeliverPart(1, to_stored(final), stored)
        )
        pulled, (reduced, out_one) = attend_back(*kept, length, carry)
        outs.append(out_one)
        halves.append(reduced)
        return pulled

    def pull_zero(kept, grads):
        pulled, (reduced,) = attend_back(*kept, length, Carry(6, ReducePart(0, grads, line)))
        halves.append(reduced)
        return pulled

    grad_middle, grads_one, small_one, _ = layer_back(
        weights_one, smalls[1], kept_one, grad_final, Carry(None), pull_one
    )
    carry = Carry(
        2, ReducePart(1, (*grads_one, *held), line), DeliverPart(1, to_stored(grad_middle), stored)
    )
    grad_start, grads_zero, small_zero, (rest_one, in_one) = layer_back(
        weights_zero, smalls[0], kept_zero, grad_middle, carry, pull_zero
    )

    def repack(small):
        vectors, fc = small
        vectors = jnp.transpose(vectors.reshape(8, fsdps, shard_width), (1, 0, 2))
        packed = jnp.concatenate([vectors, fc.reshape(fsdps, -1, shard_width)], axis=1)
        depth = w_qkv.shape[1] // 2
        return jnp.pad(
            packed.astype(bf16),
            ((0, 0), (0, depth - packed.shape[1]), (0, CHUNK - packed.shape[2])),
        )[:, None]

    pack = jnp.concatenate([repack(small_zero), repack(small_one)], axis=1)
    pack = pack.reshape(-1, CHUNK)
    rest_zero, in_zero = Carry(
        3,
        ReducePart(0, (*grads_zero, pack), line),
        DeliverPart(0, to_stored(grad_start), stored),
    ).alone()
    packed = jnp.where(first, rest_zero[0, -1], rest_zero[1, -1])[:12, :shard_width].astype(f32)
    section_out = jnp.where(first, outs[0], outs[1])[None]
    section_in_grad = jnp.where(first, in_zero, in_one)[None]
    shapes = [(matrix.shape[1] // 2, matrix.shape[2]) for matrix in (w_qkv, w_proj, w_fc, w_out)]
    near = rest_zero.shape[1] - 1
    reduced = [
        jnp.where(first, rest_zero[:, :-1], rest_one[:, :near]),
        jnp.where(first, halves[1], jnp.concatenate([rest_one[:, near:], halves[0]], axis=1)),
    ]
    big = [
        block.reshape(-1, block.shape[-1]).astype(f32)[None]
        for some, these in zip(reduced, (shapes[:2], shapes[2:]))
        for block in unchunk(some, these)
    ]

    return (
        section_out,
        section_in_grad,
        *big,
        packed[None, 0:8:4],
        packed[None, 1:8:4],
        packed[None, 2:4],
        packed[None, 6:8],
        packed[8:].reshape(1, -1),
    )


def solution(mesh):
    matrix = P("section", "fsdp", None)
    vectors = P("section", None, "fsdp")
    rows_out = P("section", "fsdp", "ctx", None)
    return jax.shard_map(
        shards,
        mesh=mesh,
        in_specs=(
            P("fsdp", "ctx", None),
            P("fsdp", None),
            P("fsdp", "ctx", None),
            *([matrix] * 4),
            *([vectors] * 4),
            P("section", "fsdp"),
        ),
        out_specs=(
            rows_out,
            rows_out,
            *([matrix] * 4),
            *([vectors] * 4),
            P("section", "fsdp"),
        ),
        check_vma=False,
    )
```
